128 devices in a mesh: rep: 16 (over y_lo, z, core), shard: 8 (over x, y_hi).
Axes of the slice: x: 4, y: 4 (y_hi: 2, y_lo: 2; y = y_hi * 2 + y_lo), z: 4, core: 2. Of those that a mesh axis runs over, the one named last changes fastest.
Arguments:
- hidden_in: float32 [16384, 1024], P(('rep', 'shard')), may hold values from -6 to 6
- doc_start: int32 [16384], P(('rep', 'shard')), may hold values from 0 to 127, as said below
- grad_out: float32 [16384, 1024], P(('rep', 'shard')), may hold values from -6 to 6
- w_qkv: bfloat16 [2, 1024, 3072], P(None, 'shard'), may hold values from -0.1875 to 0.1875
- w_proj: bfloat16 [2, 1024, 1024], P(None, 'shard'), may hold values from -0.375 to 0.375
- w_up: bfloat16 [2, 1024, 4096], P(None, 'shard'), may hold values from -0.1875 to 0.1875
- w_down: bfloat16 [2, 4096, 1024], P(None, 'shard'), may hold values from -0.09375 to 0.09375
- norm_gain: bfloat16 [2, 1024, 2], P(None, 'shard'), may hold values from 0.5 to 1.5
- d_bias: bfloat16 [2, 1024, 6], P(None, 'shard'), may hold values from -3 to 3
- up_bias: bfloat16 [2, 4096], P(None, 'shard'), may hold values from -3 to 3
Outputs:
- hidden_out: float32 [16384, 1024], P(('rep', 'shard'))
- grad_in: float32 [16384, 1024], P(('rep', 'shard'))
- grad_qkv: float32 [2, 1024, 3072], P(None, 'shard')
- grad_proj: float32 [2, 1024, 1024], P(None, 'shard')
- grad_up: float32 [2, 1024, 4096], P(None, 'shard')
- grad_down: float32 [2, 4096, 1024], P(None, 'shard')
- grad_gain: float32 [2, 1024, 2], P(None, 'shard')
- grad_dbias: float32 [2, 1024, 6], P(None, 'shard')
- grad_upbias: float32 [2, 4096], P(None, 'shard')
The draws below stay inside these ranges and needn't reach their ends.
Inputs may be any that keep to these rules, and one draw needn't show every extreme that they name: `doc_start`: each aligned run of 128 slots holds whole documents in order: the value does not fall along a run, is 0 at the run's first slot, and equals the slot's own offset at a document's first token.
All inputs are finite; a program needn't handle non-finite values.
Results may differ from the reference program's by a relative error of at most 0.025.
Values may be sent and summed in bfloat16 or wider, within the bound.
No kernel may reach another device: no remote copies, remote signals or barrier semaphores. Data moves between devices by JAX's collectives and lax.ppermute only.
A program may use at most 256 MiB of HBM per device.

```python
import jax
import jax.numpy as jnp
from jax import lax

D = 1024
HEADS = 16
HEAD_DIM = 64
FF = 4096
LAYERS = 2
TOK_DEV = 128
TOKENS = 16384


def draw_doc_start(key, part):
    run_count = TOKENS // TOK_DEV
    rate_key, cut_key = jax.random.split(jax.random.fold_in(key, 11))
    run_rates = jax.random.randint(rate_key, (run_count, 1), 4, 65)
    boundary = jax.random.randint(cut_key, (run_count, TOK_DEV), 0, 1 << 20) % run_rates == 0
    slot_ids = jnp.arange(TOK_DEV, dtype=jnp.int32)[None, :]
    first_run = jnp.arange(run_count, dtype=jnp.int32)[:, None] == 0
    boundary = boundary | (slot_ids == 0) | first_run & (slot_ids == TOK_DEV - 1)
    starts = lax.cummax(jnp.where(boundary, slot_ids, 0), axis=1)
    return starts.reshape(TOKENS).astype(jnp.int32)


def shard_levels(own_key, shape, shards, smallest, top_value):
    def one(dim, shards_of):
        draws = jax.random.uniform(jax.random.fold_in(jax.random.fold_in(own_key, 6), dim), (shards_of,), jnp.float32, smallest / len(shards), top_value / len(shards))
        return jnp.repeat(jnp.exp(draws), shape[dim] // shards_of).reshape((-1,) + (1,) * (len(shape) - dim - 1))

    gain = one(*shards[0])
    for cut in shards[1:]:
        gain = gain * one(*cut)
    return gain


def centred(own_key, dims, deviation, reach, shards=(), held_as=jnp.bfloat16):
    drawn = deviation * jax.random.normal(own_key, dims, jnp.float32)
    if shards:
        drawn = drawn * shard_levels(own_key, dims, shards, -0.22, 0.18)
    return jnp.clip(drawn, -reach, reach).astype(held_as)


def setup_inputs(seed: int = 0) -> dict:
    splits = jax.random.split(jax.random.key(seed), 11)
    return {
        "hidden_in": centred(splits[0], (TOKENS, D), 1.0, 6.0, ((0, 128),), jnp.float32),
        "doc_start": draw_doc_start(jax.random.fold_in(splits[10], 71), 0),
        "grad_out": centred(splits[2], (TOKENS, D), 1.0, 6.0, ((0, 128),), jnp.float32),
        "w_qkv": centred(splits[3], (LAYERS, D, 3 * D), D ** -0.5, 0.1875, ((1, 8),)),
        "w_proj": centred(splits[4], (LAYERS, D, D), (D // 4) ** -0.5, 0.375, ((1, 8),)),
        "w_up": centred(splits[5], (LAYERS, D, FF), D ** -0.5, 0.1875, ((1, 8),)),
        "w_down": centred(splits[6], (LAYERS, FF, D), FF ** -0.5, 0.09375, ((1, 8),)),
        "norm_gain": jnp.clip(1.0 + 0.1 * jax.random.normal(splits[7], (LAYERS, D, 2), jnp.float32), 0.5, 1.5).astype(jnp.bfloat16),
        "d_bias": centred(splits[8], (LAYERS, D, 6), 0.5, 3.0, ((1, 8),)),
        "up_bias": centred(splits[9], (LAYERS, FF), 0.5, 3.0, ((1, 8),)),
    }


epsilon = 1e-05
gelu_coef = 0.7978845608

def batch_prod(form, left, right):
    return jnp.einsum(form, left.astype(jnp.float32), right.astype(jnp.float32))

def layer_norm(stream, gains, shifts):
    average = lax.optimization_barrier(jnp.mean(stream, axis=-1, keepdims=True))
    centered = stream - average
    variance = lax.optimization_barrier(jnp.mean(centered * centered, axis=-1, keepdims=True))
    inv_std = lax.rsqrt(variance + epsilon)
    normed = centered * inv_std
    return (normed * gains + shifts, normed, inv_std)

def norm_back(grad_norm, normed, inv_std, gains):
    scaled = grad_norm * gains
    inner = scaled - lax.optimization_barrier(jnp.mean(scaled, axis=-1, keepdims=True)) - normed * lax.optimization_barrier(jnp.mean(scaled * normed, axis=-1, keepdims=True))
    return (inv_std * inner, lax.optimization_barrier(jnp.sum(grad_norm * normed, axis=0)), lax.optimization_barrier(jnp.sum(grad_norm, axis=0)))

def gelu_tanh(values):
    inner = jnp.tanh(gelu_coef * (values + 0.044715 * values * values * values))
    return 0.5 * values * (1.0 + inner)

def gelu_slope(values):
    inner = jnp.tanh(gelu_coef * (values + 0.044715 * values * values * values))
    return 0.5 * (1.0 + inner) + 0.5 * values * (1.0 - inner * inner) * gelu_coef * (1.0 + 3.0 * 0.044715 * values * values)

def scores_of(query, keys_bf, starts):
    count = query.shape[0]
    query_heads = query.reshape(count, HEADS, HEAD_DIM)
    key_heads = keys_bf.reshape(count, HEADS, HEAD_DIM)
    scores = batch_prod('qhd,khd->hqk', query_heads, key_heads) * HEAD_DIM ** (-0.5)
    offsets = jnp.arange(count, dtype=jnp.int32)
    distance = (offsets[:, None] - offsets[None, :]).astype(jnp.float32)
    head_ids = jnp.arange(HEADS, dtype=jnp.int32).astype(jnp.float32)
    slopes = 2.0 ** (-8.0 * (head_ids + 1.0) / HEADS)
    scores = scores - slopes[:, None, None] * distance[None, :, :]
    visible = (starts[:, None] == starts[None, :]) & (offsets[None, :] <= offsets[:, None])
    return jnp.where(visible[None, :, :], scores, jnp.float32(-1000000000.0))

def layer_forward(stream, starts, wqkv, wproj, wupper, wlower, gains, biases, ubias):
    count, width = stream.shape
    gains = gains.astype(jnp.float32)
    biases = biases.astype(jnp.float32)
    first_f, normed_one, inv_one = layer_norm(stream, gains[:, 0], biases[:, 0])
    first_in = first_f.astype(jnp.bfloat16)
    merged = jnp.dot(first_in, wqkv, preferred_element_type=jnp.float32)
    query = (merged[:, :width] + biases[:, 2]).astype(jnp.bfloat16)
    keys_bf = merged[:, width:2 * width].astype(jnp.bfloat16)
    values_bf = (merged[:, 2 * width:] + biases[:, 3]).astype(jnp.bfloat16)
    scores = scores_of(query, keys_bf, starts)
    top_score = lax.optimization_barrier(jnp.max(scores, axis=-1, keepdims=True))
    log_total = top_score + jnp.log(lax.optimization_barrier(jnp.sum(jnp.exp(scores - top_score), axis=-1, keepdims=True)))
    weights_bf = jnp.exp(scores - log_total).astype(jnp.bfloat16)
    context = batch_prod('hqk,khd->qhd', weights_bf, values_bf.reshape(count, HEADS, HEAD_DIM))
    context = context.reshape(count, width).astype(jnp.bfloat16)
    middle = stream + jnp.dot(context, wproj, preferred_element_type=jnp.float32) + biases[:, 4]
    second_f, normed_two, inv_two = layer_norm(middle, gains[:, 1], biases[:, 1])
    second_in = second_f.astype(jnp.bfloat16)
    upper = jnp.dot(second_in, wupper, preferred_element_type=jnp.float32) + ubias.astype(jnp.float32)
    activ = gelu_tanh(upper).astype(jnp.bfloat16)
    result = middle + jnp.dot(activ, wlower, preferred_element_type=jnp.float32) + biases[:, 5]
    kept = (first_in, normed_one, inv_one, query, keys_bf, values_bf, log_total, context, second_in, normed_two, inv_two, upper, activ)
    return (result, kept)

def layer_backward(grad_y, starts, kept, wqkv, wproj, wupper, wlower, gains, biases, ubias):
    first_in, normed_one, inv_one, query, keys_bf, values_bf, log_total, context, second_in, normed_two, inv_two, upper, activ = kept
    count, width = grad_y.shape
    gains = gains.astype(jnp.float32)
    grad_yb = grad_y.astype(jnp.bfloat16)
    g_down = jnp.dot(activ.T, grad_yb, preferred_element_type=jnp.float32)
    g_bdown = lax.optimization_barrier(jnp.sum(grad_y, axis=0))
    grad_act = jnp.dot(grad_yb, wlower.T, preferred_element_type=jnp.float32)
    grad_upper = grad_act * gelu_slope(upper)
    g_ubias = lax.optimization_barrier(jnp.sum(grad_upper, axis=0))
    grad_ub = grad_upper.astype(jnp.bfloat16)
    g_up = jnp.dot(second_in.T, grad_ub, preferred_element_type=jnp.float32)
    grad_two = jnp.dot(grad_ub, wupper.T, preferred_element_type=jnp.float32)
    back_two, g_gain_two, g_shift_two = norm_back(grad_two, normed_two, inv_two, gains[:, 1])
    grad_mid = grad_y + back_two
    grad_midb = grad_mid.astype(jnp.bfloat16)
    g_proj = jnp.dot(context.T, grad_midb, preferred_element_type=jnp.float32)
    g_bproj = lax.optimization_barrier(jnp.sum(grad_mid, axis=0))
    grad_ctx = jnp.dot(grad_midb, wproj.T, preferred_element_type=jnp.float32).astype(jnp.bfloat16)
    scores = scores_of(query, keys_bf, starts)
    probs = jnp.exp(scores - log_total)
    probs_bf = probs.astype(jnp.bfloat16)
    ctx_heads = grad_ctx.reshape(count, HEADS, HEAD_DIM)
    grad_val = batch_prod('hqk,qhd->khd', probs_bf, ctx_heads)
    grad_prob = batch_prod('qhd,khd->hqk', ctx_heads, values_bf.reshape(count, HEADS, HEAD_DIM))
    delta = lax.optimization_barrier(jnp.sum(ctx_heads.astype(jnp.float32) * context.reshape(count, HEADS, HEAD_DIM).astype(jnp.float32), axis=-1))
    grad_score = (probs * (grad_prob - jnp.transpose(delta)[:, :, None])).astype(jnp.bfloat16)
    grad_query = batch_prod('hqk,khd->qhd', grad_score, keys_bf.reshape(count, HEADS, HEAD_DIM)) * HEAD_DIM ** (-0.5)
    grad_key = batch_prod('hqk,qhd->khd', grad_score, query.reshape(count, HEADS, HEAD_DIM)) * HEAD_DIM ** (-0.5)
    grad_query = grad_query.reshape(count, width)
    grad_key = grad_key.reshape(count, width)
    grad_val = grad_val.reshape(count, width)
    g_bquery = lax.optimization_barrier(jnp.sum(grad_query, axis=0))
    g_bvalue = lax.optimization_barrier(jnp.sum(grad_val, axis=0))
    grad_merged = jnp.concatenate([grad_query, grad_key, grad_val], axis=1).astype(jnp.bfloat16)
    g_qkv = jnp.dot(first_in.T, grad_merged, preferred_element_type=jnp.float32)
    grad_one = jnp.dot(grad_merged, wqkv.T, preferred_element_type=jnp.float32)
    back_one, g_gain_one, g_shift_one = norm_back(grad_one, normed_one, inv_one, gains[:, 0])
    grad_x = grad_mid + back_one
    g_gain = jnp.stack([g_gain_one, g_gain_two], axis=1)
    g_bias = jnp.stack([g_shift_one, g_shift_two, g_bquery, g_bvalue, g_bproj, g_bdown], axis=1)
    return (grad_x, (g_qkv, g_proj, g_up, g_down, g_gain, g_bias, g_ubias))

def reference(hidden_in, doc_start, grad_out, w_qkv, w_proj, w_up, w_down, norm_gain, d_bias, up_bias):
    run_count = TOKENS // TOK_DEV
    streams = hidden_in.reshape(run_count, TOK_DEV, D)
    starts_all = doc_start.reshape(run_count, TOK_DEV)
    grads_all = grad_out.reshape(run_count, TOK_DEV, D)

    def params_of(layer_no):
        return (w_qkv[layer_no], w_proj[layer_no], w_up[layer_no], w_down[layer_no], norm_gain[layer_no], d_bias[layer_no], up_bias[layer_no])
    zeros_acc = (jnp.zeros((LAYERS, D, 3 * D), jnp.float32), jnp.zeros((LAYERS, D, D), jnp.float32), jnp.zeros((LAYERS, D, FF), jnp.float32), jnp.zeros((LAYERS, FF, D), jnp.float32), jnp.zeros((LAYERS, D, 2), jnp.float32), jnp.zeros((LAYERS, D, 6), jnp.float32), jnp.zeros((LAYERS, FF), jnp.float32))

    def one_run(totals, item):
        stream, starts, grad_y = item
        entries = []
        current = stream
        for layer_no in range(LAYERS):
            entries.append(current)
            current, unused = layer_forward(current, starts, *params_of(layer_no))
        grads_per = [None] * LAYERS
        running = grad_y
        for layer_no in reversed(range(LAYERS)):
            unused_out, kept = layer_forward(entries[layer_no], starts, *params_of(layer_no))
            running, grads_per[layer_no] = layer_backward(running, starts, kept, *params_of(layer_no))
        totals = tuple((totals[slot] + jnp.stack([grads_per[layer_no][slot] for layer_no in range(LAYERS)]) for slot in range(7)))
        return (totals, (current, running))
    totals, outputs = lax.scan(one_run, zeros_acc, (streams, starts_all, grads_all))
    hidden_out = outputs[0].reshape(TOKENS, D)
    grad_in = outputs[1].reshape(TOKENS, D)
    return (hidden_out, grad_in, totals[0], totals[1], totals[2], totals[3], totals[4], totals[5], totals[6])
```

```python
import jax
import jax.numpy as jnp
from jax import lax
from jax.experimental import pallas as pl
from jax.experimental.pallas import tpu as pltpu
from jax.sharding import Mesh
from jax.sharding import PartitionSpec as P

HEADS = 16
HEAD_DIM = 64
LAYERS = 2
D = 1024
RUN = 128

epsilon = 1e-05
gelu_coef = 0.7978845608
f32 = jnp.float32
bf16 = jnp.bfloat16

AXES = ("ylo", "z", "core", "x", "yhi")


def ring(step):
    return [(i, (i + step) % 4) for i in range(4)]


def x_up(a):
    return lax.ppermute(a, "x", ring(1))


def x_down(a):
    return lax.ppermute(a, "x", ring(3))


def x_far(a):
    return lax.ppermute(a, "x", ring(2))


def z_up(a):
    return lax.ppermute(a, "z", ring(1))


def z_down(a):
    return lax.ppermute(a, "z", ring(3))


def z_far(a):
    return lax.ppermute(a, "z", ring(2))


def y_pair(a):
    return lax.ppermute(a, ("ylo", "yhi"), [(0, 3), (3, 0), (1, 2), (2, 1)])


def y_copy(a):
    return lax.ppermute(a, "ylo", [(0, 1), (1, 0)])


def swap(a):
    return lax.ppermute(a, "core", [(0, 1), (1, 0)])


def ring_gather(a, up, down):
    half = a.shape[0] // 2
    previous = up(a)
    following = down(a)
    top = up(previous[:half])
    bottom = down(following[half:])
    return a, following, (top, bottom), previous


def ring_scatter(parts, up, down):
    own, following, far, previous = parts
    half = own.shape[0] // 2
    from_previous = up(far[:half])
    from_following = down(far[half:])
    go_up = jnp.concatenate(
        [(following[:half].astype(f32) + from_previous.astype(f32)).astype(bf16), following[half:]]
    )
    go_down = jnp.concatenate(
        [previous[:half], (previous[half:].astype(f32) + from_following.astype(f32)).astype(bf16)]
    )
    got_up = up(go_up)
    got_down = down(go_down)
    return own.astype(f32) + got_up.astype(f32) + got_down.astype(f32)


def rolled(stack, start):
    return lax.dynamic_slice_in_dim(jnp.concatenate([stack, stack[:3]]), start, 4, axis=0)


def ordered_by_core(own, core, axis):
    other = swap(own)
    first = jnp.where(core == 0, own, other)
    second = jnp.where(core == 0, other, own)
    return jnp.stack([first, second], axis=axis)


def take_kernel(order_ref, in_ref, out_ref):
    for block in range(8):
        at = pl.multiple_of(order_ref[block] * 128, 128)
        out_ref[:, block * 128 : (block + 1) * 128] = in_ref[:, pl.ds(at, 128)]


def take_blocks(a, order):
    return pl.pallas_call(
        take_kernel,
        out_shape=jax.ShapeDtypeStruct(a.shape, a.dtype),
        grid_spec=pltpu.PrefetchScalarGridSpec(
            num_scalar_prefetch=1,
            grid=(1,),
            in_specs=[pl.BlockSpec(a.shape, lambda i, order: (0, 0))],
            out_specs=pl.BlockSpec(a.shape, lambda i, order: (0, 0)),
        ),
        compiler_params=pltpu.CompilerParams(vmem_limit_bytes=4 * 1024 * 1024),
        cost_estimate=pl.CostEstimate(flops=0, bytes_accessed=2 * a.size * a.dtype.itemsize, transcendentals=0),
    )(order, a)


def head_scores(q, k, seen, distance, slope):
    s = lax.dot_general(q, k, (((1,), (1,)), ((), ())), preferred_element_type=f32) * HEAD_DIM ** (-0.5)
    s = s - slope * distance
    return jnp.where(seen, s, f32(-1000000000.0))


def visibility(row_start, col_start):
    row = lax.broadcasted_iota(jnp.int32, (RUN, RUN), 0)
    col = lax.broadcasted_iota(jnp.int32, (RUN, RUN), 1)
    seen = (row_start == col_start) & (col <= row)
    return seen, (row - col).astype(f32)


def attend_kernel(slope_ref, rows_ref, cols_ref, qkv_ref, ctx_ref):
    pair = pl.program_id(1)
    seen, distance = visibility(rows_ref[0], cols_ref[0])
    done = []
    for e in range(2):
        q = qkv_ref[:, e * 64 : e * 64 + 64]
        k = qkv_ref[:, 128 + e * 64 : 192 + e * 64]
        v = qkv_ref[:, 256 + e * 64 : 320 + e * 64]
        s = head_scores(q, k, seen, distance, slope_ref[pair * 2 + e])
        top = jnp.max(s, axis=-1, keepdims=True)
        lse = top + jnp.log(jnp.sum(jnp.exp(s - top), axis=-1, keepdims=True))
        p = jnp.exp(s - lse).astype(bf16)
        done.append(jnp.dot(p, v, preferred_element_type=f32))
    ctx_ref[...] = jnp.concatenate(done, axis=1).astype(bf16)


def attend_back_kernel(slope_ref, rows_ref, cols_ref, qkv_ref, ctx_ref, dctx_ref, dqkv_ref, dq_ref, dv_ref):
    pair = pl.program_id(1)
    seen, distance = visibility(rows_ref[0], cols_ref[0])
    dqs, dks, dvs = [], [], []
    tn = (((0,), (0,)), ((), ()))
    nt = (((1,), (1,)), ((), ()))
    for e in range(2):
        lanes = slice(e * 64, e * 64 + 64)
        q = qkv_ref[:, e * 64 : e * 64 + 64]
        k = qkv_ref[:, 128 + e * 64 : 192 + e * 64]
        v = qkv_ref[:, 256 + e * 64 : 320 + e * 64]
        s = head_scores(q, k, seen, distance, slope_ref[pair * 2 + e])
        top = jnp.max(s, axis=-1, keepdims=True)
        lse = top + jnp.log(jnp.sum(jnp.exp(s - top), axis=-1, keepdims=True))
        p = jnp.exp(s - lse)
        dctx = dctx_ref[:, lanes]
        dv = lax.dot_general(p.astype(bf16), dctx, tn, preferred_element_type=f32)
        dp = lax.dot_general(dctx, v, nt, preferred_element_type=f32)
        delta = jnp.sum(dctx.astype(f32) * ctx_ref[:, lanes].astype(f32), axis=-1, keepdims=True)
        ds = (p * (dp - delta)).astype(bf16)
        dqs.append(jnp.dot(ds, k, preferred_element_type=f32) * HEAD_DIM ** (-0.5))
        dks.append(lax.dot_general(ds, q, tn, preferred_element_type=f32) * HEAD_DIM ** (-0.5))
        dvs.append(dv)
    dq = jnp.concatenate(dqs, axis=1)
    dv = jnp.concatenate(dvs, axis=1)
    dqkv_ref[:, 0:128] = dq.astype(bf16)
    dqkv_ref[:, 128:256] = jnp.concatenate(dks, axis=1).astype(bf16)
    dqkv_ref[:, 256:384] = dv.astype(bf16)
    dq_ref[0, 0] = jnp.sum(dq, axis=0, keepdims=True)
    dv_ref[0, 0] = jnp.sum(dv, axis=0, keepdims=True)


def attend(qkv, rows, cols, slopes):
    return pl.pallas_call(
        attend_kernel,
        out_shape=jax.ShapeDtypeStruct((2 * RUN, 512), bf16),
        grid=(2, 4),
        in_specs=[
            pl.BlockSpec(memory_space=pltpu.SMEM),
            pl.BlockSpec((1, RUN, 1), lambda r, p: (r, 0, 0)),
            pl.BlockSpec((1, 1, RUN), lambda r, p: (r, 0, 0)),
            pl.BlockSpec((RUN, 384), lambda r, p: (r, p)),
        ],
        out_specs=pl.BlockSpec((RUN, 128), lambda r, p: (r, p)),
        compiler_params=pltpu.CompilerParams(vmem_limit_bytes=8 * 1024 * 1024),
        cost_estimate=pl.CostEstimate(flops=4 * 16 * RUN * RUN * 64, bytes_accessed=1 << 20, transcendentals=32 * RUN * RUN),
    )(slopes, rows, cols, qkv)


def attend_back(qkv, ctx, dctx, rows, cols, slopes):
    row_block = pl.BlockSpec((RUN, 128), lambda r, p: (r, p))
    sums = pl.BlockSpec((1, 1, 1, 128), lambda r, p: (r, p, 0, 0))
    return pl.pallas_call(
        attend_back_kernel,
        out_shape=(
            jax.ShapeDtypeStruct((2 * RUN, 1536), bf16),
            jax.ShapeDtypeStruct((2, 4, 1, 128), f32),
            jax.ShapeDtypeStruct((2, 4, 1, 128), f32),
        ),
        grid=(2, 4),
        in_specs=[
            pl.BlockSpec(memory_space=pltpu.SMEM),
            pl.BlockSpec((1, RUN, 1), lambda r, p: (r, 0, 0)),
            pl.BlockSpec((1, 1, RUN), lambda r, p: (r, 0, 0)),
            pl.BlockSpec((RUN, 384), lambda r, p: (r, p)),
            row_block,
            row_block,
        ],
        out_specs=(pl.BlockSpec((RUN, 384), lambda r, p: (r, p)), sums, sums),
        compiler_params=pltpu.CompilerParams(vmem_limit_bytes=8 * 1024 * 1024),
        cost_estimate=pl.CostEstimate(flops=10 * 16 * RUN * RUN * 64, bytes_accessed=1 << 21, transcendentals=32 * RUN * RUN),
    )(slopes, rows, cols, qkv, ctx, dctx)


def layer_norm(stream, gains, shifts):
    average = jnp.mean(stream, axis=-1, keepdims=True)
    centered = stream - average
    variance = jnp.mean(centered * centered, axis=-1, keepdims=True)
    inv_std = lax.rsqrt(variance + epsilon)
    normed = centered * inv_std
    return (normed * gains + shifts, normed, inv_std)


def norm_back(grad_norm, normed, inv_std, gains):
    scaled = grad_norm * gains
    inner = (
        scaled
        - jnp.mean(scaled, axis=-1, keepdims=True)
        - normed * jnp.mean(scaled * normed, axis=-1, keepdims=True)
    )
    return (inv_std * inner, jnp.sum(grad_norm * normed, axis=0), jnp.sum(grad_norm, axis=0))


def gelu_tanh(values):
    inner = jnp.tanh(gelu_coef * (values + 0.044715 * values * values * values))
    return 0.5 * values * (1.0 + inner)


def gelu_slope(values):
    inner = jnp.tanh(gelu_coef * (values + 0.044715 * values * values * values))
    return 0.5 * (1.0 + inner) + 0.5 * values * (1.0 - inner * inner) * gelu_coef * (
        1.0 + 3.0 * 0.044715 * values * values
    )


def dot(a, b):
    return jnp.dot(a, b, preferred_element_type=f32)


def dot_nt(a, b):
    return lax.dot_general(a, b, (((1,), (1,)), ((), ())), preferred_element_type=f32)


def dot_tn(a, b):
    return lax.dot_general(a, b, (((0,), (0,)), ((), ())), preferred_element_type=f32)


def local(hidden_in, doc_start, grad_out, w_qkv, w_proj, w_up, w_down, norm_gain, d_bias, up_bias):
    x, z, core, yhi = (lax.axis_index(n) for n in ("x", "z", "core", "yhi"))
    index = jnp.arange(8, dtype=jnp.int32)
    to_rel = ((x + index // 2) % 4) * 2 + (yhi ^ (index % 2))
    to_abs = ((index // 2 - x) % 4) * 2 + ((index % 2) ^ yhi)

    def both(own):
        return jnp.concatenate([own, swap(own)], axis=0)

    def halves_summed(partial):
        return partial[:RUN] + swap(partial[RUN:])

    small = jnp.concatenate(
        [
            jnp.transpose(jnp.concatenate([norm_gain, d_bias], axis=2), (0, 2, 1)).reshape(16, 128),
            up_bias.reshape(8, 128),
        ]
    )
    small = jnp.stack([small, y_pair(small)])
    small = jnp.where(yhi == 0, small, small[::-1])
    small = rolled(jnp.stack([small, x_down(small), x_far(small), x_up(small)]), (4 - x) % 4).astype(f32)
    wide = jnp.transpose(small[:, :, :16], (2, 0, 1, 3)).reshape(LAYERS, 8, D)
    hidden_bias = small[:, :, 16:].reshape(4, 2, LAYERS, 2, 256)

    def core_heads(vector):
        picked = lax.dynamic_index_in_dim(vector.reshape(4, 2, 2, 64), core, axis=2, keepdims=False)
        return rolled(picked.reshape(4, 128), z)

    def gather_layer(layer):
        qkv = w_qkv[layer].reshape(128, 3, 4, 2, 2, 64)
        qkv = lax.dynamic_index_in_dim(qkv, z, axis=2, keepdims=False)
        qkv = lax.dynamic_index_in_dim(qkv, core, axis=3, keepdims=False).reshape(128, 384)
        up = w_up[layer].reshape(128, 4, 2, 2, 256)
        up = lax.dynamic_index_in_dim(up, z, axis=1, keepdims=False)
        up = lax.dynamic_index_in_dim(up, core, axis=2, keepdims=False).reshape(128, 512)
        proj = lax.dynamic_index_in_dim(w_proj[layer].reshape(2, 64, D), core, axis=0, keepdims=False)
        down = lax.dynamic_index_in_dim(w_down[layer].reshape(2, 256, D), core, axis=0, keepdims=False)

        def by_z(piece):
            piece = jnp.concatenate([piece, y_pair(piece)])
            own, following, (top, bottom), previous = ring_gather(piece, x_up, x_down)
            piece = jnp.concatenate([own, following, top, bottom, previous])
            own, following, (top, bottom), previous = ring_gather(piece, z_up, z_down)
            return own, following, jnp.concatenate([top, bottom]), previous

        def by_x(piece):
            other = y_pair(piece)
            first = jnp.where(yhi == 0, piece, other)
            second = jnp.where(yhi == 0, other, piece)
            piece = jnp.concatenate([first, second])
            own, following, (top, bottom), previous = ring_gather(piece, x_up, x_down)
            stack = jnp.stack([own, following, jnp.concatenate([top, bottom]), previous])
            return rolled(stack, (z - x) % 4).reshape(4 * piece.shape[0], D)

        qkv = jnp.concatenate(by_z(qkv), axis=1)
        proj = by_x(proj)
        up = jnp.concatenate(by_z(up), axis=1)
        down = by_x(down)
        return qkv, proj, up, down

    weights = [gather_layer(layer) for layer in range(LAYERS)]

    starts = both(doc_start.reshape(1, RUN))
    rows, cols = starts.reshape(2, RUN, 1), starts.reshape(2, 1, RUN)
    head = 4 * ((z + index // 2) % 4) + 2 * (index % 2) + core
    slopes = 2.0 ** (-8.0 * (head.astype(f32) + 1.0) / HEADS)

    kept = []
    current = hidden_in
    for layer in range(LAYERS):
        wqkv, wproj, wup, wdown = weights[layer]
        gain_one, gain_two, shift_one, shift_two, bq, bv, bproj, bdown = (wide[layer, i] for i in range(8))
        bq, bv = core_heads(bq), core_heads(bv)
        bqkv = jnp.stack([bq, jnp.zeros_like(bq), bv], axis=1).reshape(1536)
        ubias = lax.dynamic_index_in_dim(hidden_bias[:, :, layer], core, axis=2, keepdims=False)
        ubias = rolled(ubias.reshape(4, 512), z).reshape(2048)
        first_f, normed_one, inv_one = layer_norm(current, gain_one, shift_one)
        first_in = both(take_blocks(first_f.astype(bf16), to_rel))
        qkv = (dot(first_in, wqkv) + bqkv).astype(bf16)
        ctx = attend(qkv, rows, cols, slopes)
        middle = current + halves_summed(dot(ctx, wproj)) + bproj
        second_f, normed_two, inv_two = layer_norm(middle, gain_two, shift_two)
        second_in = both(take_blocks(second_f.astype(bf16), to_rel))
        upper = dot(second_in, wup) + ubias
        activ = gelu_tanh(upper).astype(bf16)
        current = middle + halves_summed(dot(activ, wdown)) + bdown
        kept.append((first_in, normed_one, inv_one, qkv, ctx, second_in, normed_two, inv_two, upper, activ, gain_one, gain_two))
    hidden_out = current

    def blocks_by_z(left, right, width):
        parts = [dot_tn(left, right[:, i * width : (i + 1) * width]).astype(bf16) for i in range(4)]
        part = ring_scatter(parts, z_up, z_down).astype(bf16)
        part = ring_scatter([part[i * 256 : (i + 1) * 256] for i in range(4)], x_up, x_down).astype(bf16)
        part = part[:128].astype(f32) + y_pair(part[128:]).astype(f32)
        return part.astype(bf16)

    def blocks_by_x(left, right, width):
        parts = []
        for i in range(4):
            at = ((x + i - z) % 4) * width
            parts.append(dot_tn(lax.dynamic_slice_in_dim(left, at, width, axis=1), right).astype(bf16))
        part = ring_scatter(parts, x_up, x_down).astype(bf16).reshape(2, width // 2, D)
        keep = lax.dynamic_index_in_dim(part, yhi, axis=0, keepdims=False)
        give = lax.dynamic_index_in_dim(part, 1 - yhi, axis=0, keepdims=False)
        part = (keep.astype(f32) + y_pair(give).astype(f32)).astype(bf16).reshape(4, width // 8, D)
        parts = rolled(part, z)
        return ring_scatter([parts[i] for i in range(4)], z_up, z_down).astype(bf16)

    def shared(part):
        part = (part.astype(f32) + y_copy(part).astype(f32)).astype(bf16)
        own, following, (top, bottom), previous = ring_gather(part, z_up, z_down)
        stack = rolled(jnp.stack([own, following, jnp.concatenate([top, bottom]), previous]), (4 - z) % 4)
        return ordered_by_core(stack, core, 0)

    grads = [None] * LAYERS
    small_grads = [None] * LAYERS
    running = grad_out
    for layer in reversed(range(LAYERS)):
        wqkv, wproj, wup, wdown = weights[layer]
        first_in, normed_one, inv_one, qkv, ctx, second_in, normed_two, inv_two, upper, activ, gain_one, gain_two = kept[layer]
        g_bdown = jnp.sum(running, axis=0)
        grad_yb = both(running.astype(bf16))
        grad_upper = dot_nt(grad_yb, wdown) * gelu_slope(upper)
        g_ubias = jnp.sum(grad_upper, axis=0)
        grad_ub = grad_upper.astype(bf16)
        p_down = blocks_by_x(activ, grad_yb, 512)
        p_up = blocks_by_z(second_in, grad_ub, 512)
        grad_two = take_blocks(halves_summed(dot_nt(grad_ub, wup)), to_abs)
        back_two, g_gain_two, g_shift_two = norm_back(grad_two, normed_two, inv_two, gain_two)
        grad_mid = running + back_two
        g_bproj = jnp.sum(grad_mid, axis=0)
        grad_midb = both(grad_mid.astype(bf16))
        grad_ctx = dot_nt(grad_midb, wproj).astype(bf16)
        p_proj = blocks_by_x(ctx, grad_midb, 128)
        grad_qkv, g_bq, g_bv = attend_back(qkv, ctx, grad_ctx, rows, cols, slopes)
        p_qkv = blocks_by_z(first_in, grad_qkv, 384)
        grad_one = take_blocks(halves_summed(dot_nt(grad_qkv, wqkv)), to_abs)
        back_one, g_gain_one, g_shift_one = norm_back(grad_one, normed_one, inv_one, gain_one)
        running = grad_mid + back_one

        def spread_heads(sums):
            sums = rolled(jnp.sum(sums, axis=0).reshape(4, 128), (4 - z) % 4).reshape(4, 2, 1, 64)
            mine = lax.broadcasted_iota(jnp.int32, (4, 2, 2, 64), 2) == core
            return jnp.where(mine, sums, 0.0).reshape(D)

        hidden = rolled(g_ubias.reshape(4, 512), (4 - z) % 4).reshape(4, 2, 1, 256)
        mine = lax.broadcasted_iota(jnp.int32, (4, 2, 2, 256), 2) == core
        hidden = jnp.where(mine, hidden, 0.0).reshape(4, 2, 4, 128)
        thin = jnp.stack([g_gain_one, g_gain_two, g_shift_one, g_shift_two, spread_heads(g_bq), spread_heads(g_bv), g_bproj, g_bdown])
        thin = jnp.transpose(thin.reshape(8, 4, 2, 128), (1, 2, 0, 3))
        small_grads[layer] = jnp.concatenate([thin, hidden], axis=2)

        by_x = shared(jnp.concatenate([p_down, p_proj]))
        by_z = shared(jnp.concatenate([p_up, p_qkv], axis=1))
        g_down = by_x[:, :, :64].reshape(512, D)
        g_proj = by_x[:, :, 64:].reshape(128, D)
        g_up = jnp.transpose(by_z[..., :512].reshape(2, 4, 128, 2, 256), (2, 1, 3, 0, 4)).reshape(128, 4096)
        g_qkv = jnp.transpose(by_z[..., 512:].reshape(2, 4, 128, 3, 2, 64), (2, 3, 1, 4, 0, 5)).reshape(128, 3072)
        grads[layer] = (g_qkv, g_proj, g_up, g_down)

    part = jnp.concatenate(small_grads, axis=2)
    part = rolled(part, x)
    part = part[0] + x_up(part[1]) + x_far(part[2]) + x_down(part[3])
    keep = lax.dynamic_index_in_dim(part, yhi, axis=0, keepdims=False)
    give = lax.dynamic_index_in_dim(part, 1 - yhi, axis=0, keepdims=False)
    part = keep + y_pair(give)
    part = part + y_copy(part)
    part = part + swap(part)
    part = rolled(jnp.stack([part, z_down(part), z_far(part), z_up(part)]), (4 - z) % 4)
    part = part[0] + part[1] + part[2] + part[3]
    part = part.reshape(LAYERS, 12, 128)
    g_wide = jnp.transpose(part[:, :8], (0, 2, 1))
    stacked = [jnp.stack([grads[layer][slot] for layer in range(LAYERS)]).astype(f32) for slot in range(4)]
    return (hidden_out, running, *stacked, g_wide[:, :, :2], g_wide[:, :, 2:], part[:, 8:].reshape(LAYERS, 512))


def solution(mesh):
    fine = Mesh(mesh.devices.reshape(2, 4, 2, 4, 2), AXES)
    tokens = P(AXES)
    wide_tokens = P(AXES, None)
    params = P(None, ("x", "yhi"), None)
    return jax.shard_map(
        local,
        mesh=fine,
        in_specs=(wide_tokens, tokens, wide_tokens, params, params, params, params, params, params, P(None, ("x", "yhi"))),
        out_specs=(wide_tokens, wide_tokens, params, params, params, params, params, params, P(None, ("x", "yhi"))),
        check_vma=False,
    )
```

```python
import jax
import jax.numpy as jnp
from jax import lax
from jax.experimental import pallas as pl
from jax.experimental.pallas import tpu as pltpu
from jax.sharding import Mesh
from jax.sharding import PartitionSpec as P

HEADS = 16
HEAD_DIM = 64
LAYERS = 2
D = 1024
RUN = 128

epsilon = 1e-05
gelu_coef = 0.7978845608
f32 = jnp.float32
bf16 = jnp.bfloat16

AXES = ("ylo", "z", "core", "x", "yhi")


def ring(step):
    return [(i, (i + step) % 4) for i in range(4)]


def x_up(a):
    return lax.ppermute(a, "x", ring(1))


def x_down(a):
    return lax.ppermute(a, "x", ring(3))


def x_far(a):
    return lax.ppermute(a, "x", ring(2))


def z_up(a):
    return lax.ppermute(a, "z", ring(1))


def z_down(a):
    return lax.ppermute(a, "z", ring(3))


def z_far(a):
    return lax.ppermute(a, "z", ring(2))


def y_pair(a):
    return lax.ppermute(a, ("ylo", "yhi"), [(0, 3), (3, 0), (1, 2), (2, 1)])


def y_copy(a):
    return lax.ppermute(a, "ylo", [(0, 1), (1, 0)])


def y_far(a):
    return lax.ppermute(a, "yhi", [(0, 1), (1, 0)])


def swap(a):
    return lax.ppermute(a, "core", [(0, 1), (1, 0)])


def ring_gather(a, up, down):
    half = a.shape[0] // 2
    previous = up(a)
    following = down(a)
    top = up(previous[:half])
    bottom = down(following[half:])
    return a, following, (top, bottom), previous


def ring_scatter(parts, up, down):
    own, following, far, previous = parts
    half = own.shape[0] // 2
    from_previous = up(far[:half])
    from_following = down(far[half:])
    go_up = jnp.concatenate(
        [(following[:half].astype(f32) + from_previous.astype(f32)).astype(bf16), following[half:]]
    )
    go_down = jnp.concatenate(
        [previous[:half], (previous[half:].astype(f32) + from_following.astype(f32)).astype(bf16)]
    )
    got_up = up(go_up)
    got_down = down(go_down)
    return own.astype(f32) + got_up.astype(f32) + got_down.astype(f32)


def rolled(stack, start):
    return lax.dynamic_slice_in_dim(jnp.concatenate([stack, stack[:3]]), start, 4, axis=0)


def ordered_by_core(own, core, axis):
    other = swap(own)
    first = jnp.where(core == 0, own, other)
    second = jnp.where(core == 0, other, own)
    return jnp.stack([first, second], axis=axis)


def after(a, earlier):
    there = jnp.abs(earlier[0, 0].astype(f32)) < 1e30
    return jnp.where(there, a, jnp.zeros_like(a))


def select_kernel(at_ref, up_a, up_b, q_ref, k_ref, v_ref, down_ref, proj_ref, by_z_ref, by_x_ref):
    first = at_ref[1] == 0
    by_z_ref[0, :, 0:256] = up_a[0]
    by_z_ref[0, :, 256:512] = up_b[0]
    for t, ref in enumerate((q_ref, k_ref, v_ref)):
        low = jnp.where(first, ref[0, :, 0:64].astype(f32), ref[0, :, 64:128].astype(f32))
        high = jnp.where(first, ref[0, :, 128:192].astype(f32), ref[0, :, 192:256].astype(f32))
        by_z_ref[0, :, 512 + t * 128 : 640 + t * 128] = jnp.concatenate([low, high], axis=1).astype(bf16)
    by_x_ref[0, 0:256] = down_ref[0]
    by_x_ref[0, 256:320] = proj_ref[0]


def select_weights(at, w_qkv, w_proj, w_up, w_down):
    def lanes(block):
        return pl.BlockSpec((1, 128, 256), lambda l, at: (l, 0, block(at)))

    return pl.pallas_call(
        select_kernel,
        out_shape=(
            jax.ShapeDtypeStruct((LAYERS, 128, 896), bf16),
            jax.ShapeDtypeStruct((LAYERS, 320, D), bf16),
        ),
        grid_spec=pltpu.PrefetchScalarGridSpec(
            num_scalar_prefetch=1,
            grid=(LAYERS,),
            in_specs=[
                lanes(lambda at: 4 * at[0] + at[1]),
                lanes(lambda at: 4 * at[0] + 2 + at[1]),
                lanes(lambda at: at[0]),
                lanes(lambda at: 4 + at[0]),
                lanes(lambda at: 8 + at[0]),
                pl.BlockSpec((1, 256, D), lambda l, at: (l, at[1], 0)),
                pl.BlockSpec((1, 64, D), lambda l, at: (l, at[1], 0)),
            ],
            out_specs=(
                pl.BlockSpec((1, 128, 896), lambda l, at: (l, 0, 0)),
                pl.BlockSpec((1, 320, D), lambda l, at: (l, 0, 0)),
            ),
        ),
        compiler_params=pltpu.CompilerParams(vmem_limit_bytes=8 * 1024 * 1024),
        cost_estimate=pl.CostEstimate(flops=0, bytes_accessed=4 * 1024 * 1024, transcendentals=0),
    )(at, w_up, w_up, w_qkv, w_qkv, w_qkv, w_down, w_proj)


def take_kernel(order_ref, in_ref, out_ref):
    for block in range(8):
        at = pl.multiple_of(order_ref[block] * 128, 128)
        out_ref[:, block * 128 : (block + 1) * 128] = in_ref[:, pl.ds(at, 128)]


def take_blocks(a, order):
    return pl.pallas_call(
        take_kernel,
        out_shape=jax.ShapeDtypeStruct(a.shape, a.dtype),
        grid_spec=pltpu.PrefetchScalarGridSpec(
            num_scalar_prefetch=1,
            grid=(1,),
            in_specs=[pl.BlockSpec(a.shape, lambda i, order: (0, 0))],
            out_specs=pl.BlockSpec(a.shape, lambda i, order: (0, 0)),
        ),
        compiler_params=pltpu.CompilerParams(vmem_limit_bytes=4 * 1024 * 1024),
        cost_estimate=pl.CostEstimate(flops=0, bytes_accessed=2 * a.size * a.dtype.itemsize, transcendentals=0),
    )(order, a)


def head_scores(q, k, seen, distance, slope):
    s = lax.dot_general(q, k, (((1,), (1,)), ((), ())), preferred_element_type=f32) * HEAD_DIM ** (-0.5)
    s = s - slope * distance
    return jnp.where(seen, s, f32(-1000000000.0))


def visibility(row_start, col_start):
    row = lax.broadcasted_iota(jnp.int32, (RUN, RUN), 0)
    col = lax.broadcasted_iota(jnp.int32, (RUN, RUN), 1)
    seen = (row_start == col_start) & (col <= row)
    return seen, (row - col).astype(f32)


def attend_kernel(slope_ref, rows_ref, cols_ref, qkv_ref, ctx_ref):
    first = pl.program_id(1) * 4
    seen, distance = visibility(rows_ref[0], cols_ref[0])
    done = []
    for i in range(4):
        at = (i // 2) * 384 + (i % 2) * 64
        q = qkv_ref[:, at : at + 64]
        k = qkv_ref[:, at + 128 : at + 192]
        v = qkv_ref[:, at + 256 : at + 320]
        s = head_scores(q, k, seen, distance, slope_ref[first + i])
        top = jnp.max(s, axis=-1, keepdims=True)
        lse = top + jnp.log(jnp.sum(jnp.exp(s - top), axis=-1, keepdims=True))
        p = jnp.exp(s - lse).astype(bf16)
        done.append(jnp.dot(p, v, preferred_element_type=f32))
    ctx_ref[...] = jnp.concatenate(done, axis=1).astype(bf16)


def attend_back_kernel(slope_ref, rows_ref, cols_ref, qkv_ref, ctx_ref, dctx_ref, dqkv_ref, dq_ref, dv_ref):
    first = pl.program_id(1) * 4
    seen, distance = visibility(rows_ref[0], cols_ref[0])
    dqs, dks, dvs = [], [], []
    tn = (((0,), (0,)), ((), ()))
    nt = (((1,), (1,)), ((), ()))
    for i in range(4):
        lanes = slice(i * 64, i * 64 + 64)
        at = (i // 2) * 384 + (i % 2) * 64
        q = qkv_ref[:, at : at + 64]
        k = qkv_ref[:, at + 128 : at + 192]
        v = qkv_ref[:, at + 256 : at + 320]
        s = head_scores(q, k, seen, distance, slope_ref[first + i])
        top = jnp.max(s, axis=-1, keepdims=True)
        lse = top + jnp.log(jnp.sum(jnp.exp(s - top), axis=-1, keepdims=True))
        p = jnp.exp(s - lse)
        dctx = dctx_ref[:, lanes]
        dv = lax.dot_general(p.astype(bf16), dctx, tn, preferred_element_type=f32)
        dp = lax.dot_general(dctx, v, nt, preferred_element_type=f32)
        delta = jnp.sum(dctx.astype(f32) * ctx_ref[:, lanes].astype(f32), axis=-1, keepdims=True)
        ds = (p * (dp - delta)).astype(bf16)
        dqs.append(jnp.dot(ds, k, preferred_element_type=f32) * HEAD_DIM ** (-0.5))
        dks.append(lax.dot_general(ds, q, tn, preferred_element_type=f32) * HEAD_DIM ** (-0.5))
        dvs.append(dv)
    for pair in range(2):
        at = pair * 384
        dq = jnp.concatenate(dqs[2 * pair : 2 * pair + 2], axis=1)
        dk = jnp.concatenate(dks[2 * pair : 2 * pair + 2], axis=1)
        dv = jnp.concatenate(dvs[2 * pair : 2 * pair + 2], axis=1)
        dqkv_ref[:, at : at + 128] = dq.astype(bf16)
        dqkv_ref[:, at + 128 : at + 256] = dk.astype(bf16)
        dqkv_ref[:, at + 256 : at + 384] = dv.astype(bf16)
        dq_ref[0, 0, :, pair * 128 : pair * 128 + 128] = jnp.sum(dq, axis=0, keepdims=True)
        dv_ref[0, 0, :, pair * 128 : pair * 128 + 128] = jnp.sum(dv, axis=0, keepdims=True)


def attend(qkv, rows, cols, slopes):
    return pl.pallas_call(
        attend_kernel,
        out_shape=jax.ShapeDtypeStruct((2 * RUN, 512), bf16),
        grid=(2, 2),
        in_specs=[
            pl.BlockSpec(memory_space=pltpu.SMEM),
            pl.BlockSpec((1, RUN, 1), lambda r, p: (r, 0, 0)),
            pl.BlockSpec((1, 1, RUN), lambda r, p: (r, 0, 0)),
            pl.BlockSpec((RUN, 768), lambda r, p: (r, p)),
        ],
        out_specs=pl.BlockSpec((RUN, 256), lambda r, p: (r, p)),
        compiler_params=pltpu.CompilerParams(vmem_limit_bytes=8 * 1024 * 1024),
        cost_estimate=pl.CostEstimate(flops=4 * 16 * RUN * RUN * 64, bytes_accessed=1 << 20, transcendentals=32 * RUN * RUN),
    )(slopes, rows, cols, qkv)


def attend_back(qkv, ctx, dctx, rows, cols, slopes):
    row_block = pl.BlockSpec((RUN, 256), lambda r, p: (r, p))
    sums = pl.BlockSpec((1, 1, 1, 256), lambda r, p: (r, p, 0, 0))
    return pl.pallas_call(
        attend_back_kernel,
        out_shape=(
            jax.ShapeDtypeStruct((2 * RUN, 1536), bf16),
            jax.ShapeDtypeStruct((2, 2, 1, 256), f32),
            jax.ShapeDtypeStruct((2, 2, 1, 256), f32),
        ),
        grid=(2, 2),
        in_specs=[
            pl.BlockSpec(memory_space=pltpu.SMEM),
            pl.BlockSpec((1, RUN, 1), lambda r, p: (r, 0, 0)),
            pl.BlockSpec((1, 1, RUN), lambda r, p: (r, 0, 0)),
            pl.BlockSpec((RUN, 768), lambda r, p: (r, p)),
            row_block,
            row_block,
        ],
        out_specs=(pl.BlockSpec((RUN, 768), lambda r, p: (r, p)), sums, sums),
        compiler_params=pltpu.CompilerParams(vmem_limit_bytes=8 * 1024 * 1024),
        cost_estimate=pl.CostEstimate(flops=10 * 16 * RUN * RUN * 64, bytes_accessed=1 << 21, transcendentals=32 * RUN * RUN),
    )(slopes, rows, cols, qkv, ctx, dctx)


def layer_norm(stream, gains, shifts):
    average = jnp.mean(stream, axis=-1, keepdims=True)
    centered = stream - average
    variance = jnp.mean(centered * centered, axis=-1, keepdims=True)
    inv_std = lax.rsqrt(variance + epsilon)
    normed = centered * inv_std
    return (normed * gains + shifts, normed, inv_std)


def norm_back(grad_norm, normed, inv_std, gains):
    scaled = grad_norm * gains
    inner = (
        scaled
        - jnp.mean(scaled, axis=-1, keepdims=True)
        - normed * jnp.mean(scaled * normed, axis=-1, keepdims=True)
    )
    return (inv_std * inner, jnp.sum(grad_norm * normed, axis=0), jnp.sum(grad_norm, axis=0))


def gelu_tanh(values):
    inner = jnp.tanh(gelu_coef * (values + 0.044715 * values * values * values))
    return 0.5 * values * (1.0 + inner)


def gelu_slope(values):
    inner = jnp.tanh(gelu_coef * (values + 0.044715 * values * values * values))
    return 0.5 * (1.0 + inner) + 0.5 * values * (1.0 - inner * inner) * gelu_coef * (
        1.0 + 3.0 * 0.044715 * values * values
    )


def dot(a, b):
    return jnp.dot(a, b, preferred_element_type=f32)


def dot_nt(a, b):
    return lax.dot_general(a, b, (((1,), (1,)), ((), ())), preferred_element_type=f32)


def dot_tn(a, b):
    return lax.dot_general(a, b, (((0,), (0,)), ((), ())), preferred_element_type=f32)


def local(hidden_in, doc_start, grad_out, w_qkv, w_proj, w_up, w_down, norm_gain, d_bias, up_bias):
    x, z, core, yhi = (lax.axis_index(n) for n in ("x", "z", "core", "yhi"))
    index = jnp.arange(8, dtype=jnp.int32)
    to_rel = ((x + index // 2) % 4) * 2 + (yhi ^ (index % 2))
    to_abs = ((index // 2 - x) % 4) * 2 + ((index % 2) ^ yhi)

    def both(own):
        return jnp.concatenate([own, swap(own)], axis=0)

    def halves_summed(partial):
        return partial[:RUN] + swap(partial[RUN:])

    small = jnp.concatenate(
        [
            jnp.transpose(jnp.concatenate([norm_gain, d_bias], axis=2), (0, 2, 1)).reshape(16, 128),
            up_bias.reshape(8, 128),
        ]
    )
    small = jnp.stack([small, y_pair(small)])
    small = jnp.where(yhi == 0, small, small[::-1])
    small = rolled(jnp.stack([small, x_down(small), x_far(small), x_up(small)]), (4 - x) % 4).astype(f32)
    wide = jnp.transpose(small[:, :, :16], (2, 0, 1, 3)).reshape(LAYERS, 8, D)
    hidden_bias = small[:, :, 16:].reshape(4, 2, LAYERS, 2, 256)

    def core_heads(vector):
        picked = lax.dynamic_index_in_dim(vector.reshape(4, 2, 2, 64), core, axis=2, keepdims=False)
        return rolled(picked.reshape(4, 128), z)

    at = jnp.stack([z, core]).astype(jnp.int32)
    mine_z, mine_x = select_weights(at, w_qkv, w_proj, w_up, w_down)

    def gather_layer(layer, earlier):
        piece_z, piece_x = mine_z[layer], mine_x[layer]
        if earlier:
            piece_z, piece_x = after(piece_z, earlier[0]), after(piece_x, earlier[0])
        piece_z = jnp.concatenate([piece_z, y_pair(piece_z)])
        other = y_pair(piece_x)
        piece_x = jnp.concatenate([jnp.where(yhi == 0, piece_x, other), jnp.where(yhi == 0, other, piece_x)])
        own, following, (top, bottom), previous = ring_gather(piece_z, x_up, x_down)
        near = top
        piece_z = jnp.concatenate([own, following, top, bottom, previous])
        if earlier:
            piece_z, piece_x = after(piece_z, earlier[1]), after(piece_x, earlier[2])
        own, following, (top, bottom), previous = ring_gather(piece_z, z_up, z_down)
        far_z = top
        blocks = (own, following, jnp.concatenate([top, bottom]), previous)
        up = jnp.concatenate([block[:, :512] for block in blocks], axis=1)
        qkv = jnp.concatenate([block[:, 512:] for block in blocks], axis=1)
        own, following, (top, bottom), previous = ring_gather(piece_x, x_up, x_down)
        stack = jnp.stack([own, following, jnp.concatenate([top, bottom]), previous])
        stack = rolled(stack, (z - x) % 4).reshape(4, 2, 320, D)
        down = stack[:, :, :256].reshape(2048, D)
        proj = stack[:, :, 256:].reshape(512, D)
        return (qkv, proj, up, down), (near, far_z, top)

    weights, earlier = [], ()
    for layer in range(LAYERS):
        gathered, earlier = gather_layer(layer, earlier)
        weights.append(gathered)

    starts = both(doc_start.reshape(1, RUN))
    rows, cols = starts.reshape(2, RUN, 1), starts.reshape(2, 1, RUN)
    head = 4 * ((z + index // 2) % 4) + 2 * (index % 2) + core
    slopes = 2.0 ** (-8.0 * (head.astype(f32) + 1.0) / HEADS)

    kept = []
    current = hidden_in
    for layer in range(LAYERS):
        wqkv, wproj, wup, wdown = weights[layer]
        gain_one, gain_two, shift_one, shift_two, bq, bv, bproj, bdown = (wide[layer, i] for i in range(8))
        bq, bv = core_heads(bq), core_heads(bv)
        bqkv = jnp.stack([bq, jnp.zeros_like(bq), bv], axis=1).reshape(1536)
        ubias = lax.dynamic_index_in_dim(hidden_bias[:, :, layer], core, axis=2, keepdims=False)
        ubias = rolled(ubias.reshape(4, 512), z).reshape(2048)
        first_f, normed_one, inv_one = layer_norm(current, gain_one, shift_one)
        first_in = both(take_blocks(first_f.astype(bf16), to_rel))
        qkv = (dot(first_in, wqkv) + bqkv).astype(bf16)
        ctx = attend(qkv, rows, cols, slopes)
        middle = current + halves_summed(dot(ctx, wproj)) + bproj
        second_f, normed_two, inv_two = layer_norm(middle, gain_two, shift_two)
        second_in = both(take_blocks(second_f.astype(bf16), to_rel))
        upper = dot(second_in, wup) + ubias
        activ = gelu_tanh(upper).astype(bf16)
        current = middle + halves_summed(dot(activ, wdown)) + bdown
        kept.append((first_in, normed_one, inv_one, qkv, ctx, second_in, normed_two, inv_two, upper, activ, gain_one, gain_two))
    hidden_out = current

    def over_y(part):
        keep = lax.dynamic_index_in_dim(part, yhi, axis=0, keepdims=False)
        give = lax.dynamic_index_in_dim(part, 1 - yhi, axis=0, keepdims=False)
        near = keep.astype(f32) + y_copy(keep).astype(f32)
        return (near + (y_pair(give).astype(f32) + y_far(give).astype(f32))).astype(bf16)

    def over_z_pieces(part):
        stack = jnp.stack([part, z_down(part), z_far(part), z_up(part)])
        return ordered_by_core(rolled(stack, (4 - z) % 4), core, 0)

    def blocks_by_z(pairs):
        parts = []
        for i in range(4):
            parts.append(
                jnp.concatenate(
                    [dot_tn(left, right[:, i * w : (i + 1) * w]).astype(bf16) for left, right, w in pairs], axis=1
                )
            )
        part = ring_scatter(parts, z_up, z_down).astype(bf16)
        part = ring_scatter([part[i * 256 : (i + 1) * 256] for i in range(4)], x_up, x_down).astype(bf16)
        part = part.reshape(2, 128, part.shape[1])
        return over_z_pieces(over_y(jnp.where(yhi == 0, part, part[::-1])))

    def blocks_by_x(pairs):
        parts = []
        for i in range(4):
            block = []
            for left, right, w in pairs:
                own = lax.dynamic_slice_in_dim(left, ((x + i - z) % 4) * w, w, axis=1)
                block.append(dot_tn(own, right).astype(bf16).reshape(2, 4, w // 8, D))
            parts.append(jnp.concatenate(block, axis=2).reshape(640, D))
        part = ring_scatter(parts, x_up, x_down).astype(bf16).reshape(2, 4, 80, D)
        parts = rolled(jnp.transpose(part, (1, 0, 2, 3)), z).reshape(4, 160, D)
        part = ring_scatter([parts[i] for i in range(4)], z_up, z_down).astype(bf16)
        return over_z_pieces(over_y(part.reshape(2, 80, D)))

    grads = [None] * LAYERS
    thin_grads, head_grads, unit_grads = [None] * LAYERS, [None] * LAYERS, [None] * LAYERS
    running = grad_out
    for layer in reversed(range(LAYERS)):
        wqkv, wproj, wup, wdown = weights[layer]
        first_in, normed_one, inv_one, qkv, ctx, second_in, normed_two, inv_two, upper, activ, gain_one, gain_two = kept[layer]
        g_bdown = jnp.sum(running, axis=0)
        grad_yb = both(running.astype(bf16))
        grad_upper = dot_nt(grad_yb, wdown) * gelu_slope(upper)
        g_ubias = jnp.sum(grad_upper, axis=0)
        grad_ub = grad_upper.astype(bf16)
        grad_two = take_blocks(halves_summed(dot_nt(grad_ub, wup)), to_abs)
        back_two, g_gain_two, g_shift_two = norm_back(grad_two, normed_two, inv_two, gain_two)
        grad_mid = running + back_two
        g_bproj = jnp.sum(grad_mid, axis=0)
        grad_midb = both(grad_mid.astype(bf16))
        grad_ctx = dot_nt(grad_midb, wproj).astype(bf16)
        by_x = blocks_by_x([(activ, grad_yb, 512), (ctx, grad_midb, 128)])
        grad_qkv, g_bq, g_bv = attend_back(qkv, ctx, grad_ctx, rows, cols, slopes)
        by_z = blocks_by_z([(second_in, grad_ub, 512), (first_in, grad_qkv, 384)])
        grad_one = take_blocks(halves_summed(dot_nt(grad_qkv, wqkv)), to_abs)
        back_one, g_gain_one, g_shift_one = norm_back(grad_one, normed_one, inv_one, gain_one)
        running = grad_mid + back_one

        thin_grads[layer] = [g_gain_one, g_gain_two, g_shift_one, g_shift_two, g_bproj, g_bdown]
        head_grads[layer] = [jnp.sum(g, axis=0).reshape(4, 128) for g in (g_bq, g_bv)]
        unit_grads[layer] = g_ubias.reshape(4, 512)

        g_down = by_x[:, :, :64].reshape(512, D)
        g_proj = by_x[:, :, 64:].reshape(128, D)
        g_up = jnp.transpose(by_z[..., :512].reshape(2, 4, 128, 2, 256), (2, 1, 3, 0, 4)).reshape(128, 4096)
        g_qkv = jnp.transpose(by_z[..., 512:].reshape(2, 4, 128, 3, 2, 64), (2, 3, 1, 4, 0, 5)).reshape(128, 3072)
        grads[layer] = (g_qkv, g_proj, g_up, g_down)

    thin = jnp.stack(thin_grads[0] + thin_grads[1]).reshape(LAYERS, 6, 4, 2, 128)
    heads = jnp.stack(head_grads[0] + head_grads[1], axis=1)
    heads = rolled(heads, (4 - z) % 4).reshape(4, LAYERS, 2, 2, 1, 64)
    mine = lax.broadcasted_iota(jnp.int32, (4, LAYERS, 2, 2, 2, 64), 4) == core
    heads = jnp.where(mine, heads, 0.0).reshape(4, LAYERS, 2, 2, 128)
    units = rolled(jnp.stack(unit_grads, axis=1), (4 - z) % 4).reshape(4, LAYERS, 2, 1, 256)
    mine = lax.broadcasted_iota(jnp.int32, (4, LAYERS, 2, 2, 256), 3) == core
    units = jnp.where(mine, units, 0.0).reshape(4, LAYERS, 2, 4, 128)
    thin = jnp.transpose(thin, (2, 3, 0, 1, 4))
    heads = jnp.transpose(heads, (0, 3, 1, 2, 4))
    units = jnp.transpose(units, (0, 2, 1, 3, 4))
    part = jnp.concatenate([thin[:, :, :, :4], heads, thin[:, :, :, 4:], units], axis=3)
    part = part.reshape(4, 2, 24, 128)
    part = rolled(part, x)
    part = part[0] + x_up(part[1]) + x_far(part[2]) + x_down(part[3])
    keep = lax.dynamic_index_in_dim(part, yhi, axis=0, keepdims=False)
    give = lax.dynamic_index_in_dim(part, 1 - yhi, axis=0, keepdims=False)
    part = (keep + y_copy(keep)) + (y_pair(give) + y_far(give))
    part = part + swap(part)
    part = rolled(jnp.stack([part, z_down(part), z_far(part), z_up(part)]), (4 - z) % 4)
    part = part[0] + part[1] + part[2] + part[3]
    part = part.reshape(LAYERS, 12, 128)
    g_wide = jnp.transpose(part[:, :8], (0, 2, 1))
    stacked = [jnp.stack([grads[layer][slot] for layer in range(LAYERS)]).astype(f32) for slot in range(4)]
    return (hidden_out, running, *stacked, g_wide[:, :, :2], g_wide[:, :, 2:], part[:, 8:].reshape(LAYERS, 512))


def solution(mesh):
    fine = Mesh(mesh.devices.reshape(2, 4, 2, 4, 2), AXES)
    tokens = P(AXES)
    wide_tokens = P(AXES, None)
    params = P(None, ("x", "yhi"), None)
    return jax.shard_map(
        local,
        mesh=fine,
        in_specs=(wide_tokens, tokens, wide_tokens, params, params, params, params, params, params, P(None, ("x", "yhi"))),
        out_specs=(wide_tokens, wide_tokens, params, params, params, params, params, params, P(None, ("x", "yhi"))),
        check_vma=False,
    )
```

```python
import jax
import jax.numpy as jnp
from jax import lax
from jax.experimental import pallas as pl
from jax.experimental.pallas import tpu as pltpu
from jax.sharding import Mesh
from jax.sharding import PartitionSpec as P

HEADS = 16
HEAD_DIM = 64
LAYERS = 2
D = 1024
RUN = 128

epsilon = 1e-05
gelu_coef = 0.7978845608
f32 = jnp.float32
bf16 = jnp.bfloat16

AXES = ("ylo", "z", "core", "x", "yhi")


def ring(step):
    return [(i, (i + step) % 4) for i in range(4)]


def z_up(a):
    return lax.ppermute(a, "z", ring(1))


def z_down(a):
    return lax.ppermute(a, "z", ring(3))


def swap(a):
    return lax.ppermute(a, "core", [(0, 1), (1, 0)])


SHARD = ("x", "yhi")
REP = ("ylo", "z", "core")


def exchange(blocks, axes):
    return lax.all_to_all(blocks, axes, 0, 0, tiled=True)


def to_all(a, axes, count):
    return exchange(jnp.broadcast_to(a[None], (count, *a.shape)), axes)


def ring_gather(a, up, down):
    half = a.shape[0] // 2
    previous = up(a)
    following = down(a)
    top = up(previous[:half])
    bottom = down(following[half:])
    return a, following, (top, bottom), previous


def ring_scatter(parts, up, down):
    own, following, far, previous = parts
    half = own.shape[0] // 2
    from_previous = up(far[:half])
    from_following = down(far[half:])
    go_up = jnp.concatenate(
        [(following[:half].astype(f32) + from_previous.astype(f32)).astype(bf16), following[half:]]
    )
    go_down = jnp.concatenate(
        [previous[:half], (previous[half:].astype(f32) + from_following.astype(f32)).astype(bf16)]
    )
    got_up = up(go_up)
    got_down = down(go_down)
    return own.astype(f32) + got_up.astype(f32) + got_down.astype(f32)


def rolled(stack, start):
    return lax.dynamic_slice_in_dim(jnp.concatenate([stack, stack[:3]]), start, 4, axis=0)


def after(a, earlier):
    there = jnp.abs(earlier[0, 0].astype(f32)) < 1e30
    return jnp.where(there, a, jnp.zeros_like(a))


def select_kernel(at_ref, up_a, up_b, q_ref, k_ref, v_ref, down_ref, proj_ref, by_z_ref, by_x_ref):
    first = at_ref[1] == 0
    by_z_ref[0, :, 0:256] = up_a[0]
    by_z_ref[0, :, 256:512] = up_b[0]
    for t, ref in enumerate((q_ref, k_ref, v_ref)):
        low = jnp.where(first, ref[0, :, 0:64].astype(f32), ref[0, :, 64:128].astype(f32))
        high = jnp.where(first, ref[0, :, 128:192].astype(f32), ref[0, :, 192:256].astype(f32))
        by_z_ref[0, :, 512 + t * 128 : 640 + t * 128] = jnp.concatenate([low, high], axis=1).astype(bf16)
    by_x_ref[0, 0:256] = down_ref[0]
    by_x_ref[0, 256:320] = proj_ref[0]


def select_weights(at, w_qkv, w_proj, w_up, w_down):
    def lanes(block):
        return pl.BlockSpec((1, 128, 256), lambda l, at: (l, 0, block(at)))

    return pl.pallas_call(
        select_kernel,
        out_shape=(
            jax.ShapeDtypeStruct((LAYERS, 128, 896), bf16),
            jax.ShapeDtypeStruct((LAYERS, 320, D), bf16),
        ),
        grid_spec=pltpu.PrefetchScalarGridSpec(
            num_scalar_prefetch=1,
            grid=(LAYERS,),
            in_specs=[
                lanes(lambda at: 4 * at[0] + at[1]),
                lanes(lambda at: 4 * at[0] + 2 + at[1]),
                lanes(lambda at: at[0]),
                lanes(lambda at: 4 + at[0]),
                lanes(lambda at: 8 + at[0]),
                pl.BlockSpec((1, 256, D), lambda l, at: (l, at[1], 0)),
                pl.BlockSpec((1, 64, D), lambda l, at: (l, at[1], 0)),
            ],
            out_specs=(
                pl.BlockSpec((1, 128, 896), lambda l, at: (l, 0, 0)),
                pl.BlockSpec((1, 320, D), lambda l, at: (l, 0, 0)),
            ),
        ),
        compiler_params=pltpu.CompilerParams(vmem_limit_bytes=8 * 1024 * 1024),
        cost_estimate=pl.CostEstimate(flops=0, bytes_accessed=4 * 1024 * 1024, transcendentals=0),
    )(at, w_up, w_up, w_qkv, w_qkv, w_qkv, w_down, w_proj)


def call(kernel, scalars, operands, out_shape, grid, in_specs, out_specs, flops=0):
    moved = sum(a.size * a.dtype.itemsize for a in operands) + sum(o.size * o.dtype.itemsize for o in jax.tree.leaves(out_shape))
    return pl.pallas_call(
        kernel,
        out_shape=out_shape,
        grid_spec=pltpu.PrefetchScalarGridSpec(
            num_scalar_prefetch=1, grid=grid, in_specs=in_specs, out_specs=out_specs
        ),
        compiler_params=pltpu.CompilerParams(vmem_limit_bytes=20 * 1024 * 1024),
        cost_estimate=pl.CostEstimate(flops=flops, bytes_accessed=moved, transcendentals=0),
    )(scalars, *operands)


def split_z_kernel(at_ref, own_ref, next_ref, top_ref, bottom_ref, last_ref, up_ref, qkv_ref):
    step = pl.program_id(0)

    def put(position, block):
        up_ref[:, position * 512 : position * 512 + 512] = block[:, :512]
        qkv_ref[:, position * 384 : position * 384 + 384] = block[:, 512:]

    put(0, own_ref)
    put(1, next_ref)
    put(3, last_ref)

    @pl.when(step < 4)
    def _():
        put(2, top_ref)

    @pl.when(step >= 4)
    def _():
        put(2, bottom_ref)


def split_z(at, own, following, top, bottom, previous):
    block = pl.BlockSpec((128, 896), lambda i, at: (i, 0))
    return call(
        split_z_kernel,
        at,
        (own, following, top, bottom, previous),
        (jax.ShapeDtypeStruct((D, 2048), bf16), jax.ShapeDtypeStruct((D, 1536), bf16)),
        (8,),
        [
            block,
            block,
            pl.BlockSpec((128, 896), lambda i, at: (jnp.minimum(i, 3), 0)),
            pl.BlockSpec((128, 896), lambda i, at: (jnp.maximum(i - 4, 0), 0)),
            block,
        ],
        (pl.BlockSpec((128, 2048), lambda i, at: (i, 0)), pl.BlockSpec((128, 1536), lambda i, at: (i, 0))),
    )


def split_x_kernel(at_ref, in_ref, down_ref, proj_ref):
    for e in range(2):
        down_ref[e * 256 : e * 256 + 256] = in_ref[e, 0:256]
        proj_ref[e * 64 : e * 64 + 64] = in_ref[e, 256:320]


def split_x(at, gathered):
    return call(
        split_x_kernel,
        at,
        (gathered,),
        (jax.ShapeDtypeStruct((2048, D), bf16), jax.ShapeDtypeStruct((512, D), bf16)),
        (4,),
        [pl.BlockSpec((2, 320, D), lambda i, at: (lax.rem(i + at[0], 4), 0, 0))],
        (pl.BlockSpec((512, D), lambda i, at: (i, 0)), pl.BlockSpec((128, D), lambda i, at: (i, 0))),
    )


def grad_z_kernel(at_ref, a2_ref, dub_ref, a1_ref, dqkv_ref, out_ref):
    out_ref[:, :512] = dot_tn(a2_ref[...], dub_ref[...]).astype(bf16)
    out_ref[:, 512:] = dot_tn(a1_ref[...], dqkv_ref[...]).astype(bf16)


def grad_z(at, a2, dub, a1, dqkv, block):
    rows = pl.BlockSpec((256, 256), lambda i, at: (0, i))
    return call(
        grad_z_kernel,
        at,
        (a2, dub, a1, dqkv),
        jax.ShapeDtypeStruct((D, 896), bf16),
        (4,),
        [
            rows,
            pl.BlockSpec((256, 512), lambda i, at: (0, block)),
            rows,
            pl.BlockSpec((256, 384), lambda i, at: (0, block)),
        ],
        pl.BlockSpec((256, 896), lambda i, at: (i, 0)),
        flops=2 * 256 * D * 896,
    )


def grad_x_kernel(at_ref, m_ref, dy_ref, ctx_ref, dr_ref, out_ref):
    for e in range(2):
        out_ref[e, 0:256] = dot_tn(m_ref[:, e * 256 : e * 256 + 256], dy_ref[...]).astype(bf16)
        out_ref[e, 256:320] = dot_tn(ctx_ref[:, e * 64 : e * 64 + 64], dr_ref[...]).astype(bf16)


def grad_x(at, m, dy, ctx, dr):
    whole = pl.BlockSpec((256, D), lambda i, at: (0, 0))
    return call(
        grad_x_kernel,
        at,
        (m, dy, ctx, dr),
        jax.ShapeDtypeStruct((8, 320, D), bf16),
        (4,),
        [
            pl.BlockSpec((256, 512), lambda i, at: (0, i)),
            whole,
            pl.BlockSpec((256, 128), lambda i, at: (0, i)),
            whole,
        ],
        pl.BlockSpec((2, 320, D), lambda i, at: (lax.rem(i + at[0], 4), 0, 0)),
        flops=2 * 256 * D * 2560,
    )


def assemble_kernel(at_ref, first_ref, second_ref, up_ref, qkv_ref):
    def put(ref):
        for j in range(4):
            for e in range(2):
                for core in range(2):
                    at = j * 1024 + e * 512 + core * 256
                    up_ref[0, :, at : at + 256] = ref[0, j, core, :, e * 256 : e * 256 + 256].astype(f32)
                for t in range(3):
                    lane = 512 + t * 128 + e * 64
                    both = [ref[0, j, core, :, lane : lane + 64].astype(f32) for core in range(2)]
                    at = t * 1024 + j * 256 + e * 128
                    qkv_ref[0, :, at : at + 128] = jnp.concatenate(both, axis=1)

    @pl.when(pl.program_id(0) == 0)
    def _():
        put(first_ref)

    @pl.when(pl.program_id(0) == 1)
    def _():
        put(second_ref)


def assemble(at, first, second):
    block = (1, 4, 2, 64, 896)
    return call(
        assemble_kernel,
        at,
        (first, second),
        (jax.ShapeDtypeStruct((LAYERS, 128, 4096), f32), jax.ShapeDtypeStruct((LAYERS, 128, 3072), f32)),
        (LAYERS, 2),
        [
            pl.BlockSpec(block, lambda l, h, at: (h, 0, 0, 0, 0)),
            pl.BlockSpec(block, lambda l, h, at: (h, 0, 0, 0, 0)),
        ],
        (
            pl.BlockSpec((1, 64, 4096), lambda l, h, at: (l, h, 0)),
            pl.BlockSpec((1, 64, 3072), lambda l, h, at: (l, h, 0)),
        ),
    )


def head_scores(q, k, seen, distance, slope):
    s = lax.dot_general(q, k, (((1,), (1,)), ((), ())), preferred_element_type=f32) * HEAD_DIM ** (-0.5)
    s = s - slope * distance
    return jnp.where(seen, s, f32(-1000000000.0))


def visibility(row_start, col_start):
    row = lax.broadcasted_iota(jnp.int32, (RUN, RUN), 0)
    col = lax.broadcasted_iota(jnp.int32, (RUN, RUN), 1)
    seen = (row_start == col_start) & (col <= row)
    return seen, (row - col).astype(f32)


def attend_kernel(slope_ref, rows_ref, cols_ref, qkv_ref, ctx_ref):
    first = pl.program_id(1) * 4
    seen, distance = visibility(rows_ref[0], cols_ref[0])
    done = []
    for i in range(4):
        at = (i // 2) * 384 + (i % 2) * 64
        q = qkv_ref[:, at : at + 64]
        k = qkv_ref[:, at + 128 : at + 192]
        v = qkv_ref[:, at + 256 : at + 320]
        s = head_scores(q, k, seen, distance, slope_ref[first + i])
        top = jnp.max(s, axis=-1, keepdims=True)
        lse = top + jnp.log(jnp.sum(jnp.exp(s - top), axis=-1, keepdims=True))
        p = jnp.exp(s - lse).astype(bf16)
        done.append(jnp.dot(p, v, preferred_element_type=f32))
    ctx_ref[...] = jnp.concatenate(done, axis=1).astype(bf16)


def attend_back_kernel(slope_ref, rows_ref, cols_ref, qkv_ref, ctx_ref, dctx_ref, dqkv_ref, dq_ref, dv_ref):
    first = pl.program_id(1) * 4
    seen, distance = visibility(rows_ref[0], cols_ref[0])
    dqs, dks, dvs = [], [], []
    tn = (((0,), (0,)), ((), ()))
    nt = (((1,), (1,)), ((), ()))
    for i in range(4):
        lanes = slice(i * 64, i * 64 + 64)
        at = (i // 2) * 384 + (i % 2) * 64
        q = qkv_ref[:, at : at + 64]
        k = qkv_ref[:, at + 128 : at + 192]
        v = qkv_ref[:, at + 256 : at + 320]
        s = head_scores(q, k, seen, distance, slope_ref[first + i])
        top = jnp.max(s, axis=-1, keepdims=True)
        lse = top + jnp.log(jnp.sum(jnp.exp(s - top), axis=-1, keepdims=True))
        p = jnp.exp(s - lse)
        dctx = dctx_ref[:, lanes]
        dv = lax.dot_general(p.astype(bf16), dctx, tn, preferred_element_type=f32)
        dp = lax.dot_general(dctx, v, nt, preferred_element_type=f32)
        delta = jnp.sum(dctx.astype(f32) * ctx_ref[:, lanes].astype(f32), axis=-1, keepdims=True)
        ds = (p * (dp - delta)).astype(bf16)
        dqs.append(jnp.dot(ds, k, preferred_element_type=f32) * HEAD_DIM ** (-0.5))
        dks.append(lax.dot_general(ds, q, tn, preferred_element_type=f32) * HEAD_DIM ** (-0.5))
        dvs.append(dv)
    for pair in range(2):
        at = pair * 384
        dq = jnp.concatenate(dqs[2 * pair : 2 * pair + 2], axis=1)
        dk = jnp.concatenate(dks[2 * pair : 2 * pair + 2], axis=1)
        dv = jnp.concatenate(dvs[2 * pair : 2 * pair + 2], axis=1)
        dqkv_ref[:, at : at + 128] = dq.astype(bf16)
        dqkv_ref[:, at + 128 : at + 256] = dk.astype(bf16)
        dqkv_ref[:, at + 256 : at + 384] = dv.astype(bf16)
        dq_ref[0, 0, :, pair * 128 : pair * 128 + 128] = jnp.sum(dq, axis=0, keepdims=True)
        dv_ref[0, 0, :, pair * 128 : pair * 128 + 128] = jnp.sum(dv, axis=0, keepdims=True)


def attend(qkv, rows, cols, slopes):
    return pl.pallas_call(
        attend_kernel,
        out_shape=jax.ShapeDtypeStruct((2 * RUN, 512), bf16),
        grid=(2, 2),
        in_specs=[
            pl.BlockSpec(memory_space=pltpu.SMEM),
            pl.BlockSpec((1, RUN, 1), lambda r, p: (r, 0, 0)),
            pl.BlockSpec((1, 1, RUN), lambda r, p: (r, 0, 0)),
            pl.BlockSpec((RUN, 768), lambda r, p: (r, p)),
        ],
        out_specs=pl.BlockSpec((RUN, 256), lambda r, p: (r, p)),
        compiler_params=pltpu.CompilerParams(vmem_limit_bytes=8 * 1024 * 1024),
        cost_estimate=pl.CostEstimate(flops=4 * 16 * RUN * RUN * 64, bytes_accessed=1 << 20, transcendentals=32 * RUN * RUN),
    )(slopes, rows, cols, qkv)


def attend_back(qkv, ctx, dctx, rows, cols, slopes):
    row_block = pl.BlockSpec((RUN, 256), lambda r, p: (r, p))
    sums = pl.BlockSpec((1, 1, 1, 256), lambda r, p: (r, p, 0, 0))
    return pl.pallas_call(
        attend_back_kernel,
        out_shape=(
            jax.ShapeDtypeStruct((2 * RUN, 1536), bf16),
            jax.ShapeDtypeStruct((2, 2, 1, 256), f32),
            jax.ShapeDtypeStruct((2, 2, 1, 256), f32),
        ),
        grid=(2, 2),
        in_specs=[
            pl.BlockSpec(memory_space=pltpu.SMEM),
            pl.BlockSpec((1, RUN, 1), lambda r, p: (r, 0, 0)),
            pl.BlockSpec((1, 1, RUN), lambda r, p: (r, 0, 0)),
            pl.BlockSpec((RUN, 768), lambda r, p: (r, p)),
            row_block,
            row_block,
        ],
        out_specs=(pl.BlockSpec((RUN, 768), lambda r, p: (r, p)), sums, sums),
        compiler_params=pltpu.CompilerParams(vmem_limit_bytes=8 * 1024 * 1024),
        cost_estimate=pl.CostEstimate(flops=10 * 16 * RUN * RUN * 64, bytes_accessed=1 << 21, transcendentals=32 * RUN * RUN),
    )(slopes, rows, cols, qkv, ctx, dctx)


def layer_norm(stream, gains, shifts):
    average = jnp.mean(stream, axis=-1, keepdims=True)
    centered = stream - average
    variance = jnp.mean(centered * centered, axis=-1, keepdims=True)
    inv_std = lax.rsqrt(variance + epsilon)
    normed = centered * inv_std
    return (normed * gains + shifts, normed, inv_std)


def norm_back(grad_norm, normed, inv_std, gains):
    scaled = grad_norm * gains
    inner = (
        scaled
        - jnp.mean(scaled, axis=-1, keepdims=True)
        - normed * jnp.mean(scaled * normed, axis=-1, keepdims=True)
    )
    return (inv_std * inner, jnp.sum(grad_norm * normed, axis=0), jnp.sum(grad_norm, axis=0))


def gelu_tanh(values):
    inner = jnp.tanh(gelu_coef * (values + 0.044715 * values * values * values))
    return 0.5 * values * (1.0 + inner)


def gelu_slope(values):
    inner = jnp.tanh(gelu_coef * (values + 0.044715 * values * values * values))
    return 0.5 * (1.0 + inner) + 0.5 * values * (1.0 - inner * inner) * gelu_coef * (
        1.0 + 3.0 * 0.044715 * values * values
    )


def dot(a, b):
    return jnp.dot(a, b, preferred_element_type=f32)


def dot_nt(a, b):
    return lax.dot_general(a, b, (((1,), (1,)), ((), ())), preferred_element_type=f32)


def dot_tn(a, b):
    return lax.dot_general(a, b, (((0,), (0,)), ((), ())), preferred_element_type=f32)


def local(hidden_in, doc_start, grad_out, w_qkv, w_proj, w_up, w_down, norm_gain, d_bias, up_bias):
    z, core = lax.axis_index("z"), lax.axis_index("core")
    at = jnp.stack([z, core]).astype(jnp.int32)
    index = jnp.arange(8, dtype=jnp.int32)

    def both(own):
        return jnp.concatenate([own, swap(own)], axis=0)

    def halves_summed(partial):
        return partial[:RUN] + swap(partial[RUN:])

    small = jnp.concatenate(
        [
            jnp.transpose(jnp.concatenate([norm_gain, d_bias], axis=2), (0, 2, 1)).reshape(16, 128),
            up_bias.reshape(8, 128),
        ]
    )
    small = to_all(small, SHARD, 8).reshape(4, 2, 24, 128).astype(f32)
    wide = jnp.transpose(small[:, :, :16], (2, 0, 1, 3)).reshape(LAYERS, 8, D)
    hidden_bias = small[:, :, 16:].reshape(4, 2, LAYERS, 2, 256)

    def core_heads(vector):
        picked = lax.dynamic_index_in_dim(vector.reshape(4, 2, 2, 64), core, axis=2, keepdims=False)
        return rolled(picked.reshape(4, 128), z)

    mine_z, mine_x = select_weights(at, w_qkv, w_proj, w_up, w_down)
    weights, earlier = [], None
    for layer in range(LAYERS):
        piece_z, piece_x = mine_z[layer], mine_x[layer]
        if earlier is not None:
            piece_z, piece_x = after(piece_z, earlier[0]), after(piece_x, earlier[1])
        block_z = to_all(piece_z, SHARD, 8).reshape(D, 896)
        all_x = lax.all_gather(piece_x, SHARD, axis=0)
        earlier_z = block_z
        if earlier is not None:
            block_z = after(block_z, earlier[2])
        own, following, (top, bottom), previous = ring_gather(block_z, z_up, z_down)
        earlier = (earlier_z, all_x[0], top)
        wup, wqkv = split_z(at, own, following, top, bottom, previous)
        wdown, wproj = split_x(at, all_x)
        weights.append((wqkv, wproj, wup, wdown))

    starts = both(doc_start.reshape(1, RUN))
    rows, cols = starts.reshape(2, RUN, 1), starts.reshape(2, 1, RUN)
    head = 4 * ((z + index // 2) % 4) + 2 * (index % 2) + core
    slopes = 2.0 ** (-8.0 * (head.astype(f32) + 1.0) / HEADS)

    kept = []
    current = hidden_in
    for layer in range(LAYERS):
        wqkv, wproj, wup, wdown = weights[layer]
        gain_one, gain_two, shift_one, shift_two, bq, bv, bproj, bdown = (wide[layer, i] for i in range(8))
        bq, bv = core_heads(bq), core_heads(bv)
        bqkv = jnp.stack([bq, jnp.zeros_like(bq), bv], axis=1).reshape(1536)
        ubias = lax.dynamic_index_in_dim(hidden_bias[:, :, layer], core, axis=2, keepdims=False)
        ubias = rolled(ubias.reshape(4, 512), z).reshape(2048)
        first_f, normed_one, inv_one = layer_norm(current, gain_one, shift_one)
        first_in = both(first_f.astype(bf16))
        qkv = (dot(first_in, wqkv) + bqkv).astype(bf16)
        ctx = attend(qkv, rows, cols, slopes)
        middle = current + halves_summed(dot(ctx, wproj)) + bproj
        second_f, normed_two, inv_two = layer_norm(middle, gain_two, shift_two)
        second_in = both(second_f.astype(bf16))
        upper = dot(second_in, wup) + ubias
        activ = gelu_tanh(upper).astype(bf16)
        current = middle + halves_summed(dot(activ, wdown)) + bdown
        kept.append((first_in, normed_one, inv_one, qkv, ctx, second_in, normed_two, inv_two, upper, activ, gain_one, gain_two))
    hidden_out = current

    def summed(blocks):
        return jnp.sum(blocks.astype(f32), axis=0).astype(bf16)

    def reduce_z(a2, dub, a1, dqkv):
        parts = [grad_z(at, a2, dub, a1, dqkv, i) for i in (2, 1, 3, 0)]
        parts = [parts[i] for i in (3, 1, 0, 2)]
        part = ring_scatter(parts, z_up, z_down).astype(bf16)
        part = jnp.transpose(part.reshape(8, 2, 64, 896), (1, 0, 2, 3)).reshape(16, 64, 896)
        part = summed(exchange(part, ("ylo", "x", "yhi")))
        return lax.all_gather(part, REP, axis=0).reshape(2, 4, 2, 64, 896)

    def reduce_x(m, dy, ctx, dr):
        part = lax.psum_scatter(grad_x(at, m, dy, ctx, dr), SHARD, scatter_dimension=0, tiled=True)[0]
        part = jnp.concatenate([part[:256].reshape(8, 32, D), part[256:].reshape(8, 8, D)], axis=1)
        part = summed(exchange(part, ("ylo", "z")))
        part = lax.all_gather(part, REP, axis=0).reshape(8, 2, 40, D)
        part = jnp.transpose(part, (1, 0, 2, 3))
        return part[:, :, :32].reshape(512, D), part[:, :, 32:].reshape(128, D)

    grads_x, grads_z = [None] * LAYERS, [None] * LAYERS
    thin_grads, head_grads, unit_grads = [None] * LAYERS, [None] * LAYERS, [None] * LAYERS
    running = grad_out
    for layer in reversed(range(LAYERS)):
        wqkv, wproj, wup, wdown = weights[layer]
        first_in, normed_one, inv_one, qkv, ctx, second_in, normed_two, inv_two, upper, activ, gain_one, gain_two = kept[layer]
        g_bdown = jnp.sum(running, axis=0)
        grad_yb = both(running.astype(bf16))
        grad_upper = dot_nt(grad_yb, wdown) * gelu_slope(upper)
        g_ubias = jnp.sum(grad_upper, axis=0)
        grad_ub = grad_upper.astype(bf16)
        grad_two = halves_summed(dot_nt(grad_ub, wup))
        back_two, g_gain_two, g_shift_two = norm_back(grad_two, normed_two, inv_two, gain_two)
        grad_mid = running + back_two
        g_bproj = jnp.sum(grad_mid, axis=0)
        grad_midb = both(grad_mid.astype(bf16))
        grad_ctx = dot_nt(grad_midb, wproj).astype(bf16)
        grads_x[layer] = reduce_x(activ, grad_yb, ctx, grad_midb)
        grad_qkv, g_bq, g_bv = attend_back(qkv, ctx, grad_ctx, rows, cols, slopes)
        grads_z[layer] = reduce_z(second_in, grad_ub, first_in, grad_qkv)
        grad_one = halves_summed(dot_nt(grad_qkv, wqkv))
        back_one, g_gain_one, g_shift_one = norm_back(grad_one, normed_one, inv_one, gain_one)
        running = grad_mid + back_one

        thin_grads[layer] = [g_gain_one, g_gain_two, g_shift_one, g_shift_two, g_bproj, g_bdown]
        head_grads[layer] = [jnp.sum(g, axis=0).reshape(4, 128) for g in (g_bq, g_bv)]
        unit_grads[layer] = g_ubias.reshape(4, 512)

    thin = jnp.stack(thin_grads[0] + thin_grads[1]).reshape(LAYERS, 6, 4, 2, 128)
    heads = jnp.stack(head_grads[0] + head_grads[1], axis=1)
    heads = rolled(heads, (4 - z) % 4).reshape(4, LAYERS, 2, 2, 1, 64)
    mine = lax.broadcasted_iota(jnp.int32, (4, LAYERS, 2, 2, 2, 64), 4) == core
    heads = jnp.where(mine, heads, 0.0).reshape(4, LAYERS, 2, 2, 128)
    units = rolled(jnp.stack(unit_grads, axis=1), (4 - z) % 4).reshape(4, LAYERS, 2, 1, 256)
    mine = lax.broadcasted_iota(jnp.int32, (4, LAYERS, 2, 2, 256), 3) == core
    units = jnp.where(mine, units, 0.0).reshape(4, LAYERS, 2, 4, 128)
    thin = jnp.transpose(thin, (2, 3, 0, 1, 4))
    heads = jnp.transpose(heads, (0, 3, 1, 2, 4))
    units = jnp.transpose(units, (0, 2, 1, 3, 4))
    part = jnp.concatenate([thin[:, :, :, :4], heads, thin[:, :, :, 4:], units], axis=3)
    part = jnp.sum(exchange(part.reshape(8, 24, 128), SHARD), axis=0)
    part = jnp.sum(to_all(part, REP, 16), axis=0).reshape(LAYERS, 12, 128)
    g_wide = jnp.transpose(part[:, :8], (0, 2, 1))
    g_up, g_qkv = assemble(at, grads_z[0], grads_z[1])
    g_down, g_proj = (jnp.stack([grads_x[layer][i] for layer in range(LAYERS)]).astype(f32) for i in range(2))
    return (
        hidden_out,
        running,
        g_qkv,
        g_proj,
        g_up,
        g_down,
        g_wide[:, :, :2],
        g_wide[:, :, 2:],
        part[:, 8:].reshape(LAYERS, 512),
    )


def solution(mesh):
    fine = Mesh(mesh.devices.reshape(2, 4, 2, 4, 2), AXES)
    tokens = P(AXES)
    wide_tokens = P(AXES, None)
    params = P(None, ("x", "yhi"), None)
    return jax.shard_map(
        local,
        mesh=fine,
        in_specs=(wide_tokens, tokens, wide_tokens, params, params, params, params, params, params, P(None, ("x", "yhi"))),
        out_specs=(wide_tokens, wide_tokens, params, params, params, params, params, params, P(None, ("x", "yhi"))),
        check_vma=False,
    )
```

```python
import jax
import jax.numpy as jnp
from jax import lax
from jax.experimental import pallas as pl
from jax.experimental.pallas import tpu as pltpu
from jax.sharding import Mesh
from jax.sharding import PartitionSpec as P

HEADS = 16
HEAD_DIM = 64
LAYERS = 2
D = 1024
RUN = 128

epsilon = 1e-05
gelu_coef = 0.7978845608
f32 = jnp.float32
bf16 = jnp.bfloat16

AXES = ("ylo", "z", "core", "x", "yhi")


def ring(step):
    return [(i, (i + step) % 4) for i in range(4)]


def z_up(a):
    return lax.ppermute(a, "z", ring(1))


def z_down(a):
    return lax.ppermute(a, "z", ring(3))


def swap(a):
    return lax.ppermute(a, "core", [(0, 1), (1, 0)])


SHARD = ("x", "yhi")
REP = ("ylo", "z", "core")


def exchange(blocks, axes):
    return lax.all_to_all(blocks, axes, 0, 0, tiled=True)


def to_all(a, axes, count):
    return exchange(jnp.broadcast_to(a[None], (count, *a.shape)), axes)


def ring_gather(a, up, down):
    half = a.shape[0] // 2
    previous = up(a)
    following = down(a)
    top = up(previous[:half])
    bottom = down(following[half:])
    return a, following, (top, bottom), previous


def ring_scatter(parts, up, down):
    own, following, far, previous = parts
    half = own.shape[0] // 2
    from_previous = up(far[:half])
    from_following = down(far[half:])
    go_up = jnp.concatenate(
        [(following[:half].astype(f32) + from_previous.astype(f32)).astype(bf16), following[half:]]
    )
    go_down = jnp.concatenate(
        [previous[:half], (previous[half:].astype(f32) + from_following.astype(f32)).astype(bf16)]
    )
    got_up = up(go_up)
    got_down = down(go_down)
    total = own.astype(f32) + got_up.astype(f32) + got_down.astype(f32)
    return total, (following, previous), (from_previous, from_following), (got_up, got_down)


def rolled(stack, start):
    return lax.dynamic_slice_in_dim(jnp.concatenate([stack, stack[:3]]), start, 4, axis=0)


def after(a, *earlier):
    there = sum(jnp.abs(e[0, 0].astype(f32)) * 2.0**-40 for e in earlier) < 1e30
    return jnp.where(there, a, jnp.zeros_like(a))


def select_kernel(at_ref, up_a, up_b, q_ref, k_ref, v_ref, down_ref, proj_ref, by_z_ref, by_x_ref):
    first = at_ref[1] == 0
    by_z_ref[0, :, 0:256] = up_a[0]
    by_z_ref[0, :, 256:512] = up_b[0]
    for t, ref in enumerate((q_ref, k_ref, v_ref)):
        low = jnp.where(first, ref[0, :, 0:64].astype(f32), ref[0, :, 64:128].astype(f32))
        high = jnp.where(first, ref[0, :, 128:192].astype(f32), ref[0, :, 192:256].astype(f32))
        by_z_ref[0, :, 512 + t * 128 : 640 + t * 128] = jnp.concatenate([low, high], axis=1).astype(bf16)
    by_x_ref[0, 0:256] = down_ref[0]
    by_x_ref[0, 256:320] = proj_ref[0]


def select_weights(at, w_qkv, w_proj, w_up, w_down):
    def lanes(block):
        return pl.BlockSpec((1, 128, 256), lambda l, at: (l, 0, block(at)))

    return pl.pallas_call(
        select_kernel,
        out_shape=(
            jax.ShapeDtypeStruct((LAYERS, 128, 896), bf16),
            jax.ShapeDtypeStruct((LAYERS, 320, D), bf16),
        ),
        grid_spec=pltpu.PrefetchScalarGridSpec(
            num_scalar_prefetch=1,
            grid=(LAYERS,),
            in_specs=[
                lanes(lambda at: 4 * at[0] + at[1]),
                lanes(lambda at: 4 * at[0] + 2 + at[1]),
                lanes(lambda at: at[0]),
                lanes(lambda at: 4 + at[0]),
                lanes(lambda at: 8 + at[0]),
                pl.BlockSpec((1, 256, D), lambda l, at: (l, at[1], 0)),
                pl.BlockSpec((1, 64, D), lambda l, at: (l, at[1], 0)),
            ],
            out_specs=(
                pl.BlockSpec((1, 128, 896), lambda l, at: (l, 0, 0)),
                pl.BlockSpec((1, 320, D), lambda l, at: (l, 0, 0)),
            ),
        ),
        compiler_params=pltpu.CompilerParams(vmem_limit_bytes=8 * 1024 * 1024),
        cost_estimate=pl.CostEstimate(flops=0, bytes_accessed=4 * 1024 * 1024, transcendentals=0),
    )(at, w_up, w_up, w_qkv, w_qkv, w_qkv, w_down, w_proj)


def call(kernel, scalars, operands, out_shape, grid, in_specs, out_specs, flops=0):
    moved = sum(a.size * a.dtype.itemsize for a in operands) + sum(o.size * o.dtype.itemsize for o in jax.tree.leaves(out_shape))
    return pl.pallas_call(
        kernel,
        out_shape=out_shape,
        grid_spec=pltpu.PrefetchScalarGridSpec(
            num_scalar_prefetch=1, grid=grid, in_specs=in_specs, out_specs=out_specs
        ),
        compiler_params=pltpu.CompilerParams(vmem_limit_bytes=20 * 1024 * 1024),
        cost_estimate=pl.CostEstimate(flops=flops, bytes_accessed=moved, transcendentals=0),
    )(scalars, *operands)


def split_z_kernel(at_ref, own_ref, next_ref, top_ref, bottom_ref, last_ref, up_ref, qkv_ref):
    step = pl.program_id(0)

    def put(position, block):
        up_ref[:, position * 512 : position * 512 + 512] = block[:, :512]
        qkv_ref[:, position * 384 : position * 384 + 384] = block[:, 512:]

    put(0, own_ref)
    put(1, next_ref)
    put(3, last_ref)

    @pl.when(step < 4)
    def _():
        put(2, top_ref)

    @pl.when(step >= 4)
    def _():
        put(2, bottom_ref)


def split_z(at, own, following, top, bottom, previous):
    block = pl.BlockSpec((128, 896), lambda i, at: (i, 0))
    return call(
        split_z_kernel,
        at,
        (own, following, top, bottom, previous),
        (jax.ShapeDtypeStruct((D, 2048), bf16), jax.ShapeDtypeStruct((D, 1536), bf16)),
        (8,),
        [
            block,
            block,
            pl.BlockSpec((128, 896), lambda i, at: (jnp.minimum(i, 3), 0)),
            pl.BlockSpec((128, 896), lambda i, at: (jnp.maximum(i - 4, 0), 0)),
            block,
        ],
        (pl.BlockSpec((128, 2048), lambda i, at: (i, 0)), pl.BlockSpec((128, 1536), lambda i, at: (i, 0))),
    )


def split_x_kernel(at_ref, in_ref, down_ref, proj_ref):
    for e in range(2):
        down_ref[e * 256 : e * 256 + 256] = in_ref[e, 0:256]
        proj_ref[e * 64 : e * 64 + 64] = in_ref[e, 256:320]


def split_x(at, gathered):
    return call(
        split_x_kernel,
        at,
        (gathered,),
        (jax.ShapeDtypeStruct((2048, D), bf16), jax.ShapeDtypeStruct((512, D), bf16)),
        (4,),
        [pl.BlockSpec((2, 320, D), lambda i, at: (lax.rem(i + at[0], 4), 0, 0))],
        (pl.BlockSpec((512, D), lambda i, at: (i, 0)), pl.BlockSpec((128, D), lambda i, at: (i, 0))),
    )


def grad_z_kernel(at_ref, a2_ref, dub_ref, a1_ref, dqkv_ref, out_ref):
    out_ref[:, :512] = dot_tn(a2_ref[...], dub_ref[...]).astype(bf16)
    out_ref[:, 512:] = dot_tn(a1_ref[...], dqkv_ref[...]).astype(bf16)


def grad_z(at, a2, dub, a1, dqkv, block):
    rows = pl.BlockSpec((256, 256), lambda i, at: (0, i))
    return call(
        grad_z_kernel,
        at,
        (a2, dub, a1, dqkv),
        jax.ShapeDtypeStruct((D, 896), bf16),
        (4,),
        [
            rows,
            pl.BlockSpec((256, 512), lambda i, at: (0, block)),
            rows,
            pl.BlockSpec((256, 384), lambda i, at: (0, block)),
        ],
        pl.BlockSpec((256, 896), lambda i, at: (i, 0)),
        flops=2 * 256 * D * 896,
    )


def grad_x_kernel(at_ref, m_ref, dy_ref, ctx_ref, dr_ref, out_ref):
    for e in range(2):
        out_ref[e, 0:256] = dot_tn(m_ref[:, e * 256 : e * 256 + 256], dy_ref[...]).astype(bf16)
        out_ref[e, 256:320] = dot_tn(ctx_ref[:, e * 64 : e * 64 + 64], dr_ref[...]).astype(bf16)


def grad_x(at, m, dy, ctx, dr):
    whole = pl.BlockSpec((256, D), lambda i, at: (0, 0))
    return call(
        grad_x_kernel,
        at,
        (m, dy, ctx, dr),
        jax.ShapeDtypeStruct((8, 320, D), bf16),
        (4,),
        [
            pl.BlockSpec((256, 512), lambda i, at: (0, i)),
            whole,
            pl.BlockSpec((256, 128), lambda i, at: (0, i)),
            whole,
        ],
        pl.BlockSpec((2, 320, D), lambda i, at: (lax.rem(i + at[0], 4), 0, 0)),
        flops=2 * 256 * D * 2560,
    )


def assemble_kernel(at_ref, first_ref, second_ref, up_ref, qkv_ref):
    def put(ref):
        for j in range(4):
            for e in range(2):
                for core in range(2):
                    at = j * 1024 + e * 512 + core * 256
                    up_ref[0, :, at : at + 256] = ref[0, j, core, :, e * 256 : e * 256 + 256].astype(f32)
                for t in range(3):
                    lane = 512 + t * 128 + e * 64
                    both = [ref[0, j, core, :, lane : lane + 64].astype(f32) for core in range(2)]
                    at = t * 1024 + j * 256 + e * 128
                    qkv_ref[0, :, at : at + 128] = jnp.concatenate(both, axis=1)

    @pl.when(pl.program_id(0) == 0)
    def _():
        put(first_ref)

    @pl.when(pl.program_id(0) == 1)
    def _():
        put(second_ref)


def assemble(at, first, second):
    block = (1, 4, 2, 64, 896)
    return call(
        assemble_kernel,
        at,
        (first, second),
        (jax.ShapeDtypeStruct((LAYERS, 128, 4096), f32), jax.ShapeDtypeStruct((LAYERS, 128, 3072), f32)),
        (LAYERS, 2),
        [
            pl.BlockSpec(block, lambda l, h, at: (h, 0, 0, 0, 0)),
            pl.BlockSpec(block, lambda l, h, at: (h, 0, 0, 0, 0)),
        ],
        (
            pl.BlockSpec((1, 64, 4096), lambda l, h, at: (l, h, 0)),
            pl.BlockSpec((1, 64, 3072), lambda l, h, at: (l, h, 0)),
        ),
    )


def head_scores(q, k, seen, distance, slope):
    s = lax.dot_general(q, k, (((1,), (1,)), ((), ())), preferred_element_type=f32) * HEAD_DIM ** (-0.5)
    s = s - slope * distance
    return jnp.where(seen, s, f32(-1000000000.0))


def visibility(row_start, col_start):
    row = lax.broadcasted_iota(jnp.int32, (RUN, RUN), 0)
    col = lax.broadcasted_iota(jnp.int32, (RUN, RUN), 1)
    seen = (row_start == col_start) & (col <= row)
    return seen, (row - col).astype(f32)


def attend_kernel(slope_ref, rows_ref, cols_ref, qkv_ref, ctx_ref):
    first = pl.program_id(1) * 4
    seen, distance = visibility(rows_ref[0], cols_ref[0])
    done = []
    for i in range(4):
        at = (i // 2) * 384 + (i % 2) * 64
        q = qkv_ref[:, at : at + 64]
        k = qkv_ref[:, at + 128 : at + 192]
        v = qkv_ref[:, at + 256 : at + 320]
        s = head_scores(q, k, seen, distance, slope_ref[first + i])
        top = jnp.max(s, axis=-1, keepdims=True)
        lse = top + jnp.log(jnp.sum(jnp.exp(s - top), axis=-1, keepdims=True))
        p = jnp.exp(s - lse).astype(bf16)
        done.append(jnp.dot(p, v, preferred_element_type=f32))
    ctx_ref[...] = jnp.concatenate(done, axis=1).astype(bf16)


def attend_back_kernel(slope_ref, rows_ref, cols_ref, qkv_ref, ctx_ref, dctx_ref, dqkv_ref, dq_ref, dv_ref):
    first = pl.program_id(1) * 4
    seen, distance = visibility(rows_ref[0], cols_ref[0])
    dqs, dks, dvs = [], [], []
    tn = (((0,), (0,)), ((), ()))
    nt = (((1,), (1,)), ((), ()))
    for i in range(4):
        lanes = slice(i * 64, i * 64 + 64)
        at = (i // 2) * 384 + (i % 2) * 64
        q = qkv_ref[:, at : at + 64]
        k = qkv_ref[:, at + 128 : at + 192]
        v = qkv_ref[:, at + 256 : at + 320]
        s = head_scores(q, k, seen, distance, slope_ref[first + i])
        top = jnp.max(s, axis=-1, keepdims=True)
        lse = top + jnp.log(jnp.sum(jnp.exp(s - top), axis=-1, keepdims=True))
        p = jnp.exp(s - lse)
        dctx = dctx_ref[:, lanes]
        dv = lax.dot_general(p.astype(bf16), dctx, tn, preferred_element_type=f32)
        dp = lax.dot_general(dctx, v, nt, preferred_element_type=f32)
        delta = jnp.sum(dctx.astype(f32) * ctx_ref[:, lanes].astype(f32), axis=-1, keepdims=True)
        ds = (p * (dp - delta)).astype(bf16)
        dqs.append(jnp.dot(ds, k, preferred_element_type=f32) * HEAD_DIM ** (-0.5))
        dks.append(lax.dot_general(ds, q, tn, preferred_element_type=f32) * HEAD_DIM ** (-0.5))
        dvs.append(dv)
    for pair in range(2):
        at = pair * 384
        dq = jnp.concatenate(dqs[2 * pair : 2 * pair + 2], axis=1)
        dk = jnp.concatenate(dks[2 * pair : 2 * pair + 2], axis=1)
        dv = jnp.concatenate(dvs[2 * pair : 2 * pair + 2], axis=1)
        dqkv_ref[:, at : at + 128] = dq.astype(bf16)
        dqkv_ref[:, at + 128 : at + 256] = dk.astype(bf16)
        dqkv_ref[:, at + 256 : at + 384] = dv.astype(bf16)
        dq_ref[0, 0, :, pair * 128 : pair * 128 + 128] = jnp.sum(dq, axis=0, keepdims=True)
        dv_ref[0, 0, :, pair * 128 : pair * 128 + 128] = jnp.sum(dv, axis=0, keepdims=True)


def attend(qkv, rows, cols, slopes):
    return pl.pallas_call(
        attend_kernel,
        out_shape=jax.ShapeDtypeStruct((2 * RUN, 512), bf16),
        grid=(2, 2),
        in_specs=[
            pl.BlockSpec(memory_space=pltpu.SMEM),
            pl.BlockSpec((1, RUN, 1), lambda r, p: (r, 0, 0)),
            pl.BlockSpec((1, 1, RUN), lambda r, p: (r, 0, 0)),
            pl.BlockSpec((RUN, 768), lambda r, p: (r, p)),
        ],
        out_specs=pl.BlockSpec((RUN, 256), lambda r, p: (r, p)),
        compiler_params=pltpu.CompilerParams(vmem_limit_bytes=8 * 1024 * 1024),
        cost_estimate=pl.CostEstimate(flops=4 * 16 * RUN * RUN * 64, bytes_accessed=1 << 20, transcendentals=32 * RUN * RUN),
    )(slopes, rows, cols, qkv)


def attend_back(qkv, ctx, dctx, rows, cols, slopes):
    row_block = pl.BlockSpec((RUN, 256), lambda r, p: (r, p))
    sums = pl.BlockSpec((1, 1, 1, 256), lambda r, p: (r, p, 0, 0))
    return pl.pallas_call(
        attend_back_kernel,
        out_shape=(
            jax.ShapeDtypeStruct((2 * RUN, 1536), bf16),
            jax.ShapeDtypeStruct((2, 2, 1, 256), f32),
            jax.ShapeDtypeStruct((2, 2, 1, 256), f32),
        ),
        grid=(2, 2),
        in_specs=[
            pl.BlockSpec(memory_space=pltpu.SMEM),
            pl.BlockSpec((1, RUN, 1), lambda r, p: (r, 0, 0)),
            pl.BlockSpec((1, 1, RUN), lambda r, p: (r, 0, 0)),
            pl.BlockSpec((RUN, 768), lambda r, p: (r, p)),
            row_block,
            row_block,
        ],
        out_specs=(pl.BlockSpec((RUN, 768), lambda r, p: (r, p)), sums, sums),
        compiler_params=pltpu.CompilerParams(vmem_limit_bytes=8 * 1024 * 1024),
        cost_estimate=pl.CostEstimate(flops=10 * 16 * RUN * RUN * 64, bytes_accessed=1 << 21, transcendentals=32 * RUN * RUN),
    )(slopes, rows, cols, qkv, ctx, dctx)


def layer_norm(stream, gains, shifts):
    average = jnp.mean(stream, axis=-1, keepdims=True)
    centered = stream - average
    variance = jnp.mean(centered * centered, axis=-1, keepdims=True)
    inv_std = lax.rsqrt(variance + epsilon)
    normed = centered * inv_std
    return (normed * gains + shifts, normed, inv_std)


def norm_back(grad_norm, normed, inv_std, gains):
    scaled = grad_norm * gains
    inner = (
        scaled
        - jnp.mean(scaled, axis=-1, keepdims=True)
        - normed * jnp.mean(scaled * normed, axis=-1, keepdims=True)
    )
    return (inv_std * inner, jnp.sum(grad_norm * normed, axis=0), jnp.sum(grad_norm, axis=0))


def gelu_tanh(values):
    inner = jnp.tanh(gelu_coef * (values + 0.044715 * values * values * values))
    return 0.5 * values * (1.0 + inner)


def gelu_slope(values):
    inner = jnp.tanh(gelu_coef * (values + 0.044715 * values * values * values))
    return 0.5 * (1.0 + inner) + 0.5 * values * (1.0 - inner * inner) * gelu_coef * (
        1.0 + 3.0 * 0.044715 * values * values
    )


def dot(a, b):
    return jnp.dot(a, b, preferred_element_type=f32)


def dot_nt(a, b):
    return lax.dot_general(a, b, (((1,), (1,)), ((), ())), preferred_element_type=f32)


def dot_tn(a, b):
    return lax.dot_general(a, b, (((0,), (0,)), ((), ())), preferred_element_type=f32)


def local(hidden_in, doc_start, grad_out, w_qkv, w_proj, w_up, w_down, norm_gain, d_bias, up_bias):
    z, core = lax.axis_index("z"), lax.axis_index("core")
    at = jnp.stack([z, core]).astype(jnp.int32)
    index = jnp.arange(8, dtype=jnp.int32)

    def both(own):
        return jnp.concatenate([own, swap(own)], axis=0)

    def halves_summed(partial):
        return partial[:RUN] + swap(partial[RUN:])

    small = jnp.concatenate(
        [
            jnp.transpose(jnp.concatenate([norm_gain, d_bias], axis=2), (0, 2, 1)).reshape(16, 128),
            up_bias.reshape(8, 128),
        ]
    )
    small = to_all(small, SHARD, 8).reshape(4, 2, 24, 128).astype(f32)
    wide = jnp.transpose(small[:, :, :16], (2, 0, 1, 3)).reshape(LAYERS, 8, D)
    hidden_bias = small[:, :, 16:].reshape(4, 2, LAYERS, 2, 256)

    def core_heads(vector):
        picked = lax.dynamic_index_in_dim(vector.reshape(4, 2, 2, 64), core, axis=2, keepdims=False)
        return rolled(picked.reshape(4, 128), z)

    mine_z, mine_x = select_weights(at, w_qkv, w_proj, w_up, w_down)
    weights, earlier = [], None
    for layer in range(LAYERS):
        piece_z, piece_x = mine_z[layer], mine_x[layer]
        if earlier is None:
            block_z = to_all(piece_z, SHARD, 8).reshape(D, 896)
            all_x = to_all(after(piece_x, block_z), SHARD, 8)
            first_z = block_z
        else:
            block_z = to_all(after(piece_z, first_z), SHARD, 8).reshape(D, 896)
            all_x = lax.all_gather(after(piece_x, first_z), SHARD, axis=0)
            block_z = after(block_z, earlier)
        own, following, (top, bottom), previous = ring_gather(block_z, z_up, z_down)
        earlier = top
        wup, wqkv = split_z(at, own, following, top, bottom, previous)
        wdown, wproj = split_x(at, all_x)
        weights.append((wqkv, wproj, wup, wdown))

    starts = both(doc_start.reshape(1, RUN))
    rows, cols = starts.reshape(2, RUN, 1), starts.reshape(2, 1, RUN)
    head = 4 * ((z + index // 2) % 4) + 2 * (index % 2) + core
    slopes = 2.0 ** (-8.0 * (head.astype(f32) + 1.0) / HEADS)

    kept = []
    current = hidden_in
    for layer in range(LAYERS):
        wqkv, wproj, wup, wdown = weights[layer]
        gain_one, gain_two, shift_one, shift_two, bq, bv, bproj, bdown = (wide[layer, i] for i in range(8))
        bq, bv = core_heads(bq), core_heads(bv)
        bqkv = jnp.stack([bq, jnp.zeros_like(bq), bv], axis=1).reshape(1536)
        ubias = lax.dynamic_index_in_dim(hidden_bias[:, :, layer], core, axis=2, keepdims=False)
        ubias = rolled(ubias.reshape(4, 512), z).reshape(2048)
        first_f, normed_one, inv_one = layer_norm(current, gain_one, shift_one)
        first_in = both(first_f.astype(bf16))
        qkv = (dot(first_in, wqkv) + bqkv).astype(bf16)
        ctx = attend(qkv, rows, cols, slopes)
        middle = current + halves_summed(dot(ctx, wproj)) + bproj
        second_f, normed_two, inv_two = layer_norm(middle, gain_two, shift_two)
        second_in = both(second_f.astype(bf16))
        upper = dot(second_in, wup) + ubias
        activ = gelu_tanh(upper).astype(bf16)
        current = middle + halves_summed(dot(activ, wdown)) + bdown
        kept.append((first_in, normed_one, inv_one, qkv, ctx, second_in, normed_two, inv_two, upper, activ, gain_one, gain_two))
    hidden_out = current

    def summed(blocks):
        return jnp.sum(blocks.astype(f32), axis=0).astype(bf16)

    def reduce_z(a2, dub, a1, dqkv):
        parts = [grad_z(at, a2, dub, a1, dqkv, i) for i in (2, 1, 3, 0)]
        parts = [parts[i] for i in (3, 1, 0, 2)]
        total, sent, near, got = ring_scatter(parts, z_up, z_down)
        part = total.astype(bf16)
        part = jnp.transpose(part.reshape(8, 2, 64, 896), (1, 0, 2, 3)).reshape(16, 64, 896)
        part = summed(exchange(part, ("ylo", "x", "yhi")))
        return lax.all_gather(part, REP, axis=0).reshape(2, 4, 2, 64, 896), (sent, near, got)

    def finish_x(blocks, later):
        part = summed(after(blocks, later))
        part = jnp.concatenate([part[:256].reshape(8, 32, D), part[256:].reshape(8, 8, D)], axis=1)
        part = summed(exchange(part, ("ylo", "z")))
        part = lax.all_gather(part, REP, axis=0).reshape(8, 2, 40, D)
        part = jnp.transpose(part, (1, 0, 2, 3))
        return part[:, :, :32].reshape(512, D), part[:, :, 32:].reshape(128, D)

    grads_x, grads_z = [None] * LAYERS, [None] * LAYERS
    thin_grads, head_grads, unit_grads = [None] * LAYERS, [None] * LAYERS, [None] * LAYERS
    running, ring_state = grad_out, None
    for layer in reversed(range(LAYERS)):
        wqkv, wproj, wup, wdown = weights[layer]
        first_in, normed_one, inv_one, qkv, ctx, second_in, normed_two, inv_two, upper, activ, gain_one, gain_two = kept[layer]
        if ring_state is not None:
            running = after(running, *ring_state[0])
        g_bdown = jnp.sum(running, axis=0)
        grad_yb = both(running.astype(bf16))
        grad_upper = dot_nt(grad_yb, wdown) * gelu_slope(upper)
        g_ubias = jnp.sum(grad_upper, axis=0)
        grad_ub = grad_upper.astype(bf16)
        grad_two = halves_summed(dot_nt(grad_ub, wup))
        back_two, g_gain_two, g_shift_two = norm_back(grad_two, normed_two, inv_two, gain_two)
        grad_mid = running + back_two
        g_bproj = jnp.sum(grad_mid, axis=0)
        grad_midb = grad_mid.astype(bf16)
        if ring_state is not None:
            grad_midb = after(grad_midb, *ring_state[1])
            grads_x[layer + 1] = finish_x(waiting_x, grad_midb)
        grad_midb = both(grad_midb)
        grad_ctx = dot_nt(grad_midb, wproj).astype(bf16)
        waiting_x = exchange(grad_x(at, activ, grad_yb, ctx, grad_midb), SHARD)
        grad_qkv, g_bq, g_bv = attend_back(qkv, ctx, grad_ctx, rows, cols, slopes)
        if ring_state is not None:
            grad_qkv = after(grad_qkv, *ring_state[2])
        grads_z[layer], ring_state = reduce_z(second_in, grad_ub, first_in, grad_qkv)
        grad_one = halves_summed(dot_nt(grad_qkv, wqkv))
        back_one, g_gain_one, g_shift_one = norm_back(grad_one, normed_one, inv_one, gain_one)
        running = grad_mid + back_one

        thin_grads[layer] = [g_gain_one, g_gain_two, g_shift_one, g_shift_two, g_bproj, g_bdown]
        head_grads[layer] = [jnp.sum(g, axis=0).reshape(4, 128) for g in (g_bq, g_bv)]
        unit_grads[layer] = g_ubias.reshape(4, 512)

    grads_x[0] = finish_x(waiting_x, running)

    thin = jnp.stack(thin_grads[0] + thin_grads[1]).reshape(LAYERS, 6, 4, 2, 128)
    heads = jnp.stack(head_grads[0] + head_grads[1], axis=1)
    heads = rolled(heads, (4 - z) % 4).reshape(4, LAYERS, 2, 2, 1, 64)
    mine = lax.broadcasted_iota(jnp.int32, (4, LAYERS, 2, 2, 2, 64), 4) == core
    heads = jnp.where(mine, heads, 0.0).reshape(4, LAYERS, 2, 2, 128)
    units = rolled(jnp.stack(unit_grads, axis=1), (4 - z) % 4).reshape(4, LAYERS, 2, 1, 256)
    mine = lax.broadcasted_iota(jnp.int32, (4, LAYERS, 2, 2, 256), 3) == core
    units = jnp.where(mine, units, 0.0).reshape(4, LAYERS, 2, 4, 128)
    thin = jnp.transpose(thin, (2, 3, 0, 1, 4))
    heads = jnp.transpose(heads, (0, 3, 1, 2, 4))
    units = jnp.transpose(units, (0, 2, 1, 3, 4))
    part = jnp.concatenate([thin[:, :, :, :4], heads, thin[:, :, :, 4:], units], axis=3)
    part = jnp.sum(exchange(part.reshape(8, 24, 128), SHARD), axis=0)
    part = jnp.sum(to_all(part, REP, 16), axis=0).reshape(LAYERS, 12, 128)
    g_wide = jnp.transpose(part[:, :8], (0, 2, 1))
    g_up, g_qkv = assemble(at, grads_z[0], grads_z[1])
    g_down, g_proj = (jnp.stack([grads_x[layer][i] for layer in range(LAYERS)]).astype(f32) for i in range(2))
    return (
        hidden_out,
        running,
        g_qkv,
        g_proj,
        g_up,
        g_down,
        g_wide[:, :, :2],
        g_wide[:, :, 2:],
        part[:, 8:].reshape(LAYERS, 512),
    )


def solution(mesh):
    fine = Mesh(mesh.devices.reshape(2, 4, 2, 4, 2), AXES)
    tokens = P(AXES)
    wide_tokens = P(AXES, None)
    params = P(None, ("x", "yhi"), None)
    return jax.shard_map(
        local,
        mesh=fine,
        in_specs=(wide_tokens, tokens, wide_tokens, params, params, params, params, params, params, P(None, ("x", "yhi"))),
        out_specs=(wide_tokens, wide_tokens, params, params, params, params, params, params, P(None, ("x", "yhi"))),
        check_vma=False,
    )
```

```python
import jax
import jax.numpy as jnp
from jax import lax
from jax.experimental import pallas as pl
from jax.experimental.pallas import tpu as pltpu
from jax.sharding import Mesh
from jax.sharding import PartitionSpec as P

HEADS = 16
HEAD_DIM = 64
LAYERS = 2
D = 1024
RUN = 128

epsilon = 1e-05
gelu_coef = 0.7978845608
f32 = jnp.float32
bf16 = jnp.bfloat16

AXES = ("ylo", "z", "core", "x", "yhi")


def ring(step):
    return [(i, (i + step) % 4) for i in range(4)]


def z_up(a):
    return lax.ppermute(a, "z", ring(1))


def z_down(a):
    return lax.ppermute(a, "z", ring(3))


def swap(a):
    return lax.ppermute(a, "core", [(0, 1), (1, 0)])


SHARD = ("x", "yhi")
REP = ("ylo", "z", "core")


def exchange(blocks, axes):
    return lax.all_to_all(blocks, axes, 0, 0, tiled=True)


def to_all(a, axes, count):
    return exchange(jnp.broadcast_to(a[None], (count, *a.shape)), axes)


def ring_gather(a, up, down):
    half = a.shape[0] // 2
    previous = up(a)
    following = down(a)
    top = up(previous[:half])
    bottom = down(following[half:])
    return a, following, (top, bottom), previous


def ring_scatter(parts, up, down):
    own, following, far, previous = parts
    half = own.shape[0] // 2
    from_previous = up(far[:half])
    from_following = down(far[half:])
    plain_up = up(following[half:])
    plain_down = down(previous[:half])
    sum_up = up((following[:half].astype(f32) + from_previous.astype(f32)).astype(bf16))
    sum_down = down((previous[half:].astype(f32) + from_following.astype(f32)).astype(bf16))
    top = own[:half].astype(f32) + sum_up.astype(f32) + plain_down.astype(f32)
    bottom = own[half:].astype(f32) + plain_up.astype(f32) + sum_down.astype(f32)
    return (top, bottom), (following, previous), (from_previous, from_following), (sum_up, sum_down)


def rolled(stack, start):
    return lax.dynamic_slice_in_dim(jnp.concatenate([stack, stack[:3]]), start, 4, axis=0)


def after(a, *earlier):
    there = sum(jnp.abs(e[0, 0].astype(f32)) * 2.0**-40 for e in earlier) < 1e30
    return jnp.where(there, a, jnp.zeros_like(a))


def select_kernel(at_ref, up_a, up_b, q_ref, k_ref, v_ref, down_ref, proj_ref, by_z_ref, by_x_ref):
    first = at_ref[1] == 0
    by_z_ref[0, :, 0:256] = up_a[0]
    by_z_ref[0, :, 256:512] = up_b[0]
    for t, ref in enumerate((q_ref, k_ref, v_ref)):
        low = jnp.where(first, ref[0, :, 0:64].astype(f32), ref[0, :, 64:128].astype(f32))
        high = jnp.where(first, ref[0, :, 128:192].astype(f32), ref[0, :, 192:256].astype(f32))
        by_z_ref[0, :, 512 + t * 128 : 640 + t * 128] = jnp.concatenate([low, high], axis=1).astype(bf16)
    by_x_ref[0, 0:256] = down_ref[0]
    by_x_ref[0, 256:320] = proj_ref[0]


def select_weights(at, w_qkv, w_proj, w_up, w_down):
    def lanes(block):
        return pl.BlockSpec((1, 128, 256), lambda l, at: (l, 0, block(at)))

    return pl.pallas_call(
        select_kernel,
        out_shape=(
            jax.ShapeDtypeStruct((LAYERS, 128, 896), bf16),
            jax.ShapeDtypeStruct((LAYERS, 320, D), bf16),
        ),
        grid_spec=pltpu.PrefetchScalarGridSpec(
            num_scalar_prefetch=1,
            grid=(LAYERS,),
            in_specs=[
                lanes(lambda at: 4 * at[0] + at[1]),
                lanes(lambda at: 4 * at[0] + 2 + at[1]),
                lanes(lambda at: at[0]),
                lanes(lambda at: 4 + at[0]),
                lanes(lambda at: 8 + at[0]),
                pl.BlockSpec((1, 256, D), lambda l, at: (l, at[1], 0)),
                pl.BlockSpec((1, 64, D), lambda l, at: (l, at[1], 0)),
            ],
            out_specs=(
                pl.BlockSpec((1, 128, 896), lambda l, at: (l, 0, 0)),
                pl.BlockSpec((1, 320, D), lambda l, at: (l, 0, 0)),
            ),
        ),
        compiler_params=pltpu.CompilerParams(vmem_limit_bytes=8 * 1024 * 1024),
        cost_estimate=pl.CostEstimate(flops=0, bytes_accessed=4 * 1024 * 1024, transcendentals=0),
    )(at, w_up, w_up, w_qkv, w_qkv, w_qkv, w_down, w_proj)


def call(kernel, scalars, operands, out_shape, grid, in_specs, out_specs, flops=0):
    moved = sum(a.size * a.dtype.itemsize for a in operands) + sum(o.size * o.dtype.itemsize for o in jax.tree.leaves(out_shape))
    return pl.pallas_call(
        kernel,
        out_shape=out_shape,
        grid_spec=pltpu.PrefetchScalarGridSpec(
            num_scalar_prefetch=1, grid=grid, in_specs=in_specs, out_specs=out_specs
        ),
        compiler_params=pltpu.CompilerParams(vmem_limit_bytes=20 * 1024 * 1024),
        cost_estimate=pl.CostEstimate(flops=flops, bytes_accessed=moved, transcendentals=0),
    )(scalars, *operands)


def split_z_kernel(at_ref, own_ref, next_ref, top_ref, bottom_ref, last_ref, up_ref, qkv_ref):
    step = pl.program_id(0)

    def put(position, block):
        up_ref[:, position * 512 : position * 512 + 512] = block[:, :512]
        qkv_ref[:, position * 384 : position * 384 + 384] = block[:, 512:]

    put(0, own_ref)
    put(1, next_ref)
    put(3, last_ref)

    @pl.when(step < 4)
    def _():
        put(2, top_ref)

    @pl.when(step >= 4)
    def _():
        put(2, bottom_ref)


def split_z(at, own, following, top, bottom, previous):
    block = pl.BlockSpec((128, 896), lambda i, at: (i, 0))
    return call(
        split_z_kernel,
        at,
        (own, following, top, bottom, previous),
        (jax.ShapeDtypeStruct((D, 2048), bf16), jax.ShapeDtypeStruct((D, 1536), bf16)),
        (8,),
        [
            block,
            block,
            pl.BlockSpec((128, 896), lambda i, at: (jnp.minimum(i, 3), 0)),
            pl.BlockSpec((128, 896), lambda i, at: (jnp.maximum(i - 4, 0), 0)),
            block,
        ],
        (pl.BlockSpec((128, 2048), lambda i, at: (i, 0)), pl.BlockSpec((128, 1536), lambda i, at: (i, 0))),
    )


def split_x_kernel(at_ref, in_ref, down_ref, proj_ref):
    for e in range(2):
        down_ref[e * 256 : e * 256 + 256] = in_ref[e, 0:256]
        proj_ref[e * 64 : e * 64 + 64] = in_ref[e, 256:320]


def split_x(at, gathered):
    return call(
        split_x_kernel,
        at,
        (gathered,),
        (jax.ShapeDtypeStruct((2048, D), bf16), jax.ShapeDtypeStruct((512, D), bf16)),
        (4,),
        [pl.BlockSpec((2, gathered.shape[1], D), lambda i, at: (lax.rem(i + at[0], 4), 0, 0))],
        (pl.BlockSpec((512, D), lambda i, at: (i, 0)), pl.BlockSpec((128, D), lambda i, at: (i, 0))),
    )


def grad_z_kernel(at_ref, a2_ref, dub_ref, a1_ref, dqkv_ref, out_ref):
    out_ref[:, :512] = dot_tn(a2_ref[...], dub_ref[...]).astype(bf16)
    out_ref[:, 512:] = dot_tn(a1_ref[...], dqkv_ref[...]).astype(bf16)


def grad_z(at, a2, dub, a1, dqkv, block):
    rows = pl.BlockSpec((256, 256), lambda i, at: (0, i))
    return call(
        grad_z_kernel,
        at,
        (a2, dub, a1, dqkv),
        jax.ShapeDtypeStruct((D, 896), bf16),
        (4,),
        [
            rows,
            pl.BlockSpec((256, 512), lambda i, at: (0, block)),
            rows,
            pl.BlockSpec((256, 384), lambda i, at: (0, block)),
        ],
        pl.BlockSpec((256, 896), lambda i, at: (i, 0)),
        flops=2 * 256 * D * 896,
    )


def grad_x_kernel(at_ref, m_ref, dy_ref, ctx_ref, dr_ref, out_ref):
    for e in range(2):
        out_ref[e, 0:256] = dot_tn(m_ref[:, e * 256 : e * 256 + 256], dy_ref[...]).astype(bf16)
        out_ref[e, 256:320] = dot_tn(ctx_ref[:, e * 64 : e * 64 + 64], dr_ref[...]).astype(bf16)


def grad_x(at, m, dy, ctx, dr):
    whole = pl.BlockSpec((256, D), lambda i, at: (0, 0))
    return call(
        grad_x_kernel,
        at,
        (m, dy, ctx, dr),
        jax.ShapeDtypeStruct((8, 320, D), bf16),
        (4,),
        [
            pl.BlockSpec((256, 512), lambda i, at: (0, i)),
            whole,
            pl.BlockSpec((256, 128), lambda i, at: (0, i)),
            whole,
        ],
        pl.BlockSpec((2, 320, D), lambda i, at: (lax.rem(i + at[0], 4), 0, 0)),
        flops=2 * 256 * D * 2560,
    )


def assemble_kernel(at_ref, first_ref, second_ref, up_ref, qkv_ref):
    def put(ref):
        for j in range(4):
            for e in range(2):
                for core in range(2):
                    at = j * 1024 + e * 512 + core * 256
                    up_ref[0, :, at : at + 256] = ref[0, j, core, :, e * 256 : e * 256 + 256].astype(f32)
                for t in range(3):
                    lane = 512 + t * 128 + e * 64
                    both = [ref[0, j, core, :, lane : lane + 64].astype(f32) for core in range(2)]
                    at = t * 1024 + j * 256 + e * 128
                    qkv_ref[0, :, at : at + 128] = jnp.concatenate(both, axis=1)

    @pl.when(pl.program_id(0) == 0)
    def _():
        put(first_ref)

    @pl.when(pl.program_id(0) == 1)
    def _():
        put(second_ref)


def assemble(at, first, second):
    block = (1, 4, 2, 64, 896)
    return call(
        assemble_kernel,
        at,
        (first, second),
        (jax.ShapeDtypeStruct((LAYERS, 128, 4096), f32), jax.ShapeDtypeStruct((LAYERS, 128, 3072), f32)),
        (LAYERS, 2),
        [
            pl.BlockSpec(block, lambda l, h, at: (h, 0, 0, 0, 0)),
            pl.BlockSpec(block, lambda l, h, at: (h, 0, 0, 0, 0)),
        ],
        (
            pl.BlockSpec((1, 64, 4096), lambda l, h, at: (l, h, 0)),
            pl.BlockSpec((1, 64, 3072), lambda l, h, at: (l, h, 0)),
        ),
    )


def head_scores(q, k, seen, distance, slope):
    s = lax.dot_general(q, k, (((1,), (1,)), ((), ())), preferred_element_type=f32) * HEAD_DIM ** (-0.5)
    s = s - slope * distance
    return jnp.where(seen, s, f32(-1000000000.0))


def visibility(row_start, col_start):
    row = lax.broadcasted_iota(jnp.int32, (RUN, RUN), 0)
    col = lax.broadcasted_iota(jnp.int32, (RUN, RUN), 1)
    seen = (row_start == col_start) & (col <= row)
    return seen, (row - col).astype(f32)


def attend_kernel(slope_ref, rows_ref, cols_ref, qkv_ref, ctx_ref):
    first = pl.program_id(1) * 4
    seen, distance = visibility(rows_ref[0], cols_ref[0])
    done = []
    for i in range(4):
        at = (i // 2) * 384 + (i % 2) * 64
        q = qkv_ref[:, at : at + 64]
        k = qkv_ref[:, at + 128 : at + 192]
        v = qkv_ref[:, at + 256 : at + 320]
        s = head_scores(q, k, seen, distance, slope_ref[first + i])
        top = jnp.max(s, axis=-1, keepdims=True)
        lse = top + jnp.log(jnp.sum(jnp.exp(s - top), axis=-1, keepdims=True))
        p = jnp.exp(s - lse).astype(bf16)
        done.append(jnp.dot(p, v, preferred_element_type=f32))
    ctx_ref[...] = jnp.concatenate(done, axis=1).astype(bf16)


def attend_back_kernel(slope_ref, rows_ref, cols_ref, qkv_ref, ctx_ref, dctx_ref, dqkv_ref, dq_ref, dv_ref):
    first = pl.program_id(1) * 4
    seen, distance = visibility(rows_ref[0], cols_ref[0])
    dqs, dks, dvs = [], [], []
    tn = (((0,), (0,)), ((), ()))
    nt = (((1,), (1,)), ((), ()))
    for i in range(4):
        lanes = slice(i * 64, i * 64 + 64)
        at = (i // 2) * 384 + (i % 2) * 64
        q = qkv_ref[:, at : at + 64]
        k = qkv_ref[:, at + 128 : at + 192]
        v = qkv_ref[:, at + 256 : at + 320]
        s = head_scores(q, k, seen, distance, slope_ref[first + i])
        top = jnp.max(s, axis=-1, keepdims=True)
        lse = top + jnp.log(jnp.sum(jnp.exp(s - top), axis=-1, keepdims=True))
        p = jnp.exp(s - lse)
        dctx = dctx_ref[:, lanes]
        dv = lax.dot_general(p.astype(bf16), dctx, tn, preferred_element_type=f32)
        dp = lax.dot_general(dctx, v, nt, preferred_element_type=f32)
        delta = jnp.sum(dctx.astype(f32) * ctx_ref[:, lanes].astype(f32), axis=-1, keepdims=True)
        ds = (p * (dp - delta)).astype(bf16)
        dqs.append(jnp.dot(ds, k, preferred_element_type=f32) * HEAD_DIM ** (-0.5))
        dks.append(lax.dot_general(ds, q, tn, preferred_element_type=f32) * HEAD_DIM ** (-0.5))
        dvs.append(dv)
    for pair in range(2):
        at = pair * 384
        dq = jnp.concatenate(dqs[2 * pair : 2 * pair + 2], axis=1)
        dk = jnp.concatenate(dks[2 * pair : 2 * pair + 2], axis=1)
        dv = jnp.concatenate(dvs[2 * pair : 2 * pair + 2], axis=1)
        dqkv_ref[:, at : at + 128] = dq.astype(bf16)
        dqkv_ref[:, at + 128 : at + 256] = dk.astype(bf16)
        dqkv_ref[:, at + 256 : at + 384] = dv.astype(bf16)
        dq_ref[0, 0, :, pair * 128 : pair * 128 + 128] = jnp.sum(dq, axis=0, keepdims=True)
        dv_ref[0, 0, :, pair * 128 : pair * 128 + 128] = jnp.sum(dv, axis=0, keepdims=True)


def attend(qkv, rows, cols, slopes):
    return pl.pallas_call(
        attend_kernel,
        out_shape=jax.ShapeDtypeStruct((2 * RUN, 512), bf16),
        grid=(2, 2),
        in_specs=[
            pl.BlockSpec(memory_space=pltpu.SMEM),
            pl.BlockSpec((1, RUN, 1), lambda r, p: (r, 0, 0)),
            pl.BlockSpec((1, 1, RUN), lambda r, p: (r, 0, 0)),
            pl.BlockSpec((RUN, 768), lambda r, p: (r, p)),
        ],
        out_specs=pl.BlockSpec((RUN, 256), lambda r, p: (r, p)),
        compiler_params=pltpu.CompilerParams(vmem_limit_bytes=8 * 1024 * 1024),
        cost_estimate=pl.CostEstimate(flops=4 * 16 * RUN * RUN * 64, bytes_accessed=1 << 20, transcendentals=32 * RUN * RUN),
    )(slopes, rows, cols, qkv)


def attend_back(qkv, ctx, dctx, rows, cols, slopes):
    row_block = pl.BlockSpec((RUN, 256), lambda r, p: (r, p))
    sums = pl.BlockSpec((1, 1, 1, 256), lambda r, p: (r, p, 0, 0))
    return pl.pallas_call(
        attend_back_kernel,
        out_shape=(
            jax.ShapeDtypeStruct((2 * RUN, 1536), bf16),
            jax.ShapeDtypeStruct((2, 2, 1, 256), f32),
            jax.ShapeDtypeStruct((2, 2, 1, 256), f32),
        ),
        grid=(2, 2),
        in_specs=[
            pl.BlockSpec(memory_space=pltpu.SMEM),
            pl.BlockSpec((1, RUN, 1), lambda r, p: (r, 0, 0)),
            pl.BlockSpec((1, 1, RUN), lambda r, p: (r, 0, 0)),
            pl.BlockSpec((RUN, 768), lambda r, p: (r, p)),
            row_block,
            row_block,
        ],
        out_specs=(pl.BlockSpec((RUN, 768), lambda r, p: (r, p)), sums, sums),
        compiler_params=pltpu.CompilerParams(vmem_limit_bytes=8 * 1024 * 1024),
        cost_estimate=pl.CostEstimate(flops=10 * 16 * RUN * RUN * 64, bytes_accessed=1 << 21, transcendentals=32 * RUN * RUN),
    )(slopes, rows, cols, qkv, ctx, dctx)


def layer_norm(stream, gains, shifts):
    average = jnp.mean(stream, axis=-1, keepdims=True)
    centered = stream - average
    variance = jnp.mean(centered * centered, axis=-1, keepdims=True)
    inv_std = lax.rsqrt(variance + epsilon)
    normed = centered * inv_std
    return (normed * gains + shifts, normed, inv_std)


def norm_back(grad_norm, normed, inv_std, gains):
    scaled = grad_norm * gains
    inner = (
        scaled
        - jnp.mean(scaled, axis=-1, keepdims=True)
        - normed * jnp.mean(scaled * normed, axis=-1, keepdims=True)
    )
    return (inv_std * inner, jnp.sum(grad_norm * normed, axis=0), jnp.sum(grad_norm, axis=0))


def gelu_tanh(values):
    inner = jnp.tanh(gelu_coef * (values + 0.044715 * values * values * values))
    return 0.5 * values * (1.0 + inner)


def gelu_slope(values):
    inner = jnp.tanh(gelu_coef * (values + 0.044715 * values * values * values))
    return 0.5 * (1.0 + inner) + 0.5 * values * (1.0 - inner * inner) * gelu_coef * (
        1.0 + 3.0 * 0.044715 * values * values
    )


def dot(a, b):
    return jnp.dot(a, b, preferred_element_type=f32)


def dot_nt(a, b):
    return lax.dot_general(a, b, (((1,), (1,)), ((), ())), preferred_element_type=f32)


def dot_tn(a, b):
    return lax.dot_general(a, b, (((0,), (0,)), ((), ())), preferred_element_type=f32)


def local(hidden_in, doc_start, grad_out, w_qkv, w_proj, w_up, w_down, norm_gain, d_bias, up_bias):
    z, core = lax.axis_index("z"), lax.axis_index("core")
    at = jnp.stack([z, core]).astype(jnp.int32)
    index = jnp.arange(8, dtype=jnp.int32)

    def both(own):
        return jnp.concatenate([own, swap(own)], axis=0)

    def halves_summed(product, a, w):
        theirs = swap(product(a[RUN:], w))
        return product(a[:RUN], w) + theirs

    small = jnp.concatenate(
        [
            jnp.transpose(jnp.concatenate([norm_gain, d_bias], axis=2), (0, 2, 1)).reshape(16, 128),
            up_bias.reshape(8, 128),
        ]
    )

    mine_z, mine_x = select_weights(at, w_qkv, w_proj, w_up, w_down)
    weights = []
    piece_x = jnp.concatenate([mine_x[0], small.reshape(3, D), jnp.zeros((5, D), bf16)])
    block_z = to_all(mine_z[0], SHARD, 8).reshape(D, 896)
    all_x = to_all(after(piece_x, block_z), SHARD, 8)
    all_small = all_x[:, 320:323]
    next_z = lax.all_gather(after(mine_z[1], block_z), SHARD, axis=0).reshape(D, 896)
    for layer in range(LAYERS):
        own, following, (top, bottom), previous = ring_gather(block_z, z_up, z_down)
        wup, wqkv = split_z(at, own, following, top, bottom, previous)
        wdown, wproj = split_x(at, all_x)
        weights.append((wqkv, wproj, wup, wdown))
        if layer == 0:
            block_z = after(next_z, top)
            all_x = lax.all_gather(after(mine_x[1], previous, following, all_x[0]), SHARD, axis=0)

    small = all_small.reshape(4, 2, 24, 128).astype(f32)
    wide = jnp.transpose(small[:, :, :16], (2, 0, 1, 3)).reshape(LAYERS, 8, D)
    hidden_bias = small[:, :, 16:].reshape(4, 2, LAYERS, 2, 256)

    def core_heads(vector):
        picked = lax.dynamic_index_in_dim(vector.reshape(4, 2, 2, 64), core, axis=2, keepdims=False)
        return rolled(picked.reshape(4, 128), z)

    starts = both(doc_start.reshape(1, RUN))
    rows, cols = starts.reshape(2, RUN, 1), starts.reshape(2, 1, RUN)
    head = 4 * ((z + index // 2) % 4) + 2 * (index % 2) + core
    slopes = 2.0 ** (-8.0 * (head.astype(f32) + 1.0) / HEADS)

    kept = []
    current = hidden_in
    for layer in range(LAYERS):
        wqkv, wproj, wup, wdown = weights[layer]
        gain_one, gain_two, shift_one, shift_two, bq, bv, bproj, bdown = (wide[layer, i] for i in range(8))
        bq, bv = core_heads(bq), core_heads(bv)
        bqkv = jnp.stack([bq, jnp.zeros_like(bq), bv], axis=1).reshape(1536)
        ubias = lax.dynamic_index_in_dim(hidden_bias[:, :, layer], core, axis=2, keepdims=False)
        ubias = rolled(ubias.reshape(4, 512), z).reshape(2048)
        first_f, normed_one, inv_one = layer_norm(current, gain_one, shift_one)
        first_in = both(first_f.astype(bf16))
        qkv = (dot(first_in, wqkv) + bqkv).astype(bf16)
        ctx = attend(qkv, rows, cols, slopes)
        middle = current + halves_summed(dot, ctx, wproj) + bproj
        second_f, normed_two, inv_two = layer_norm(middle, gain_two, shift_two)
        second_in = both(second_f.astype(bf16))
        upper = dot(second_in, wup) + ubias
        activ = gelu_tanh(upper).astype(bf16)
        current = middle + halves_summed(dot, activ, wdown) + bdown
        kept.append((first_in, normed_one, inv_one, qkv, ctx, second_in, normed_two, inv_two, upper, activ, gain_one, gain_two))
    hidden_out = current

    def summed(blocks):
        return jnp.sum(blocks.astype(f32), axis=0).astype(bf16)

    def ring_z(a2, dub, a1, dqkv):
        parts = [grad_z(at, a2, dub, a1, dqkv, i) for i in (2, 1, 3, 0)]
        parts = [parts[i] for i in (3, 1, 0, 2)]
        (top, bottom), sent, near, got = ring_scatter(parts, z_up, z_down)
        part = jnp.concatenate([top.astype(bf16).reshape(8, 64, 896), bottom.astype(bf16).reshape(8, 64, 896)])
        return part, (sent, near, got)

    def finish_x(blocks, later):
        part = summed(after(blocks, later))
        part = jnp.concatenate([part[:256].reshape(8, 32, D), part[256:320].reshape(8, 8, D)], axis=1)
        return summed(exchange(part, ("ylo", "z")))

    def share(part_z, part_x, *earlier):
        part = jnp.concatenate([part_z.reshape(56, D), part_x])
        parts = lax.all_gather(after(part, *earlier) if earlier else part, REP, axis=0)
        by_z = parts[:, :56].reshape(2, 4, 2, 64, 896)
        by_x = jnp.transpose(parts[:, 56:].reshape(8, 2, 40, D), (1, 0, 2, 3))
        return by_z, (by_x[:, :, :32].reshape(512, D), by_x[:, :, 32:].reshape(128, D))

    grads_x, grads_z = [None] * LAYERS, [None] * LAYERS
    thin_grads, head_grads, unit_grads = [None] * LAYERS, [None] * LAYERS, [None] * LAYERS
    running, ring_state = grad_out, None
    for layer in reversed(range(LAYERS)):
        wqkv, wproj, wup, wdown = weights[layer]
        first_in, normed_one, inv_one, qkv, ctx, second_in, normed_two, inv_two, upper, activ, gain_one, gain_two = kept[layer]
        if ring_state is not None:
            running = after(running, *ring_state[0])
        g_bdown = jnp.sum(running, axis=0)
        grad_yb = both(running.astype(bf16))
        grad_upper = dot_nt(grad_yb, wdown) * gelu_slope(upper)
        g_ubias = jnp.sum(grad_upper, axis=0)
        grad_ub = grad_upper.astype(bf16)
        grad_two = halves_summed(dot_nt, grad_ub, wup)
        back_two, g_gain_two, g_shift_two = norm_back(grad_two, normed_two, inv_two, gain_two)
        grad_mid = running + back_two
        g_bproj = jnp.sum(grad_mid, axis=0)
        grad_midb = grad_mid.astype(bf16)
        if ring_state is not None:
            grad_midb = after(grad_midb, *ring_state[1])
            later_x = waiting_x
        grad_midb = both(grad_midb)
        grad_ctx = dot_nt(grad_midb, wproj).astype(bf16)
        waiting_x = exchange(grad_x(at, activ, grad_yb, ctx, grad_midb), SHARD)
        grad_qkv, g_bq, g_bv = attend_back(qkv, ctx, grad_ctx, rows, cols, slopes)
        if ring_state is not None:
            grad_qkv = after(grad_qkv, *ring_state[2])
            later_x = finish_x(later_x, grad_ctx)
            later_z = lax.psum_scatter(after(part_z, grad_ctx), ("x", "yhi", "ylo"), scatter_dimension=0, tiled=True)[0]
        part_z, ring_state = ring_z(second_in, grad_ub, first_in, grad_qkv)
        if layer == 0:
            grad_qkv = after(grad_qkv, *ring_state[0])
        grad_one = halves_summed(dot_nt, grad_qkv, wqkv)
        if layer == 0:
            grad_one = after(grad_one, *ring_state[1])
            grads_z[1], grads_x[1] = share(later_z, later_x, *ring_state[1])
        back_one, g_gain_one, g_shift_one = norm_back(grad_one, normed_one, inv_one, gain_one)
        running = grad_mid + back_one

        thin_grads[layer] = [g_gain_one, g_gain_two, g_shift_one, g_shift_two, g_bproj, g_bdown]
        head_grads[layer] = [jnp.sum(g, axis=0).reshape(4, 128) for g in (g_bq, g_bv)]
        unit_grads[layer] = g_ubias.reshape(4, 512)

    part_x = finish_x(waiting_x, running)
    part_z = summed(exchange(after(part_z, part_x), ("x", "yhi", "ylo")))
    grads_z[0], grads_x[0] = share(part_z, part_x)

    thin = jnp.stack(thin_grads[0] + thin_grads[1]).reshape(LAYERS, 6, 4, 2, 128)
    heads = jnp.stack(head_grads[0] + head_grads[1], axis=1)
    heads = rolled(heads, (4 - z) % 4).reshape(4, LAYERS, 2, 2, 1, 64)
    mine = lax.broadcasted_iota(jnp.int32, (4, LAYERS, 2, 2, 2, 64), 4) == core
    heads = jnp.where(mine, heads, 0.0).reshape(4, LAYERS, 2, 2, 128)
    units = rolled(jnp.stack(unit_grads, axis=1), (4 - z) % 4).reshape(4, LAYERS, 2, 1, 256)
    mine = lax.broadcasted_iota(jnp.int32, (4, LAYERS, 2, 2, 256), 3) == core
    units = jnp.where(mine, units, 0.0).reshape(4, LAYERS, 2, 4, 128)
    thin = jnp.transpose(thin, (2, 3, 0, 1, 4))
    heads = jnp.transpose(heads, (0, 3, 1, 2, 4))
    units = jnp.transpose(units, (0, 2, 1, 3, 4))
    part = jnp.concatenate([thin[:, :, :, :4], heads, thin[:, :, :, 4:], units], axis=3)
    part = jnp.sum(exchange(part.reshape(8, 24, 128), SHARD), axis=0)
    part = jnp.sum(to_all(part, REP, 16), axis=0).reshape(LAYERS, 12, 128)
    g_wide = jnp.transpose(part[:, :8], (0, 2, 1))
    g_up, g_qkv = assemble(at, grads_z[0], grads_z[1])
    g_down, g_proj = (jnp.stack([grads_x[layer][i] for layer in range(LAYERS)]).astype(f32) for i in range(2))
    return (
        hidden_out,
        running,
        g_qkv,
        g_proj,
        g_up,
        g_down,
        g_wide[:, :, :2],
        g_wide[:, :, 2:],
        part[:, 8:].reshape(LAYERS, 512),
    )


def solution(mesh):
    fine = Mesh(mesh.devices.reshape(2, 4, 2, 4, 2), AXES)
    tokens = P(AXES)
    wide_tokens = P(AXES, None)
    params = P(None, ("x", "yhi"), None)
    return jax.shard_map(
        local,
        mesh=fine,
        in_specs=(wide_tokens, tokens, wide_tokens, params, params, params, params, params, params, P(None, ("x", "yhi"))),
        out_specs=(wide_tokens, wide_tokens, params, params, params, params, params, params, P(None, ("x", "yhi"))),
        check_vma=False,
    )
```

```python
import jax
import jax.numpy as jnp
from jax import lax
from jax.experimental import pallas as pl
from jax.experimental.pallas import tpu as pltpu
from jax.sharding import Mesh
from jax.sharding import PartitionSpec as P

HEADS = 16
HEAD_DIM = 64
LAYERS = 2
D = 1024
RUN = 128

epsilon = 1e-05
gelu_coef = 0.7978845608
f32 = jnp.float32
bf16 = jnp.bfloat16

AXES = ("ylo", "z", "core", "x", "yhi")


def ring(step):
    return [(i, (i + step) % 4) for i in range(4)]


def z_up(a):
    return lax.ppermute(a, "z", ring(1))


def z_down(a):
    return lax.ppermute(a, "z", ring(3))


def x_up(a):
    return lax.ppermute(a, "x", ring(1))


def x_down(a):
    return lax.ppermute(a, "x", ring(3))


def y_pair(a):
    return lax.ppermute(a, ("ylo", "yhi"), [(0, 3), (3, 0), (1, 2), (2, 1)])


def swap(a):
    return lax.ppermute(a, "core", [(0, 1), (1, 0)])


SHARD = ("x", "yhi")
REP = ("ylo", "z", "core")


def exchange(blocks, axes):
    return lax.all_to_all(blocks, axes, 0, 0, tiled=True)


def to_all(a, axes, count):
    return exchange(jnp.broadcast_to(a[None], (count, *a.shape)), axes)


def ring_gather(a, up, down):
    half = a.shape[0] // 2
    previous = up(a)
    following = down(a)
    top = up(previous[:half])
    bottom = down(following[half:])
    return a, following, (top, bottom), previous


def ring_scatter(parts, up, down):
    own, following, far, previous = parts
    half = own.shape[0] // 2
    from_previous = up(far[:half])
    from_following = down(far[half:])
    go_up = jnp.concatenate(
        [(following[:half].astype(f32) + from_previous.astype(f32)).astype(bf16), following[half:]]
    )
    go_down = jnp.concatenate(
        [previous[:half], (previous[half:].astype(f32) + from_following.astype(f32)).astype(bf16)]
    )
    got_up = up(go_up)
    got_down = down(go_down)
    total = own.astype(f32) + got_up.astype(f32) + got_down.astype(f32)
    return total, (following, previous), (from_previous, from_following), (got_up, got_down)


def rolled(stack, start):
    return lax.dynamic_slice_in_dim(jnp.concatenate([stack, stack[:3]]), start, 4, axis=0)


def after(a, *earlier):
    there = sum(jnp.abs(e[0, 0].astype(f32)) * 2.0**-40 for e in earlier) < 1e30
    return jnp.where(there, a, jnp.zeros_like(a))


def select_kernel(at_ref, up_a, up_b, q_ref, k_ref, v_ref, down_ref, proj_ref, by_z_ref, by_x_ref):
    first = at_ref[1] == 0
    by_z_ref[0, :, 0:256] = up_a[0]
    by_z_ref[0, :, 256:512] = up_b[0]
    for t, ref in enumerate((q_ref, k_ref, v_ref)):
        low = jnp.where(first, ref[0, :, 0:64].astype(f32), ref[0, :, 64:128].astype(f32))
        high = jnp.where(first, ref[0, :, 128:192].astype(f32), ref[0, :, 192:256].astype(f32))
        by_z_ref[0, :, 512 + t * 128 : 640 + t * 128] = jnp.concatenate([low, high], axis=1).astype(bf16)
    by_x_ref[0, 0:256] = down_ref[0]
    by_x_ref[0, 256:320] = proj_ref[0]


def select_weights(at, w_qkv, w_proj, w_up, w_down):
    def lanes(block):
        return pl.BlockSpec((1, 128, 256), lambda l, at: (l, 0, block(at)))

    return pl.pallas_call(
        select_kernel,
        out_shape=(
            jax.ShapeDtypeStruct((LAYERS, 128, 896), bf16),
            jax.ShapeDtypeStruct((LAYERS, 320, D), bf16),
        ),
        grid_spec=pltpu.PrefetchScalarGridSpec(
            num_scalar_prefetch=1,
            grid=(LAYERS,),
            in_specs=[
                lanes(lambda at: 4 * at[0] + at[1]),
                lanes(lambda at: 4 * at[0] + 2 + at[1]),
                lanes(lambda at: at[0]),
                lanes(lambda at: 4 + at[0]),
                lanes(lambda at: 8 + at[0]),
                pl.BlockSpec((1, 256, D), lambda l, at: (l, at[1], 0)),
                pl.BlockSpec((1, 64, D), lambda l, at: (l, at[1], 0)),
            ],
            out_specs=(
                pl.BlockSpec((1, 128, 896), lambda l, at: (l, 0, 0)),
                pl.BlockSpec((1, 320, D), lambda l, at: (l, 0, 0)),
            ),
        ),
        compiler_params=pltpu.CompilerParams(vmem_limit_bytes=8 * 1024 * 1024),
        cost_estimate=pl.CostEstimate(flops=0, bytes_accessed=4 * 1024 * 1024, transcendentals=0),
    )(at, w_up, w_up, w_qkv, w_qkv, w_qkv, w_down, w_proj)


def call(kernel, scalars, operands, out_shape, grid, in_specs, out_specs, flops=0):
    moved = sum(a.size * a.dtype.itemsize for a in operands) + sum(o.size * o.dtype.itemsize for o in jax.tree.leaves(out_shape))
    return pl.pallas_call(
        kernel,
        out_shape=out_shape,
        grid_spec=pltpu.PrefetchScalarGridSpec(
            num_scalar_prefetch=1, grid=grid, in_specs=in_specs, out_specs=out_specs
        ),
        compiler_params=pltpu.CompilerParams(vmem_limit_bytes=20 * 1024 * 1024),
        cost_estimate=pl.CostEstimate(flops=flops, bytes_accessed=moved, transcendentals=0),
    )(scalars, *operands)


def split_z_kernel(at_ref, own_ref, next_ref, top_ref, bottom_ref, last_ref, up_ref, qkv_ref):
    step = pl.program_id(0)

    def put(position, block):
        up_ref[:, position * 512 : position * 512 + 512] = block[:, :512]
        qkv_ref[:, position * 384 : position * 384 + 384] = block[:, 512:]

    put(0, own_ref)
    put(1, next_ref)
    put(3, last_ref)

    @pl.when(step < 4)
    def _():
        put(2, top_ref)

    @pl.when(step >= 4)
    def _():
        put(2, bottom_ref)


def split_z(at, own, following, top, bottom, previous):
    block = pl.BlockSpec((128, 896), lambda i, at: (i, 0))
    return call(
        split_z_kernel,
        at,
        (own, following, top, bottom, previous),
        (jax.ShapeDtypeStruct((D, 2048), bf16), jax.ShapeDtypeStruct((D, 1536), bf16)),
        (8,),
        [
            block,
            block,
            pl.BlockSpec((128, 896), lambda i, at: (jnp.minimum(i, 3), 0)),
            pl.BlockSpec((128, 896), lambda i, at: (jnp.maximum(i - 4, 0), 0)),
            block,
        ],
        (pl.BlockSpec((128, 2048), lambda i, at: (i, 0)), pl.BlockSpec((128, 1536), lambda i, at: (i, 0))),
    )


def split_x_kernel(at_ref, in_ref, down_ref, proj_ref):
    for e in range(2):
        down_ref[e * 256 : e * 256 + 256] = in_ref[e, 0:256]
        proj_ref[e * 64 : e * 64 + 64] = in_ref[e, 256:320]


def split_x(at, gathered):
    return call(
        split_x_kernel,
        at,
        (gathered,),
        (jax.ShapeDtypeStruct((2048, D), bf16), jax.ShapeDtypeStruct((512, D), bf16)),
        (4,),
        [pl.BlockSpec((2, gathered.shape[1], D), lambda i, at: (lax.rem(i + at[0], 4), 0, 0))],
        (pl.BlockSpec((512, D), lambda i, at: (i, 0)), pl.BlockSpec((128, D), lambda i, at: (i, 0))),
    )


def grad_z_kernel(at_ref, a2_ref, dub_ref, a1_ref, dqkv_ref, out_ref):
    out_ref[:, :512] = dot_tn(a2_ref[...], dub_ref[...]).astype(bf16)
    out_ref[:, 512:] = dot_tn(a1_ref[...], dqkv_ref[...]).astype(bf16)


def grad_z(at, a2, dub, a1, dqkv, block):
    rows = pl.BlockSpec((256, 256), lambda i, at: (0, i))
    return call(
        grad_z_kernel,
        at,
        (a2, dub, a1, dqkv),
        jax.ShapeDtypeStruct((D, 896), bf16),
        (4,),
        [
            rows,
            pl.BlockSpec((256, 512), lambda i, at: (0, block)),
            rows,
            pl.BlockSpec((256, 384), lambda i, at: (0, block)),
        ],
        pl.BlockSpec((256, 896), lambda i, at: (i, 0)),
        flops=2 * 256 * D * 896,
    )


def grad_x_kernel(at_ref, m_ref, dy_ref, ctx_ref, dr_ref, out_ref):
    for e in range(2):
        out_ref[e, 0:256] = dot_tn(m_ref[:, e * 256 : e * 256 + 256], dy_ref[...]).astype(bf16)
        out_ref[e, 256:320] = dot_tn(ctx_ref[:, e * 64 : e * 64 + 64], dr_ref[...]).astype(bf16)


def grad_x(at, m, dy, ctx, dr):
    whole = pl.BlockSpec((256, D), lambda i, at: (0, 0))
    return call(
        grad_x_kernel,
        at,
        (m, dy, ctx, dr),
        jax.ShapeDtypeStruct((8, 320, D), bf16),
        (4,),
        [
            pl.BlockSpec((256, 512), lambda i, at: (0, i)),
            whole,
            pl.BlockSpec((256, 128), lambda i, at: (0, i)),
            whole,
        ],
        pl.BlockSpec((2, 320, D), lambda i, at: (lax.rem(i + at[0], 4), 0, 0)),
        flops=2 * 256 * D * 2560,
    )


def assemble_kernel(at_ref, first_ref, second_ref, up_ref, qkv_ref):
    def put(ref):
        for j in range(4):
            for e in range(2):
                for core in range(2):
                    at = j * 1024 + e * 512 + core * 256
                    up_ref[0, :, at : at + 256] = ref[0, j, core, :, e * 256 : e * 256 + 256].astype(f32)
                for t in range(3):
                    lane = 512 + t * 128 + e * 64
                    both = [ref[0, j, core, :, lane : lane + 64].astype(f32) for core in range(2)]
                    at = t * 1024 + j * 256 + e * 128
                    qkv_ref[0, :, at : at + 128] = jnp.concatenate(both, axis=1)

    @pl.when(pl.program_id(0) == 0)
    def _():
        put(first_ref)

    @pl.when(pl.program_id(0) == 1)
    def _():
        put(second_ref)


def assemble(at, first, second):
    block = (1, 4, 2, 64, 896)
    return call(
        assemble_kernel,
        at,
        (first, second),
        (jax.ShapeDtypeStruct((LAYERS, 128, 4096), f32), jax.ShapeDtypeStruct((LAYERS, 128, 3072), f32)),
        (LAYERS, 2),
        [
            pl.BlockSpec(block, lambda l, h, at: (h, 0, 0, 0, 0)),
            pl.BlockSpec(block, lambda l, h, at: (h, 0, 0, 0, 0)),
        ],
        (
            pl.BlockSpec((1, 64, 4096), lambda l, h, at: (l, h, 0)),
            pl.BlockSpec((1, 64, 3072), lambda l, h, at: (l, h, 0)),
        ),
    )


def head_scores(q, k, seen, distance, slope):
    s = lax.dot_general(q, k, (((1,), (1,)), ((), ())), preferred_element_type=f32) * HEAD_DIM ** (-0.5)
    s = s - slope * distance
    return jnp.where(seen, s, f32(-1000000000.0))


def visibility(row_start, col_start):
    row = lax.broadcasted_iota(jnp.int32, (RUN, RUN), 0)
    col = lax.broadcasted_iota(jnp.int32, (RUN, RUN), 1)
    seen = (row_start == col_start) & (col <= row)
    return seen, (row - col).astype(f32)


def attend_kernel(slope_ref, rows_ref, cols_ref, qkv_ref, ctx_ref):
    first = pl.program_id(1) * 4
    seen, distance = visibility(rows_ref[0], cols_ref[0])
    done = []
    for i in range(4):
        at = (i // 2) * 384 + (i % 2) * 64
        q = qkv_ref[:, at : at + 64]
        k = qkv_ref[:, at + 128 : at + 192]
        v = qkv_ref[:, at + 256 : at + 320]
        s = head_scores(q, k, seen, distance, slope_ref[first + i])
        top = jnp.max(s, axis=-1, keepdims=True)
        lse = top + jnp.log(jnp.sum(jnp.exp(s - top), axis=-1, keepdims=True))
        p = jnp.exp(s - lse).astype(bf16)
        done.append(jnp.dot(p, v, preferred_element_type=f32))
    ctx_ref[...] = jnp.concatenate(done, axis=1).astype(bf16)


def attend_back_kernel(slope_ref, rows_ref, cols_ref, qkv_ref, ctx_ref, dctx_ref, dqkv_ref, dq_ref, dv_ref):
    first = pl.program_id(1) * 4
    seen, distance = visibility(rows_ref[0], cols_ref[0])
    dqs, dks, dvs = [], [], []
    tn = (((0,), (0,)), ((), ()))
    nt = (((1,), (1,)), ((), ()))
    for i in range(4):
        lanes = slice(i * 64, i * 64 + 64)
        at = (i // 2) * 384 + (i % 2) * 64
        q = qkv_ref[:, at : at + 64]
        k = qkv_ref[:, at + 128 : at + 192]
        v = qkv_ref[:, at + 256 : at + 320]
        s = head_scores(q, k, seen, distance, slope_ref[first + i])
        top = jnp.max(s, axis=-1, keepdims=True)
        lse = top + jnp.log(jnp.sum(jnp.exp(s - top), axis=-1, keepdims=True))
        p = jnp.exp(s - lse)
        dctx = dctx_ref[:, lanes]
        dv = lax.dot_general(p.astype(bf16), dctx, tn, preferred_element_type=f32)
        dp = lax.dot_general(dctx, v, nt, preferred_element_type=f32)
        delta = jnp.sum(dctx.astype(f32) * ctx_ref[:, lanes].astype(f32), axis=-1, keepdims=True)
        ds = (p * (dp - delta)).astype(bf16)
        dqs.append(jnp.dot(ds, k, preferred_element_type=f32) * HEAD_DIM ** (-0.5))
        dks.append(lax.dot_general(ds, q, tn, preferred_element_type=f32) * HEAD_DIM ** (-0.5))
        dvs.append(dv)
    for pair in range(2):
        at = pair * 384
        dq = jnp.concatenate(dqs[2 * pair : 2 * pair + 2], axis=1)
        dk = jnp.concatenate(dks[2 * pair : 2 * pair + 2], axis=1)
        dv = jnp.concatenate(dvs[2 * pair : 2 * pair + 2], axis=1)
        dqkv_ref[:, at : at + 128] = dq.astype(bf16)
        dqkv_ref[:, at + 128 : at + 256] = dk.astype(bf16)
        dqkv_ref[:, at + 256 : at + 384] = dv.astype(bf16)
        dq_ref[0, 0, :, pair * 128 : pair * 128 + 128] = jnp.sum(dq, axis=0, keepdims=True)
        dv_ref[0, 0, :, pair * 128 : pair * 128 + 128] = jnp.sum(dv, axis=0, keepdims=True)


def attend(qkv, rows, cols, slopes):
    return pl.pallas_call(
        attend_kernel,
        out_shape=jax.ShapeDtypeStruct((2 * RUN, 512), bf16),
        grid=(2, 2),
        in_specs=[
            pl.BlockSpec(memory_space=pltpu.SMEM),
            pl.BlockSpec((1, RUN, 1), lambda r, p: (r, 0, 0)),
            pl.BlockSpec((1, 1, RUN), lambda r, p: (r, 0, 0)),
            pl.BlockSpec((RUN, 768), lambda r, p: (r, p)),
        ],
        out_specs=pl.BlockSpec((RUN, 256), lambda r, p: (r, p)),
        compiler_params=pltpu.CompilerParams(vmem_limit_bytes=8 * 1024 * 1024),
        cost_estimate=pl.CostEstimate(flops=4 * 16 * RUN * RUN * 64, bytes_accessed=1 << 20, transcendentals=32 * RUN * RUN),
    )(slopes, rows, cols, qkv)


def attend_back(qkv, ctx, dctx, rows, cols, slopes):
    row_block = pl.BlockSpec((RUN, 256), lambda r, p: (r, p))
    sums = pl.BlockSpec((1, 1, 1, 256), lambda r, p: (r, p, 0, 0))
    return pl.pallas_call(
        attend_back_kernel,
        out_shape=(
            jax.ShapeDtypeStruct((2 * RUN, 1536), bf16),
            jax.ShapeDtypeStruct((2, 2, 1, 256), f32),
            jax.ShapeDtypeStruct((2, 2, 1, 256), f32),
        ),
        grid=(2, 2),
        in_specs=[
            pl.BlockSpec(memory_space=pltpu.SMEM),
            pl.BlockSpec((1, RUN, 1), lambda r, p: (r, 0, 0)),
            pl.BlockSpec((1, 1, RUN), lambda r, p: (r, 0, 0)),
            pl.BlockSpec((RUN, 768), lambda r, p: (r, p)),
            row_block,
            row_block,
        ],
        out_specs=(pl.BlockSpec((RUN, 768), lambda r, p: (r, p)), sums, sums),
        compiler_params=pltpu.CompilerParams(vmem_limit_bytes=8 * 1024 * 1024),
        cost_estimate=pl.CostEstimate(flops=10 * 16 * RUN * RUN * 64, bytes_accessed=1 << 21, transcendentals=32 * RUN * RUN),
    )(slopes, rows, cols, qkv, ctx, dctx)


def layer_norm(stream, gains, shifts):
    average = jnp.mean(stream, axis=-1, keepdims=True)
    centered = stream - average
    variance = jnp.mean(centered * centered, axis=-1, keepdims=True)
    inv_std = lax.rsqrt(variance + epsilon)
    normed = centered * inv_std
    return (normed * gains + shifts, normed, inv_std)


def norm_back(grad_norm, normed, inv_std, gains):
    scaled = grad_norm * gains
    inner = (
        scaled
        - jnp.mean(scaled, axis=-1, keepdims=True)
        - normed * jnp.mean(scaled * normed, axis=-1, keepdims=True)
    )
    return (inv_std * inner, jnp.sum(grad_norm * normed, axis=0), jnp.sum(grad_norm, axis=0))


def gelu_tanh(values):
    inner = jnp.tanh(gelu_coef * (values + 0.044715 * values * values * values))
    return 0.5 * values * (1.0 + inner)


def gelu_slope(values):
    inner = jnp.tanh(gelu_coef * (values + 0.044715 * values * values * values))
    return 0.5 * (1.0 + inner) + 0.5 * values * (1.0 - inner * inner) * gelu_coef * (
        1.0 + 3.0 * 0.044715 * values * values
    )


def dot(a, b):
    return jnp.dot(a, b, preferred_element_type=f32)


def dot_nt(a, b):
    return lax.dot_general(a, b, (((1,), (1,)), ((), ())), preferred_element_type=f32)


def dot_tn(a, b):
    return lax.dot_general(a, b, (((0,), (0,)), ((), ())), preferred_element_type=f32)


def local(hidden_in, doc_start, grad_out, w_qkv, w_proj, w_up, w_down, norm_gain, d_bias, up_bias):
    x, yhi, z, core = (lax.axis_index(n) for n in ("x", "yhi", "z", "core"))
    at = jnp.stack([z, core]).astype(jnp.int32)
    at_x = jnp.stack([(z - x + 4) % 4, core]).astype(jnp.int32)
    index = jnp.arange(8, dtype=jnp.int32)

    def both(own):
        return jnp.concatenate([own, swap(own)], axis=0)

    def halves_summed(product, a, w):
        theirs = swap(product(a[RUN:], w))
        return product(a[:RUN], w) + theirs

    small = jnp.concatenate(
        [
            jnp.transpose(jnp.concatenate([norm_gain, d_bias], axis=2), (0, 2, 1)).reshape(16, 128),
            up_bias.reshape(8, 128),
        ]
    )

    mine_z, mine_x = select_weights(at, w_qkv, w_proj, w_up, w_down)
    weights = []
    thin = jnp.concatenate([small, jnp.zeros((4, 128), bf16)]).reshape(4, 896)
    first_z = to_all(jnp.concatenate([mine_z[0], thin, jnp.zeros((4, 896), bf16)]), SHARD, 8)
    all_small = first_z[:, 128:132].reshape(8, 28, 128)[:, :24]
    block_z = first_z[:, :128].reshape(D, 896)
    other = y_pair(mine_x[0])
    piece_x = jnp.concatenate([jnp.where(yhi == 0, mine_x[0], other), jnp.where(yhi == 0, other, mine_x[0])])
    own, following, (top, bottom), previous = ring_gather(after(piece_x, block_z), x_up, x_down)
    all_x = jnp.concatenate([own, following, top, bottom, previous]).reshape(8, 320, D)
    next_x = lax.all_gather(after(mine_x[1], block_z), SHARD, axis=0)
    for layer in range(LAYERS):
        own, following, (top, bottom), previous = ring_gather(block_z, z_up, z_down)
        wup, wqkv = split_z(at, own, following, top, bottom, previous)
        wdown, wproj = split_x(at_x if layer == 0 else at, all_x)
        weights.append((wqkv, wproj, wup, wdown))
        if layer == 0:
            next_z = to_all(after(mine_z[1], previous, following), SHARD, 8).reshape(D, 896)
            block_z, all_x = after(next_z, top, bottom), next_x

    small = all_small.reshape(4, 2, 24, 128).astype(f32)
    wide = jnp.transpose(small[:, :, :16], (2, 0, 1, 3)).reshape(LAYERS, 8, D)
    hidden_bias = small[:, :, 16:].reshape(4, 2, LAYERS, 2, 256)

    def core_heads(vector):
        picked = lax.dynamic_index_in_dim(vector.reshape(4, 2, 2, 64), core, axis=2, keepdims=False)
        return rolled(picked.reshape(4, 128), z)

    starts = both(doc_start.reshape(1, RUN))
    rows, cols = starts.reshape(2, RUN, 1), starts.reshape(2, 1, RUN)
    head = 4 * ((z + index // 2) % 4) + 2 * (index % 2) + core
    slopes = 2.0 ** (-8.0 * (head.astype(f32) + 1.0) / HEADS)

    kept = []
    current = hidden_in
    for layer in range(LAYERS):
        wqkv, wproj, wup, wdown = weights[layer]
        gain_one, gain_two, shift_one, shift_two, bq, bv, bproj, bdown = (wide[layer, i] for i in range(8))
        bq, bv = core_heads(bq), core_heads(bv)
        bqkv = jnp.stack([bq, jnp.zeros_like(bq), bv], axis=1).reshape(1536)
        ubias = lax.dynamic_index_in_dim(hidden_bias[:, :, layer], core, axis=2, keepdims=False)
        ubias = rolled(ubias.reshape(4, 512), z).reshape(2048)
        first_f, normed_one, inv_one = layer_norm(current, gain_one, shift_one)
        first_in = both(first_f.astype(bf16))
        qkv = (dot(first_in, wqkv) + bqkv).astype(bf16)
        ctx = attend(qkv, rows, cols, slopes)
        if layer == 0:
            ctx = after(ctx, next_z)
        middle = current + halves_summed(dot, ctx, wproj) + bproj
        second_f, normed_two, inv_two = layer_norm(middle, gain_two, shift_two)
        second_in = both(second_f.astype(bf16))
        upper = dot(second_in, wup) + ubias
        activ = gelu_tanh(upper).astype(bf16)
        current = middle + halves_summed(dot, activ, wdown) + bdown
        kept.append((first_in, normed_one, inv_one, qkv, ctx, second_in, normed_two, inv_two, upper, activ, gain_one, gain_two))
    hidden_out = current

    def summed(blocks):
        return jnp.sum(blocks.astype(f32), axis=0).astype(bf16)

    def ring_z(a2, dub, a1, dqkv):
        parts = [grad_z(at, a2, dub, a1, dqkv, i) for i in (2, 1, 3, 0)]
        parts = [parts[i] for i in (3, 1, 0, 2)]
        total, sent, near, got = ring_scatter(parts, z_up, z_down)
        return total.astype(bf16).reshape(16, 64, 896), (sent, near, got)

    def ring_x(m, dy, ctx, dr):
        parts = grad_x(at_x, m, dy, ctx, dr)
        total, _, near, got = ring_scatter([parts[2 * i : 2 * i + 2].reshape(640, D) for i in range(4)], x_up, x_down)
        part = total.astype(bf16).reshape(2, 320, D)
        part = jnp.concatenate([part[:, :256].reshape(2, 8, 32, D), part[:, 256:].reshape(2, 8, 8, D)], axis=2)
        return jnp.transpose(part, (1, 0, 2, 3)).reshape(16, 40, D), (near, got)

    def finish(part_z, part_x, *earlier):
        part_x = summed(exchange(part_x, ("ylo", "z", "yhi")))
        part_z = exchange(part_z, ("x", "yhi", "ylo"))
        return summed(after(part_z, *earlier) if earlier else part_z), part_x

    def share(part_z, part_x, *earlier):
        part = jnp.concatenate([part_z.reshape(56, D), part_x])
        parts = lax.all_gather(after(part, *earlier) if earlier else part, REP, axis=0)
        by_z = parts[:, :56].reshape(2, 4, 2, 64, 896)
        by_x = jnp.transpose(parts[:, 56:].reshape(8, 2, 40, D), (1, 0, 2, 3))
        return by_z, (by_x[:, :, :32].reshape(512, D), by_x[:, :, 32:].reshape(128, D))

    grads_x, grads_z = [None] * LAYERS, [None] * LAYERS
    thin_grads, head_grads, unit_grads = [None] * LAYERS, [None] * LAYERS, [None] * LAYERS
    running, ring_state = grad_out, None
    for layer in reversed(range(LAYERS)):
        wqkv, wproj, wup, wdown = weights[layer]
        first_in, normed_one, inv_one, qkv, ctx, second_in, normed_two, inv_two, upper, activ, gain_one, gain_two = kept[layer]
        if ring_state is not None:
            running = after(running, *ring_state[0])
        g_bdown = jnp.sum(running, axis=0)
        grad_yb = both(running.astype(bf16))
        grad_upper = dot_nt(grad_yb, wdown) * gelu_slope(upper)
        g_ubias = jnp.sum(grad_upper, axis=0)
        grad_ub = grad_upper.astype(bf16)
        grad_two = halves_summed(dot_nt, grad_ub, wup)
        back_two, g_gain_two, g_shift_two = norm_back(grad_two, normed_two, inv_two, gain_two)
        grad_mid = running + back_two
        g_bproj = jnp.sum(grad_mid, axis=0)
        grad_midb = grad_mid.astype(bf16)
        if ring_state is not None:
            grad_midb = after(grad_midb, *ring_state[1], *x_state[0])
            part_x_before = part_x
            later_state = x_state
        grad_midb = both(grad_midb)
        grad_ctx = dot_nt(grad_midb, wproj).astype(bf16)
        part_x, x_state = ring_x(activ, grad_yb, ctx, grad_midb)
        grad_qkv, g_bq, g_bv = attend_back(qkv, ctx, grad_ctx, rows, cols, slopes)
        if ring_state is not None:
            later = (after(part_z, grad_qkv), part_x_before)
            grad_qkv = after(grad_qkv, *ring_state[2], *later_state[1])
        part_z, ring_state = ring_z(second_in, grad_ub, first_in, grad_qkv)
        if layer == 0:
            grad_qkv = after(grad_qkv, *ring_state[0])
        grad_one = halves_summed(dot_nt, grad_qkv, wqkv)
        if layer == 0:
            grad_one = after(grad_one, *ring_state[1])
            grads_z[1], grads_x[1] = share(*finish(*later, *ring_state[1]))
        back_one, g_gain_one, g_shift_one = norm_back(grad_one, normed_one, inv_one, gain_one)
        running = grad_mid + back_one

        thin_grads[layer] = [g_gain_one, g_gain_two, g_shift_one, g_shift_two, g_bproj, g_bdown]
        head_grads[layer] = [jnp.sum(g, axis=0).reshape(4, 128) for g in (g_bq, g_bv)]
        unit_grads[layer] = g_ubias.reshape(4, 512)

    grads_z[0], grads_x[0] = share(*finish(part_z, part_x))

    thin = jnp.stack(thin_grads[0] + thin_grads[1]).reshape(LAYERS, 6, 4, 2, 128)
    heads = jnp.stack(head_grads[0] + head_grads[1], axis=1)
    heads = rolled(heads, (4 - z) % 4).reshape(4, LAYERS, 2, 2, 1, 64)
    mine = lax.broadcasted_iota(jnp.int32, (4, LAYERS, 2, 2, 2, 64), 4) == core
    heads = jnp.where(mine, heads, 0.0).reshape(4, LAYERS, 2, 2, 128)
    units = rolled(jnp.stack(unit_grads, axis=1), (4 - z) % 4).reshape(4, LAYERS, 2, 1, 256)
    mine = lax.broadcasted_iota(jnp.int32, (4, LAYERS, 2, 2, 256), 3) == core
    units = jnp.where(mine, units, 0.0).reshape(4, LAYERS, 2, 4, 128)
    thin = jnp.transpose(thin, (2, 3, 0, 1, 4))
    heads = jnp.transpose(heads, (0, 3, 1, 2, 4))
    units = jnp.transpose(units, (0, 2, 1, 3, 4))
    part = jnp.concatenate([thin[:, :, :, :4], heads, thin[:, :, :, 4:], units], axis=3)
    part = jnp.sum(exchange(part.reshape(8, 24, 128), SHARD), axis=0)
    part = jnp.sum(to_all(part, REP, 16), axis=0).reshape(LAYERS, 12, 128)
    g_wide = jnp.transpose(part[:, :8], (0, 2, 1))
    g_up, g_qkv = assemble(at, grads_z[0], grads_z[1])
    g_down, g_proj = (jnp.stack([grads_x[layer][i] for layer in range(LAYERS)]).astype(f32) for i in range(2))
    return (
        hidden_out,
        running,
        g_qkv,
        g_proj,
        g_up,
        g_down,
        g_wide[:, :, :2],
        g_wide[:, :, 2:],
        part[:, 8:].reshape(LAYERS, 512),
    )


def solution(mesh):
    fine = Mesh(mesh.devices.reshape(2, 4, 2, 4, 2), AXES)
    tokens = P(AXES)
    wide_tokens = P(AXES, None)
    params = P(None, ("x", "yhi"), None)
    return jax.shard_map(
        local,
        mesh=fine,
        in_specs=(wide_tokens, tokens, wide_tokens, params, params, params, params, params, params, P(None, ("x", "yhi"))),
        out_specs=(wide_tokens, wide_tokens, params, params, params, params, params, params, P(None, ("x", "yhi"))),
        check_vma=False,
    )
```

```python
import jax
import jax.numpy as jnp
from jax import lax
from jax.experimental import pallas as pl
from jax.experimental.pallas import tpu as pltpu
from jax.sharding import Mesh
from jax.sharding import PartitionSpec as P

HEADS = 16
HEAD_DIM = 64
LAYERS = 2
D = 1024
RUN = 128

epsilon = 1e-05
gelu_coef = 0.7978845608
f32 = jnp.float32
bf16 = jnp.bfloat16

AXES = ("ylo", "z", "core", "x", "yhi")


def ring(step):
    return [(i, (i + step) % 4) for i in range(4)]


def z_up(a):
    return lax.ppermute(a, "z", ring(1))


def z_down(a):
    return lax.ppermute(a, "z", ring(3))


def x_up(a):
    return lax.ppermute(a, "x", ring(1))


def x_down(a):
    return lax.ppermute(a, "x", ring(3))


def y_pair(a):
    return lax.ppermute(a, ("ylo", "yhi"), [(0, 3), (3, 0), (1, 2), (2, 1)])


def swap(a):
    return lax.ppermute(a, "core", [(0, 1), (1, 0)])


SHARD = ("x", "yhi")
REP = ("ylo", "z", "core")


def exchange(blocks, axes):
    return lax.all_to_all(blocks, axes, 0, 0, tiled=True)


def to_all(a, axes, count):
    return exchange(jnp.broadcast_to(a[None], (count, *a.shape)), axes)


def ring_gather(a, up, down):
    half = a.shape[0] // 2
    previous = up(a)
    following = down(a)
    top = up(previous[:half])
    bottom = down(following[half:])
    return a, following, (top, bottom), previous


def ring_scatter(parts, up, down):
    own, following, far, previous = parts
    half = own.shape[0] // 2
    from_previous = up(far[:half])
    from_following = down(far[half:])
    go_up = jnp.concatenate(
        [(following[:half].astype(f32) + from_previous.astype(f32)).astype(bf16), following[half:]]
    )
    go_down = jnp.concatenate(
        [previous[:half], (previous[half:].astype(f32) + from_following.astype(f32)).astype(bf16)]
    )
    got_up = up(go_up)
    got_down = down(go_down)
    total = own.astype(f32) + got_up.astype(f32) + got_down.astype(f32)
    return total, (following, previous), (from_previous, from_following), (got_up, got_down)


def rolled(stack, start):
    return lax.dynamic_slice_in_dim(jnp.concatenate([stack, stack[:3]]), start, 4, axis=0)


def after(a, *earlier):
    there = sum(jnp.abs(e[0, 0].astype(f32)) * 2.0**-40 for e in earlier) < 1e30
    return jnp.where(there, a, jnp.zeros_like(a))


def select_kernel(at_ref, up_a, up_b, q_ref, k_ref, v_ref, down_ref, proj_ref, by_z_ref, by_x_ref):
    first = at_ref[1] == 0
    by_z_ref[0, :, 0:256] = up_a[0]
    by_z_ref[0, :, 256:512] = up_b[0]
    for t, ref in enumerate((q_ref, k_ref, v_ref)):
        low = jnp.where(first, ref[0, :, 0:64].astype(f32), ref[0, :, 64:128].astype(f32))
        high = jnp.where(first, ref[0, :, 128:192].astype(f32), ref[0, :, 192:256].astype(f32))
        by_z_ref[0, :, 512 + t * 128 : 640 + t * 128] = jnp.concatenate([low, high], axis=1).astype(bf16)
    by_x_ref[0, 0:256] = down_ref[0]
    by_x_ref[0, 256:320] = proj_ref[0]


def select_weights(at, w_qkv, w_proj, w_up, w_down):
    def lanes(block):
        return pl.BlockSpec((1, 128, 256), lambda l, at: (l, 0, block(at)))

    return pl.pallas_call(
        select_kernel,
        out_shape=(
            jax.ShapeDtypeStruct((LAYERS, 128, 896), bf16),
            jax.ShapeDtypeStruct((LAYERS, 320, D), bf16),
        ),
        grid_spec=pltpu.PrefetchScalarGridSpec(
            num_scalar_prefetch=1,
            grid=(LAYERS,),
            in_specs=[
                lanes(lambda at: 4 * at[0] + at[1]),
                lanes(lambda at: 4 * at[0] + 2 + at[1]),
                lanes(lambda at: at[0]),
                lanes(lambda at: 4 + at[0]),
                lanes(lambda at: 8 + at[0]),
                pl.BlockSpec((1, 256, D), lambda l, at: (l, at[1], 0)),
                pl.BlockSpec((1, 64, D), lambda l, at: (l, at[1], 0)),
            ],
            out_specs=(
                pl.BlockSpec((1, 128, 896), lambda l, at: (l, 0, 0)),
                pl.BlockSpec((1, 320, D), lambda l, at: (l, 0, 0)),
            ),
        ),
        compiler_params=pltpu.CompilerParams(vmem_limit_bytes=8 * 1024 * 1024),
        cost_estimate=pl.CostEstimate(flops=0, bytes_accessed=4 * 1024 * 1024, transcendentals=0),
    )(at, w_up, w_up, w_qkv, w_qkv, w_qkv, w_down, w_proj)


def call(kernel, scalars, operands, out_shape, grid, in_specs, out_specs, flops=0):
    moved = sum(a.size * a.dtype.itemsize for a in operands) + sum(o.size * o.dtype.itemsize for o in jax.tree.leaves(out_shape))
    return pl.pallas_call(
        kernel,
        out_shape=out_shape,
        grid_spec=pltpu.PrefetchScalarGridSpec(
            num_scalar_prefetch=1, grid=grid, in_specs=in_specs, out_specs=out_specs
        ),
        compiler_params=pltpu.CompilerParams(vmem_limit_bytes=20 * 1024 * 1024),
        cost_estimate=pl.CostEstimate(flops=flops, bytes_accessed=moved, transcendentals=0),
    )(scalars, *operands)


def split_z_kernel(at_ref, own_ref, next_ref, top_ref, bottom_ref, last_ref, up_ref, qkv_ref):
    step = pl.program_id(0)

    def put(position, block):
        up_ref[:, position * 512 : position * 512 + 512] = block[:, :512]
        qkv_ref[:, position * 384 : position * 384 + 384] = block[:, 512:]

    put(0, own_ref)
    put(1, next_ref)
    put(3, last_ref)

    @pl.when(step < 4)
    def _():
        put(2, top_ref)

    @pl.when(step >= 4)
    def _():
        put(2, bottom_ref)


def split_z(at, own, following, top, bottom, previous):
    block = pl.BlockSpec((128, 896), lambda i, at: (i, 0))
    return call(
        split_z_kernel,
        at,
        (own, following, top, bottom, previous),
        (jax.ShapeDtypeStruct((D, 2048), bf16), jax.ShapeDtypeStruct((D, 1536), bf16)),
        (8,),
        [
            block,
            block,
            pl.BlockSpec((128, 896), lambda i, at: (jnp.minimum(i, 3), 0)),
            pl.BlockSpec((128, 896), lambda i, at: (jnp.maximum(i - 4, 0), 0)),
            block,
        ],
        (pl.BlockSpec((128, 2048), lambda i, at: (i, 0)), pl.BlockSpec((128, 1536), lambda i, at: (i, 0))),
    )


def split_x_kernel(at_ref, in_ref, down_ref, proj_ref):
    for e in range(2):
        down_ref[e * 256 : e * 256 + 256] = in_ref[e, 0:256]
        proj_ref[e * 64 : e * 64 + 64] = in_ref[e, 256:320]


def split_x(at, gathered):
    return call(
        split_x_kernel,
        at,
        (gathered,),
        (jax.ShapeDtypeStruct((2048, D), bf16), jax.ShapeDtypeStruct((512, D), bf16)),
        (4,),
        [pl.BlockSpec((2, gathered.shape[1], D), lambda i, at: (lax.rem(i + at[0], 4), 0, 0))],
        (pl.BlockSpec((512, D), lambda i, at: (i, 0)), pl.BlockSpec((128, D), lambda i, at: (i, 0))),
    )


def grad_z_kernel(at_ref, a2_ref, dub_ref, a1_ref, dqkv_ref, out_ref):
    out_ref[:, :512] = dot_tn(a2_ref[...], dub_ref[...]).astype(bf16)
    out_ref[:, 512:] = dot_tn(a1_ref[...], dqkv_ref[...]).astype(bf16)


def grad_z(at, a2, dub, a1, dqkv, block):
    rows = pl.BlockSpec((256, 256), lambda i, at: (0, i))
    return call(
        grad_z_kernel,
        at,
        (a2, dub, a1, dqkv),
        jax.ShapeDtypeStruct((D, 896), bf16),
        (4,),
        [
            rows,
            pl.BlockSpec((256, 512), lambda i, at: (0, block)),
            rows,
            pl.BlockSpec((256, 384), lambda i, at: (0, block)),
        ],
        pl.BlockSpec((256, 896), lambda i, at: (i, 0)),
        flops=2 * 256 * D * 896,
    )


def grad_x_kernel(at_ref, m_ref, dy_ref, ctx_ref, dr_ref, out_ref):
    for e in range(2):
        out_ref[e, 0:256] = dot_tn(m_ref[:, e * 256 : e * 256 + 256], dy_ref[...]).astype(bf16)
        out_ref[e, 256:320] = dot_tn(ctx_ref[:, e * 64 : e * 64 + 64], dr_ref[...]).astype(bf16)


def grad_x(at, m, dy, ctx, dr):
    whole = pl.BlockSpec((256, D), lambda i, at: (0, 0))
    return call(
        grad_x_kernel,
        at,
        (m, dy, ctx, dr),
        jax.ShapeDtypeStruct((8, 320, D), bf16),
        (4,),
        [
            pl.BlockSpec((256, 512), lambda i, at: (0, i)),
            whole,
            pl.BlockSpec((256, 128), lambda i, at: (0, i)),
            whole,
        ],
        pl.BlockSpec((2, 320, D), lambda i, at: (lax.rem(i + at[0], 4), 0, 0)),
        flops=2 * 256 * D * 2560,
    )


def assemble_kernel(at_ref, first_ref, second_ref, up_ref, qkv_ref, down_ref, proj_ref):
    def put(ref):
        for j in range(4):
            for e in range(2):
                for core in range(2):
                    at = j * 1024 + e * 512 + core * 256
                    up_ref[0, :, at : at + 256] = ref[0, j, core, :, e * 256 : e * 256 + 256].astype(f32)
                for t in range(3):
                    lane = 512 + t * 128 + e * 64
                    both = [ref[0, j, core, :, lane : lane + 64].astype(f32) for core in range(2)]
                    at = t * 1024 + j * 256 + e * 128
                    qkv_ref[0, :, at : at + 128] = jnp.concatenate(both, axis=1)
            for core in range(2):
                rest = ref[0, j, core, :, 896:].astype(f32)
                for b in range(8):
                    lanes = slice(b * 128, b * 128 + 128)
                    for g in range(4):
                        at = j * 32 + g * 8
                        down_ref[0, core, 0, at : at + 8, lanes] = rest[b * 8 : b * 8 + 8, g * 128 : g * 128 + 128]
                    proj_ref[0, core, 0, j * 8 : j * 8 + 8, lanes] = rest[b * 8 : b * 8 + 8, 512:640]

    @pl.when(pl.program_id(0) == 0)
    def _():
        put(first_ref)

    @pl.when(pl.program_id(0) == 1)
    def _():
        put(second_ref)


def assemble(at, first, second):
    block = (1, 4, 2, 64, 1536)
    return call(
        assemble_kernel,
        at,
        (first, second),
        (
            jax.ShapeDtypeStruct((LAYERS, 128, 4096), f32),
            jax.ShapeDtypeStruct((LAYERS, 128, 3072), f32),
            jax.ShapeDtypeStruct((LAYERS, 2, 2, 128, D), f32),
            jax.ShapeDtypeStruct((LAYERS, 2, 2, 32, D), f32),
        ),
        (LAYERS, 2),
        [
            pl.BlockSpec(block, lambda l, h, at: (h, 0, 0, 0, 0)),
            pl.BlockSpec(block, lambda l, h, at: (h, 0, 0, 0, 0)),
        ],
        (
            pl.BlockSpec((1, 64, 4096), lambda l, h, at: (l, h, 0)),
            pl.BlockSpec((1, 64, 3072), lambda l, h, at: (l, h, 0)),
            pl.BlockSpec((1, 2, 1, 128, D), lambda l, h, at: (l, 0, h, 0, 0)),
            pl.BlockSpec((1, 2, 1, 32, D), lambda l, h, at: (l, 0, h, 0, 0)),
        ),
    )


def head_scores(q, k, seen, distance, slope):
    s = lax.dot_general(q, k, (((1,), (1,)), ((), ())), preferred_element_type=f32) * HEAD_DIM ** (-0.5)
    s = s - slope * distance
    return jnp.where(seen, s, f32(-1000000000.0))


def visibility(row_start, col_start):
    row = lax.broadcasted_iota(jnp.int32, (RUN, RUN), 0)
    col = lax.broadcasted_iota(jnp.int32, (RUN, RUN), 1)
    seen = (row_start == col_start) & (col <= row)
    return seen, (row - col).astype(f32)


def attend_kernel(slope_ref, rows_ref, cols_ref, qkv_ref, ctx_ref):
    first = pl.program_id(1) * 4
    seen, distance = visibility(rows_ref[0], cols_ref[0])
    done = []
    for i in range(4):
        at = (i // 2) * 384 + (i % 2) * 64
        q = qkv_ref[:, at : at + 64]
        k = qkv_ref[:, at + 128 : at + 192]
        v = qkv_ref[:, at + 256 : at + 320]
        s = head_scores(q, k, seen, distance, slope_ref[first + i])
        top = jnp.max(s, axis=-1, keepdims=True)
        lse = top + jnp.log(jnp.sum(jnp.exp(s - top), axis=-1, keepdims=True))
        p = jnp.exp(s - lse).astype(bf16)
        done.append(jnp.dot(p, v, preferred_element_type=f32))
    ctx_ref[...] = jnp.concatenate(done, axis=1).astype(bf16)


def attend_back_kernel(slope_ref, rows_ref, cols_ref, qkv_ref, ctx_ref, dctx_ref, dqkv_ref, dq_ref, dv_ref):
    first = pl.program_id(1) * 4
    seen, distance = visibility(rows_ref[0], cols_ref[0])
    dqs, dks, dvs = [], [], []
    tn = (((0,), (0,)), ((), ()))
    nt = (((1,), (1,)), ((), ()))
    for i in range(4):
        lanes = slice(i * 64, i * 64 + 64)
        at = (i // 2) * 384 + (i % 2) * 64
        q = qkv_ref[:, at : at + 64]
        k = qkv_ref[:, at + 128 : at + 192]
        v = qkv_ref[:, at + 256 : at + 320]
        s = head_scores(q, k, seen, distance, slope_ref[first + i])
        top = jnp.max(s, axis=-1, keepdims=True)
        lse = top + jnp.log(jnp.sum(jnp.exp(s - top), axis=-1, keepdims=True))
        p = jnp.exp(s - lse)
        dctx = dctx_ref[:, lanes]
        dv = lax.dot_general(p.astype(bf16), dctx, tn, preferred_element_type=f32)
        dp = lax.dot_general(dctx, v, nt, preferred_element_type=f32)
        delta = jnp.sum(dctx.astype(f32) * ctx_ref[:, lanes].astype(f32), axis=-1, keepdims=True)
        ds = (p * (dp - delta)).astype(bf16)
        dqs.append(jnp.dot(ds, k, preferred_element_type=f32) * HEAD_DIM ** (-0.5))
        dks.append(lax.dot_general(ds, q, tn, preferred_element_type=f32) * HEAD_DIM ** (-0.5))
        dvs.append(dv)
    for pair in range(2):
        at = pair * 384
        dq = jnp.concatenate(dqs[2 * pair : 2 * pair + 2], axis=1)
        dk = jnp.concatenate(dks[2 * pair : 2 * pair + 2], axis=1)
        dv = jnp.concatenate(dvs[2 * pair : 2 * pair + 2], axis=1)
        dqkv_ref[:, at : at + 128] = dq.astype(bf16)
        dqkv_ref[:, at + 128 : at + 256] = dk.astype(bf16)
        dqkv_ref[:, at + 256 : at + 384] = dv.astype(bf16)
        dq_ref[0, 0, :, pair * 128 : pair * 128 + 128] = jnp.sum(dq, axis=0, keepdims=True)
        dv_ref[0, 0, :, pair * 128 : pair * 128 + 128] = jnp.sum(dv, axis=0, keepdims=True)


def attend(qkv, rows, cols, slopes):
    return pl.pallas_call(
        attend_kernel,
        out_shape=jax.ShapeDtypeStruct((2 * RUN, 512), bf16),
        grid=(2, 2),
        in_specs=[
            pl.BlockSpec(memory_space=pltpu.SMEM),
            pl.BlockSpec((1, RUN, 1), lambda r, p: (r, 0, 0)),
            pl.BlockSpec((1, 1, RUN), lambda r, p: (r, 0, 0)),
            pl.BlockSpec((RUN, 768), lambda r, p: (r, p)),
        ],
        out_specs=pl.BlockSpec((RUN, 256), lambda r, p: (r, p)),
        compiler_params=pltpu.CompilerParams(vmem_limit_bytes=8 * 1024 * 1024),
        cost_estimate=pl.CostEstimate(flops=4 * 16 * RUN * RUN * 64, bytes_accessed=1 << 20, transcendentals=32 * RUN * RUN),
    )(slopes, rows, cols, qkv)


def attend_back(qkv, ctx, dctx, rows, cols, slopes):
    row_block = pl.BlockSpec((RUN, 256), lambda r, p: (r, p))
    sums = pl.BlockSpec((1, 1, 1, 256), lambda r, p: (r, p, 0, 0))
    return pl.pallas_call(
        attend_back_kernel,
        out_shape=(
            jax.ShapeDtypeStruct((2 * RUN, 1536), bf16),
            jax.ShapeDtypeStruct((2, 2, 1, 256), f32),
            jax.ShapeDtypeStruct((2, 2, 1, 256), f32),
        ),
        grid=(2, 2),
        in_specs=[
            pl.BlockSpec(memory_space=pltpu.SMEM),
            pl.BlockSpec((1, RUN, 1), lambda r, p: (r, 0, 0)),
            pl.BlockSpec((1, 1, RUN), lambda r, p: (r, 0, 0)),
            pl.BlockSpec((RUN, 768), lambda r, p: (r, p)),
            row_block,
            row_block,
        ],
        out_specs=(pl.BlockSpec((RUN, 768), lambda r, p: (r, p)), sums, sums),
        compiler_params=pltpu.CompilerParams(vmem_limit_bytes=8 * 1024 * 1024),
        cost_estimate=pl.CostEstimate(flops=10 * 16 * RUN * RUN * 64, bytes_accessed=1 << 21, transcendentals=32 * RUN * RUN),
    )(slopes, rows, cols, qkv, ctx, dctx)


def layer_norm(stream, gains, shifts):
    average = jnp.mean(stream, axis=-1, keepdims=True)
    centered = stream - average
    variance = jnp.mean(centered * centered, axis=-1, keepdims=True)
    inv_std = lax.rsqrt(variance + epsilon)
    normed = centered * inv_std
    return (normed * gains + shifts, normed, inv_std)


def norm_back(grad_norm, normed, inv_std, gains):
    scaled = grad_norm * gains
    inner = (
        scaled
        - jnp.mean(scaled, axis=-1, keepdims=True)
        - normed * jnp.mean(scaled * normed, axis=-1, keepdims=True)
    )
    return (inv_std * inner, jnp.sum(grad_norm * normed, axis=0), jnp.sum(grad_norm, axis=0))


def gelu_tanh(values):
    inner = jnp.tanh(gelu_coef * (values + 0.044715 * values * values * values))
    return 0.5 * values * (1.0 + inner)


def gelu_slope(values):
    inner = jnp.tanh(gelu_coef * (values + 0.044715 * values * values * values))
    return 0.5 * (1.0 + inner) + 0.5 * values * (1.0 - inner * inner) * gelu_coef * (
        1.0 + 3.0 * 0.044715 * values * values
    )


def dot(a, b):
    return jnp.dot(a, b, preferred_element_type=f32)


def dot_nt(a, b):
    return lax.dot_general(a, b, (((1,), (1,)), ((), ())), preferred_element_type=f32)


def dot_tn(a, b):
    return lax.dot_general(a, b, (((0,), (0,)), ((), ())), preferred_element_type=f32)


def local(hidden_in, doc_start, grad_out, w_qkv, w_proj, w_up, w_down, norm_gain, d_bias, up_bias):
    x, yhi, z, core = (lax.axis_index(n) for n in ("x", "yhi", "z", "core"))
    at = jnp.stack([z, core]).astype(jnp.int32)
    at_x = jnp.stack([(z - x + 4) % 4, core]).astype(jnp.int32)
    index = jnp.arange(8, dtype=jnp.int32)

    def both(own):
        return jnp.concatenate([own, swap(own)], axis=0)

    def halves_summed(product, a, w):
        theirs = swap(product(a[RUN:], w))
        return product(a[:RUN], w) + theirs

    small = jnp.concatenate(
        [
            jnp.transpose(jnp.concatenate([norm_gain, d_bias], axis=2), (0, 2, 1)).reshape(16, 128),
            up_bias.reshape(8, 128),
        ]
    )

    mine_z, mine_x = select_weights(at, w_qkv, w_proj, w_up, w_down)
    weights = []
    thin = jnp.concatenate([small, jnp.zeros((4, 128), bf16)]).reshape(4, 896)
    first_z = to_all(jnp.concatenate([mine_z[0], thin, jnp.zeros((4, 896), bf16)]), SHARD, 8)
    all_small = first_z[:, 128:132].reshape(8, 28, 128)[:, :24]
    block_z = first_z[:, :128].reshape(D, 896)
    other = y_pair(mine_x[0])
    piece_x = jnp.concatenate([jnp.where(yhi == 0, mine_x[0], other), jnp.where(yhi == 0, other, mine_x[0])])
    own, following, (top, bottom), previous = ring_gather(after(piece_x, block_z), x_up, x_down)
    all_x = jnp.concatenate([own, following, top, bottom, previous]).reshape(8, 320, D)
    next_x = lax.all_gather(after(mine_x[1], block_z), SHARD, axis=0)
    for layer in range(LAYERS):
        own, following, (top, bottom), previous = ring_gather(block_z, z_up, z_down)
        wup, wqkv = split_z(at, own, following, top, bottom, previous)
        wdown, wproj = split_x(at_x if layer == 0 else at, all_x)
        weights.append((wqkv, wproj, wup, wdown))
        if layer == 0:
            next_z = to_all(after(mine_z[1], previous, following), SHARD, 8).reshape(D, 896)
            block_z, all_x = after(next_z, top, bottom), next_x
        else:
            second_ring = (previous, following)

    small = all_small.reshape(4, 2, 24, 128).astype(f32)
    wide = jnp.transpose(small[:, :, :16], (2, 0, 1, 3)).reshape(LAYERS, 8, D)
    hidden_bias = small[:, :, 16:].reshape(4, 2, LAYERS, 2, 256)

    def core_heads(vector):
        picked = lax.dynamic_index_in_dim(vector.reshape(4, 2, 2, 64), core, axis=2, keepdims=False)
        return rolled(picked.reshape(4, 128), z)

    starts = both(doc_start.reshape(1, RUN))
    rows, cols = starts.reshape(2, RUN, 1), starts.reshape(2, 1, RUN)
    head = 4 * ((z + index // 2) % 4) + 2 * (index % 2) + core
    slopes = 2.0 ** (-8.0 * (head.astype(f32) + 1.0) / HEADS)

    kept = []
    current = hidden_in
    for layer in range(LAYERS):
        wqkv, wproj, wup, wdown = weights[layer]
        gain_one, gain_two, shift_one, shift_two, bq, bv, bproj, bdown = (wide[layer, i] for i in range(8))
        bq, bv = core_heads(bq), core_heads(bv)
        bqkv = jnp.stack([bq, jnp.zeros_like(bq), bv], axis=1).reshape(1536)
        ubias = lax.dynamic_index_in_dim(hidden_bias[:, :, layer], core, axis=2, keepdims=False)
        ubias = rolled(ubias.reshape(4, 512), z).reshape(2048)
        first_f, normed_one, inv_one = layer_norm(current, gain_one, shift_one)
        first_in = both(first_f.astype(bf16))
        if layer == 0:
            first_in = after(first_in, next_z)
        qkv = (dot(first_in, wqkv) + bqkv).astype(bf16)
        ctx = attend(qkv, rows, cols, slopes)
        if layer == 0:
            ctx = after(ctx, *second_ring)
        middle = current + halves_summed(dot, ctx, wproj) + bproj
        second_f, normed_two, inv_two = layer_norm(middle, gain_two, shift_two)
        second_in = both(second_f.astype(bf16))
        upper = dot(second_in, wup) + ubias
        activ = gelu_tanh(upper).astype(bf16)
        current = middle + halves_summed(dot, activ, wdown) + bdown
        kept.append((first_in, normed_one, inv_one, qkv, ctx, second_in, normed_two, inv_two, upper, activ, gain_one, gain_two))
    hidden_out = current

    def summed(blocks):
        return jnp.sum(blocks.astype(f32), axis=0).astype(bf16)

    def ring_z(a2, dub, a1, dqkv):
        parts = [grad_z(at, a2, dub, a1, dqkv, i) for i in (2, 1, 3, 0)]
        parts = [parts[i] for i in (3, 1, 0, 2)]
        total, sent, near, got = ring_scatter(parts, z_up, z_down)
        return total.astype(bf16).reshape(16, 64, 896), (sent, near, got)

    def ring_x(m, dy, ctx, dr):
        parts = grad_x(at_x, m, dy, ctx, dr)
        total, _, near, got = ring_scatter([parts[2 * i : 2 * i + 2].reshape(640, D) for i in range(4)], x_up, x_down)
        part = total.astype(bf16).reshape(2, 320, D)
        part = jnp.concatenate([part[:, :256].reshape(2, 8, 32, D), part[:, 256:].reshape(2, 8, 8, D)], axis=2)
        return jnp.transpose(part, (1, 0, 2, 3)).reshape(16, 40, D), (near, got)

    def finish(part_z, part_x, *earlier):
        part_x = summed(exchange(part_x, ("ylo", "z", "yhi")))
        part_z = exchange(part_z, ("x", "yhi", "ylo"))
        return summed(after(part_z, *earlier) if earlier else part_z), part_x

    def share(part_z, part_x):
        part_x = jnp.transpose(part_x.reshape(5, 8, 8, 128), (2, 1, 0, 3)).reshape(64, 640)
        parts = lax.all_gather(jnp.concatenate([part_z, part_x], axis=1), REP, axis=0)
        return parts.reshape(2, 4, 2, 64, 1536)

    shared = [None] * LAYERS
    thin_grads, head_grads, unit_grads = [None] * LAYERS, [None] * LAYERS, [None] * LAYERS
    running, ring_state = grad_out, None
    for layer in reversed(range(LAYERS)):
        wqkv, wproj, wup, wdown = weights[layer]
        first_in, normed_one, inv_one, qkv, ctx, second_in, normed_two, inv_two, upper, activ, gain_one, gain_two = kept[layer]
        if ring_state is not None:
            running = after(running, *ring_state[0])
        g_bdown = jnp.sum(running, axis=0)
        grad_yb = both(running.astype(bf16))
        grad_upper = dot_nt(grad_yb, wdown) * gelu_slope(upper)
        g_ubias = jnp.sum(grad_upper, axis=0)
        grad_ub = grad_upper.astype(bf16)
        grad_two = halves_summed(dot_nt, grad_ub, wup)
        back_two, g_gain_two, g_shift_two = norm_back(grad_two, normed_two, inv_two, gain_two)
        grad_mid = running + back_two
        g_bproj = jnp.sum(grad_mid, axis=0)
        grad_midb = grad_mid.astype(bf16)
        if ring_state is not None:
            grad_midb = after(grad_midb, *ring_state[1], *x_state[0])
            part_x_before = part_x
        grad_midb = both(grad_midb)
        grad_ctx = dot_nt(grad_midb, wproj).astype(bf16)
        part_x, x_state = ring_x(activ, grad_yb, ctx, grad_midb)
        grad_qkv, g_bq, g_bv = attend_back(qkv, ctx, grad_ctx, rows, cols, slopes)
        if ring_state is not None:
            later = (after(part_z, grad_qkv), part_x_before)
            grad_qkv = after(grad_qkv, *ring_state[2], *x_state[0])
        part_z, ring_state = ring_z(second_in, grad_ub, first_in, grad_qkv)
        if layer == 0:
            grad_qkv = after(grad_qkv, *ring_state[0])
        grad_one = halves_summed(dot_nt, grad_qkv, wqkv)
        if layer == 0:
            grad_one = after(grad_one, *ring_state[1])
            shared[1] = share(*finish(*later, *ring_state[1]))
        back_one, g_gain_one, g_shift_one = norm_back(grad_one, normed_one, inv_one, gain_one)
        running = grad_mid + back_one

        thin_grads[layer] = [g_gain_one, g_gain_two, g_shift_one, g_shift_two, g_bproj, g_bdown]
        head_grads[layer] = [jnp.sum(g, axis=0).reshape(4, 128) for g in (g_bq, g_bv)]
        unit_grads[layer] = g_ubias.reshape(4, 512)

    shared[0] = share(*finish(part_z, part_x))

    thin = jnp.stack(thin_grads[0] + thin_grads[1]).reshape(LAYERS, 6, 4, 2, 128)
    heads = jnp.stack(head_grads[0] + head_grads[1], axis=1)
    heads = rolled(heads, (4 - z) % 4).reshape(4, LAYERS, 2, 2, 1, 64)
    mine = lax.broadcasted_iota(jnp.int32, (4, LAYERS, 2, 2, 2, 64), 4) == core
    heads = jnp.where(mine, heads, 0.0).reshape(4, LAYERS, 2, 2, 128)
    units = rolled(jnp.stack(unit_grads, axis=1), (4 - z) % 4).reshape(4, LAYERS, 2, 1, 256)
    mine = lax.broadcasted_iota(jnp.int32, (4, LAYERS, 2, 2, 256), 3) == core
    units = jnp.where(mine, units, 0.0).reshape(4, LAYERS, 2, 4, 128)
    thin = jnp.transpose(thin, (2, 3, 0, 1, 4))
    heads = jnp.transpose(heads, (0, 3, 1, 2, 4))
    units = jnp.transpose(units, (0, 2, 1, 3, 4))
    part = jnp.concatenate([thin[:, :, :, :4], heads, thin[:, :, :, 4:], units], axis=3)
    part = jnp.sum(exchange(part.reshape(8, 24, 128), SHARD), axis=0)
    part = jnp.sum(to_all(part, REP, 16), axis=0).reshape(LAYERS, 12, 128)
    g_wide = jnp.transpose(part[:, :8], (0, 2, 1))
    g_up, g_qkv, g_down, g_proj = assemble(at, shared[0], shared[1])
    return (
        hidden_out,
        running,
        g_qkv,
        g_proj.reshape(LAYERS, 128, D),
        g_up,
        g_down.reshape(LAYERS, 512, D),
        g_wide[:, :, :2],
        g_wide[:, :, 2:],
        part[:, 8:].reshape(LAYERS, 512),
    )


def solution(mesh):
    fine = Mesh(mesh.devices.reshape(2, 4, 2, 4, 2), AXES)
    tokens = P(AXES)
    wide_tokens = P(AXES, None)
    params = P(None, ("x", "yhi"), None)
    return jax.shard_map(
        local,
        mesh=fine,
        in_specs=(wide_tokens, tokens, wide_tokens, params, params, params, params, params, params, P(None, ("x", "yhi"))),
        out_specs=(wide_tokens, wide_tokens, params, params, params, params, params, params, P(None, ("x", "yhi"))),
        check_vma=False,
    )
```

```python
import jax
import jax.numpy as jnp
from jax import lax
from jax.experimental import pallas as pl
from jax.experimental.pallas import tpu as pltpu
from jax.sharding import Mesh
from jax.sharding import PartitionSpec as P

HEADS = 16
HEAD_DIM = 64
LAYERS = 2
D = 1024
RUN = 128

epsilon = 1e-05
gelu_coef = 0.7978845608
f32 = jnp.float32
bf16 = jnp.bfloat16

AXES = ("ylo", "z", "core", "x", "yhi")


def ring(step):
    return [(i, (i + step) % 4) for i in range(4)]


def z_up(a):
    return lax.ppermute(a, "z", ring(1))


def z_down(a):
    return lax.ppermute(a, "z", ring(3))


def x_up(a):
    return lax.ppermute(a, "x", ring(1))


def x_down(a):
    return lax.ppermute(a, "x", ring(3))


def y_pair(a):
    return lax.ppermute(a, ("ylo", "yhi"), [(0, 3), (3, 0), (1, 2), (2, 1)])


def swap(a):
    return lax.ppermute(a, "core", [(0, 1), (1, 0)])


SHARD = ("x", "yhi")
REP = ("ylo", "z", "core")


def exchange(blocks, axes):
    return lax.all_to_all(blocks, axes, 0, 0, tiled=True)


def to_all(a, axes, count):
    return exchange(jnp.broadcast_to(a[None], (count, *a.shape)), axes)


def ring_gather(a, up, down):
    half = a.shape[0] // 2
    previous = up(a)
    following = down(a)
    top = up(previous[:half])
    bottom = down(following[half:])
    return a, following, (top, bottom), previous


def ring_scatter(parts, up, down):
    own, following, far, previous = parts
    half = own.shape[0] // 2
    from_previous = up(far[:half])
    from_following = down(far[half:])
    go_up = jnp.concatenate(
        [(following[:half].astype(f32) + from_previous.astype(f32)).astype(bf16), following[half:]]
    )
    go_down = jnp.concatenate(
        [previous[:half], (previous[half:].astype(f32) + from_following.astype(f32)).astype(bf16)]
    )
    got_up = up(go_up)
    got_down = down(go_down)
    total = own.astype(f32) + got_up.astype(f32) + got_down.astype(f32)
    return total, (following, previous), (from_previous, from_following), (got_up, got_down)


def rolled(stack, start):
    return lax.dynamic_slice_in_dim(jnp.concatenate([stack, stack[:3]]), start, 4, axis=0)


def after(a, *earlier):
    there = sum(jnp.abs(e[0, 0].astype(f32)) * 2.0**-40 for e in earlier) < 1e30
    return jnp.where(there, a, jnp.zeros_like(a))


def select_kernel(at_ref, up_a, up_b, q_ref, k_ref, v_ref, down_ref, proj_ref, by_z_ref, by_x_ref):
    first = at_ref[1] == 0
    by_z_ref[0, :, 0:256] = up_a[0]
    by_z_ref[0, :, 256:512] = up_b[0]
    for t, ref in enumerate((q_ref, k_ref, v_ref)):
        low = jnp.where(first, ref[0, :, 0:64].astype(f32), ref[0, :, 64:128].astype(f32))
        high = jnp.where(first, ref[0, :, 128:192].astype(f32), ref[0, :, 192:256].astype(f32))
        by_z_ref[0, :, 512 + t * 128 : 640 + t * 128] = jnp.concatenate([low, high], axis=1).astype(bf16)
    by_x_ref[0, 0:256] = down_ref[0]
    by_x_ref[0, 256:320] = proj_ref[0]


def select_weights(at, w_qkv, w_proj, w_up, w_down):
    def lanes(block):
        return pl.BlockSpec((1, 128, 256), lambda l, at: (l, 0, block(at)))

    return pl.pallas_call(
        select_kernel,
        out_shape=(
            jax.ShapeDtypeStruct((LAYERS, 128, 896), bf16),
            jax.ShapeDtypeStruct((LAYERS, 320, D), bf16),
        ),
        grid_spec=pltpu.PrefetchScalarGridSpec(
            num_scalar_prefetch=1,
            grid=(LAYERS,),
            in_specs=[
                lanes(lambda at: 4 * at[0] + at[1]),
                lanes(lambda at: 4 * at[0] + 2 + at[1]),
                lanes(lambda at: at[0]),
                lanes(lambda at: 4 + at[0]),
                lanes(lambda at: 8 + at[0]),
                pl.BlockSpec((1, 256, D), lambda l, at: (l, at[1], 0)),
                pl.BlockSpec((1, 64, D), lambda l, at: (l, at[1], 0)),
            ],
            out_specs=(
                pl.BlockSpec((1, 128, 896), lambda l, at: (l, 0, 0)),
                pl.BlockSpec((1, 320, D), lambda l, at: (l, 0, 0)),
            ),
        ),
        compiler_params=pltpu.CompilerParams(vmem_limit_bytes=8 * 1024 * 1024),
        cost_estimate=pl.CostEstimate(flops=0, bytes_accessed=4 * 1024 * 1024, transcendentals=0),
    )(at, w_up, w_up, w_qkv, w_qkv, w_qkv, w_down, w_proj)


def call(kernel, scalars, operands, out_shape, grid, in_specs, out_specs, flops=0):
    moved = sum(a.size * a.dtype.itemsize for a in operands) + sum(o.size * o.dtype.itemsize for o in jax.tree.leaves(out_shape))
    return pl.pallas_call(
        kernel,
        out_shape=out_shape,
        grid_spec=pltpu.PrefetchScalarGridSpec(
            num_scalar_prefetch=1, grid=grid, in_specs=in_specs, out_specs=out_specs
        ),
        compiler_params=pltpu.CompilerParams(vmem_limit_bytes=20 * 1024 * 1024),
        cost_estimate=pl.CostEstimate(flops=flops, bytes_accessed=moved, transcendentals=0),
    )(scalars, *operands)


def split_z_kernel(at_ref, own_ref, next_ref, top_ref, bottom_ref, last_ref, up_ref, qkv_ref):
    step = pl.program_id(0)

    def put(position, block):
        up_ref[:, position * 512 : position * 512 + 512] = block[:, :512]
        qkv_ref[:, position * 384 : position * 384 + 384] = block[:, 512:]

    put(0, own_ref)
    put(1, next_ref)
    put(3, last_ref)

    @pl.when(step < 4)
    def _():
        put(2, top_ref)

    @pl.when(step >= 4)
    def _():
        put(2, bottom_ref)


def split_z(at, own, following, top, bottom, previous):
    block = pl.BlockSpec((128, 896), lambda i, at: (i, 0))
    return call(
        split_z_kernel,
        at,
        (own, following, top, bottom, previous),
        (jax.ShapeDtypeStruct((D, 2048), bf16), jax.ShapeDtypeStruct((D, 1536), bf16)),
        (8,),
        [
            block,
            block,
            pl.BlockSpec((128, 896), lambda i, at: (jnp.minimum(i, 3), 0)),
            pl.BlockSpec((128, 896), lambda i, at: (jnp.maximum(i - 4, 0), 0)),
            block,
        ],
        (pl.BlockSpec((128, 2048), lambda i, at: (i, 0)), pl.BlockSpec((128, 1536), lambda i, at: (i, 0))),
    )


def split_x_kernel(at_ref, in_ref, down_ref, proj_ref):
    for e in range(2):
        down_ref[e * 256 : e * 256 + 256] = in_ref[e, 0:256]
        proj_ref[e * 64 : e * 64 + 64] = in_ref[e, 256:320]


def split_x(at, gathered):
    return call(
        split_x_kernel,
        at,
        (gathered,),
        (jax.ShapeDtypeStruct((2048, D), bf16), jax.ShapeDtypeStruct((512, D), bf16)),
        (4,),
        [pl.BlockSpec((2, gathered.shape[1], D), lambda i, at: (lax.rem(i + at[0], 4), 0, 0))],
        (pl.BlockSpec((512, D), lambda i, at: (i, 0)), pl.BlockSpec((128, D), lambda i, at: (i, 0))),
    )


def grad_z_kernel(at_ref, a2_ref, dub_ref, a1_ref, dqkv_ref, out_ref):
    out_ref[:, :512] = dot_tn(a2_ref[...], dub_ref[...]).astype(bf16)
    out_ref[:, 512:] = dot_tn(a1_ref[...], dqkv_ref[...]).astype(bf16)


def grad_z(at, a2, dub, a1, dqkv, block):
    rows = pl.BlockSpec((256, 256), lambda i, at: (0, i))
    return call(
        grad_z_kernel,
        at,
        (a2, dub, a1, dqkv),
        jax.ShapeDtypeStruct((D, 896), bf16),
        (4,),
        [
            rows,
            pl.BlockSpec((256, 512), lambda i, at: (0, block)),
            rows,
            pl.BlockSpec((256, 384), lambda i, at: (0, block)),
        ],
        pl.BlockSpec((256, 896), lambda i, at: (i, 0)),
        flops=2 * 256 * D * 896,
    )


def grad_x_kernel(at_ref, m_ref, dy_ref, ctx_ref, dr_ref, out_ref):
    for e in range(2):
        out_ref[e, 0:256] = dot_tn(m_ref[:, e * 256 : e * 256 + 256], dy_ref[...]).astype(bf16)
        out_ref[e, 256:320] = dot_tn(ctx_ref[:, e * 64 : e * 64 + 64], dr_ref[...]).astype(bf16)


def grad_x(at, m, dy, ctx, dr):
    whole = pl.BlockSpec((256, D), lambda i, at: (0, 0))
    return call(
        grad_x_kernel,
        at,
        (m, dy, ctx, dr),
        jax.ShapeDtypeStruct((8, 320, D), bf16),
        (4,),
        [
            pl.BlockSpec((256, 512), lambda i, at: (0, i)),
            whole,
            pl.BlockSpec((256, 128), lambda i, at: (0, i)),
            whole,
        ],
        pl.BlockSpec((2, 320, D), lambda i, at: (lax.rem(i + at[0], 4), 0, 0)),
        flops=2 * 256 * D * 2560,
    )


def assemble_kernel(at_ref, first_ref, second_ref, up_ref, qkv_ref, down_ref, proj_ref):
    def put(ref):
        for j in range(4):
            for e in range(2):
                for core in range(2):
                    at = j * 1024 + e * 512 + core * 256
                    up_ref[0, :, at : at + 256] = ref[0, j, core, :, e * 256 : e * 256 + 256].astype(f32)
                for t in range(3):
                    lane = 512 + t * 128 + e * 64
                    both = [ref[0, j, core, :, lane : lane + 64].astype(f32) for core in range(2)]
                    at = t * 1024 + j * 256 + e * 128
                    qkv_ref[0, :, at : at + 128] = jnp.concatenate(both, axis=1)
            for core in range(2):
                rest = ref[0, j, core, :, 896:].astype(f32)
                for b in range(8):
                    lanes = slice(b * 128, b * 128 + 128)
                    for g in range(4):
                        at = j * 32 + g * 8
                        down_ref[0, core, 0, at : at + 8, lanes] = rest[b * 8 : b * 8 + 8, g * 128 : g * 128 + 128]
                    proj_ref[0, core, 0, j * 8 : j * 8 + 8, lanes] = rest[b * 8 : b * 8 + 8, 512:640]

    @pl.when(pl.program_id(0) == 0)
    def _():
        put(first_ref)

    @pl.when(pl.program_id(0) == 1)
    def _():
        put(second_ref)


def assemble(at, first, second):
    block = (1, 4, 2, 64, 1536)
    return call(
        assemble_kernel,
        at,
        (first, second),
        (
            jax.ShapeDtypeStruct((LAYERS, 128, 4096), f32),
            jax.ShapeDtypeStruct((LAYERS, 128, 3072), f32),
            jax.ShapeDtypeStruct((LAYERS, 2, 2, 128, D), f32),
            jax.ShapeDtypeStruct((LAYERS, 2, 2, 32, D), f32),
        ),
        (LAYERS, 2),
        [
            pl.BlockSpec(block, lambda l, h, at: (h, 0, 0, 0, 0)),
            pl.BlockSpec(block, lambda l, h, at: (h, 0, 0, 0, 0)),
        ],
        (
            pl.BlockSpec((1, 64, 4096), lambda l, h, at: (l, h, 0)),
            pl.BlockSpec((1, 64, 3072), lambda l, h, at: (l, h, 0)),
            pl.BlockSpec((1, 2, 1, 128, D), lambda l, h, at: (l, 0, h, 0, 0)),
            pl.BlockSpec((1, 2, 1, 32, D), lambda l, h, at: (l, 0, h, 0, 0)),
        ),
    )


def head_scores(q, k, seen, distance, slope):
    s = lax.dot_general(q, k, (((1,), (1,)), ((), ())), preferred_element_type=f32) * HEAD_DIM ** (-0.5)
    s = s - slope * distance
    return jnp.where(seen, s, f32(-1000000000.0))


def visibility(row_start, col_start):
    row = lax.broadcasted_iota(jnp.int32, (RUN, RUN), 0)
    col = lax.broadcasted_iota(jnp.int32, (RUN, RUN), 1)
    seen = (row_start == col_start) & (col <= row)
    return seen, (row - col).astype(f32)


def attend_kernel(slope_ref, rows_ref, cols_ref, qkv_ref, ctx_ref):
    first = pl.program_id(1) * 4
    seen, distance = visibility(rows_ref[0], cols_ref[0])
    done = []
    for i in range(4):
        at = (i // 2) * 384 + (i % 2) * 64
        q = qkv_ref[:, at : at + 64]
        k = qkv_ref[:, at + 128 : at + 192]
        v = qkv_ref[:, at + 256 : at + 320]
        s = head_scores(q, k, seen, distance, slope_ref[first + i])
        top = jnp.max(s, axis=-1, keepdims=True)
        lse = top + jnp.log(jnp.sum(jnp.exp(s - top), axis=-1, keepdims=True))
        p = jnp.exp(s - lse).astype(bf16)
        done.append(jnp.dot(p, v, preferred_element_type=f32))
    ctx_ref[...] = jnp.concatenate(done, axis=1).astype(bf16)


def attend_back_kernel(slope_ref, rows_ref, cols_ref, qkv_ref, ctx_ref, dctx_ref, dqkv_ref, dq_ref, dv_ref):
    first = pl.program_id(1) * 4
    seen, distance = visibility(rows_ref[0], cols_ref[0])
    dqs, dks, dvs = [], [], []
    tn = (((0,), (0,)), ((), ()))
    nt = (((1,), (1,)), ((), ()))
    for i in range(4):
        lanes = slice(i * 64, i * 64 + 64)
        at = (i // 2) * 384 + (i % 2) * 64
        q = qkv_ref[:, at : at + 64]
        k = qkv_ref[:, at + 128 : at + 192]
        v = qkv_ref[:, at + 256 : at + 320]
        s = head_scores(q, k, seen, distance, slope_ref[first + i])
        top = jnp.max(s, axis=-1, keepdims=True)
        lse = top + jnp.log(jnp.sum(jnp.exp(s - top), axis=-1, keepdims=True))
        p = jnp.exp(s - lse)
        dctx = dctx_ref[:, lanes]
        dv = lax.dot_general(p.astype(bf16), dctx, tn, preferred_element_type=f32)
        dp = lax.dot_general(dctx, v, nt, preferred_element_type=f32)
        delta = jnp.sum(dctx.astype(f32) * ctx_ref[:, lanes].astype(f32), axis=-1, keepdims=True)
        ds = (p * (dp - delta)).astype(bf16)
        dqs.append(jnp.dot(ds, k, preferred_element_type=f32) * HEAD_DIM ** (-0.5))
        dks.append(lax.dot_general(ds, q, tn, preferred_element_type=f32) * HEAD_DIM ** (-0.5))
        dvs.append(dv)
    for pair in range(2):
        at = pair * 384
        dq = jnp.concatenate(dqs[2 * pair : 2 * pair + 2], axis=1)
        dk = jnp.concatenate(dks[2 * pair : 2 * pair + 2], axis=1)
        dv = jnp.concatenate(dvs[2 * pair : 2 * pair + 2], axis=1)
        dqkv_ref[:, at : at + 128] = dq.astype(bf16)
        dqkv_ref[:, at + 128 : at + 256] = dk.astype(bf16)
        dqkv_ref[:, at + 256 : at + 384] = dv.astype(bf16)
        dq_ref[0, 0, :, pair * 128 : pair * 128 + 128] = jnp.sum(dq, axis=0, keepdims=True)
        dv_ref[0, 0, :, pair * 128 : pair * 128 + 128] = jnp.sum(dv, axis=0, keepdims=True)


def attend(qkv, rows, cols, slopes):
    return pl.pallas_call(
        attend_kernel,
        out_shape=jax.ShapeDtypeStruct((2 * RUN, 512), bf16),
        grid=(2, 2),
        in_specs=[
            pl.BlockSpec(memory_space=pltpu.SMEM),
            pl.BlockSpec((1, RUN, 1), lambda r, p: (r, 0, 0)),
            pl.BlockSpec((1, 1, RUN), lambda r, p: (r, 0, 0)),
            pl.BlockSpec((RUN, 768), lambda r, p: (r, p)),
        ],
        out_specs=pl.BlockSpec((RUN, 256), lambda r, p: (r, p)),
        compiler_params=pltpu.CompilerParams(vmem_limit_bytes=8 * 1024 * 1024),
        cost_estimate=pl.CostEstimate(flops=4 * 16 * RUN * RUN * 64, bytes_accessed=1 << 20, transcendentals=32 * RUN * RUN),
    )(slopes, rows, cols, qkv)


def attend_back(qkv, ctx, dctx, rows, cols, slopes):
    row_block = pl.BlockSpec((RUN, 256), lambda r, p: (r, p))
    sums = pl.BlockSpec((1, 1, 1, 256), lambda r, p: (r, p, 0, 0))
    return pl.pallas_call(
        attend_back_kernel,
        out_shape=(
            jax.ShapeDtypeStruct((2 * RUN, 1536), bf16),
            jax.ShapeDtypeStruct((2, 2, 1, 256), f32),
            jax.ShapeDtypeStruct((2, 2, 1, 256), f32),
        ),
        grid=(2, 2),
        in_specs=[
            pl.BlockSpec(memory_space=pltpu.SMEM),
            pl.BlockSpec((1, RUN, 1), lambda r, p: (r, 0, 0)),
            pl.BlockSpec((1, 1, RUN), lambda r, p: (r, 0, 0)),
            pl.BlockSpec((RUN, 768), lambda r, p: (r, p)),
            row_block,
            row_block,
        ],
        out_specs=(pl.BlockSpec((RUN, 768), lambda r, p: (r, p)), sums, sums),
        compiler_params=pltpu.CompilerParams(vmem_limit_bytes=8 * 1024 * 1024),
        cost_estimate=pl.CostEstimate(flops=10 * 16 * RUN * RUN * 64, bytes_accessed=1 << 21, transcendentals=32 * RUN * RUN),
    )(slopes, rows, cols, qkv, ctx, dctx)


def layer_norm(stream, gains, shifts):
    average = jnp.mean(stream, axis=-1, keepdims=True)
    centered = stream - average
    variance = jnp.mean(centered * centered, axis=-1, keepdims=True)
    inv_std = lax.rsqrt(variance + epsilon)
    normed = centered * inv_std
    return (normed * gains + shifts, normed, inv_std)


def norm_back(grad_norm, normed, inv_std, gains):
    scaled = grad_norm * gains
    inner = (
        scaled
        - jnp.mean(scaled, axis=-1, keepdims=True)
        - normed * jnp.mean(scaled * normed, axis=-1, keepdims=True)
    )
    return (inv_std * inner, jnp.sum(grad_norm * normed, axis=0), jnp.sum(grad_norm, axis=0))


def gelu_tanh(values):
    inner = jnp.tanh(gelu_coef * (values + 0.044715 * values * values * values))
    return 0.5 * values * (1.0 + inner)


def gelu_slope(values):
    inner = jnp.tanh(gelu_coef * (values + 0.044715 * values * values * values))
    return 0.5 * (1.0 + inner) + 0.5 * values * (1.0 - inner * inner) * gelu_coef * (
        1.0 + 3.0 * 0.044715 * values * values
    )


def dot(a, b):
    return jnp.dot(a, b, preferred_element_type=f32)


def dot_nt(a, b):
    return lax.dot_general(a, b, (((1,), (1,)), ((), ())), preferred_element_type=f32)


def dot_tn(a, b):
    return lax.dot_general(a, b, (((0,), (0,)), ((), ())), preferred_element_type=f32)


def local(hidden_in, doc_start, grad_out, w_qkv, w_proj, w_up, w_down, norm_gain, d_bias, up_bias):
    x, yhi, z, core = (lax.axis_index(n) for n in ("x", "yhi", "z", "core"))
    at = jnp.stack([z, core]).astype(jnp.int32)
    at_x = jnp.stack([(z - x + 4) % 4, core]).astype(jnp.int32)
    index = jnp.arange(8, dtype=jnp.int32)

    def both(own):
        return jnp.concatenate([own, swap(own)], axis=0)

    def halves_summed(product, a, w):
        theirs = swap(product(a[RUN:], w))
        return product(a[:RUN], w) + theirs

    small = jnp.concatenate(
        [
            jnp.transpose(jnp.concatenate([norm_gain, d_bias], axis=2), (0, 2, 1)).reshape(16, 128),
            up_bias.reshape(8, 128),
        ]
    )

    mine_z, mine_x = select_weights(at, w_qkv, w_proj, w_up, w_down)
    weights = []
    thin = jnp.concatenate([small, jnp.zeros((4, 128), bf16)]).reshape(4, 896)
    first_z = to_all(jnp.concatenate([mine_z[0], thin, jnp.zeros((4, 896), bf16)]), SHARD, 8)
    all_small = first_z[:, 128:132].reshape(8, 28, 128)[:, :24]
    block_z = first_z[:, :128].reshape(D, 896)
    other = y_pair(mine_x[0])
    piece_x = jnp.concatenate([jnp.where(yhi == 0, mine_x[0], other), jnp.where(yhi == 0, other, mine_x[0])])
    own, following, (top, bottom), previous = ring_gather(after(piece_x, block_z), x_up, x_down)
    all_x = jnp.concatenate([own, following, top, bottom, previous]).reshape(8, 320, D)
    first_ring_x = (previous, following)
    next_x = lax.all_gather(after(mine_x[1], block_z), SHARD, axis=0)
    for layer in range(LAYERS):
        own, following, (top, bottom), previous = ring_gather(block_z, z_up, z_down)
        wup, wqkv = split_z(at, own, following, top, bottom, previous)
        wdown, wproj = split_x(at_x if layer == 0 else at, all_x)
        weights.append((wqkv, wproj, wup, wdown))
        if layer == 0:
            next_z = to_all(after(mine_z[1], previous, following, *first_ring_x), SHARD, 8).reshape(D, 896)
            block_z, all_x = after(next_z, top, bottom), next_x
        else:
            second_ring = (previous, following)

    small = all_small.reshape(4, 2, 24, 128).astype(f32)
    wide = jnp.transpose(small[:, :, :16], (2, 0, 1, 3)).reshape(LAYERS, 8, D)
    hidden_bias = small[:, :, 16:].reshape(4, 2, LAYERS, 2, 256)

    def core_heads(vector):
        picked = lax.dynamic_index_in_dim(vector.reshape(4, 2, 2, 64), core, axis=2, keepdims=False)
        return rolled(picked.reshape(4, 128), z)

    starts = both(doc_start.reshape(1, RUN))
    rows, cols = starts.reshape(2, RUN, 1), starts.reshape(2, 1, RUN)
    head = 4 * ((z + index // 2) % 4) + 2 * (index % 2) + core
    slopes = 2.0 ** (-8.0 * (head.astype(f32) + 1.0) / HEADS)

    kept = []
    current = hidden_in
    for layer in range(LAYERS):
        wqkv, wproj, wup, wdown = weights[layer]
        gain_one, gain_two, shift_one, shift_two, bq, bv, bproj, bdown = (wide[layer, i] for i in range(8))
        bq, bv = core_heads(bq), core_heads(bv)
        bqkv = jnp.stack([bq, jnp.zeros_like(bq), bv], axis=1).reshape(1536)
        ubias = lax.dynamic_index_in_dim(hidden_bias[:, :, layer], core, axis=2, keepdims=False)
        ubias = rolled(ubias.reshape(4, 512), z).reshape(2048)
        first_f, normed_one, inv_one = layer_norm(current, gain_one, shift_one)
        first_in = both(first_f.astype(bf16))
        if layer == 0:
            first_in = after(first_in, next_z)
        qkv = (dot(first_in, wqkv) + bqkv).astype(bf16)
        ctx = attend(qkv, rows, cols, slopes)
        if layer == 0:
            ctx = after(ctx, *second_ring)
        middle = current + halves_summed(dot, ctx, wproj) + bproj
        second_f, normed_two, inv_two = layer_norm(middle, gain_two, shift_two)
        second_in = both(second_f.astype(bf16))
        upper = dot(second_in, wup) + ubias
        activ = gelu_tanh(upper).astype(bf16)
        current = middle + halves_summed(dot, activ, wdown) + bdown
        kept.append((first_in, normed_one, inv_one, qkv, ctx, second_in, normed_two, inv_two, upper, activ, gain_one, gain_two))
    hidden_out = current

    def summed(blocks):
        return jnp.sum(blocks.astype(f32), axis=0).astype(bf16)

    def ring_z(a2, dub, a1, dqkv):
        parts = [grad_z(at, a2, dub, a1, dqkv, i) for i in (2, 1, 3, 0)]
        parts = [parts[i] for i in (3, 1, 0, 2)]
        total, sent, near, got = ring_scatter(parts, z_up, z_down)
        return total.astype(bf16).reshape(16, 64, 896), (sent, near, got)

    def ring_x(m, dy, ctx, dr):
        parts = grad_x(at_x, m, dy, ctx, dr)
        total, _, near, got = ring_scatter([parts[2 * i : 2 * i + 2].reshape(640, D) for i in range(4)], x_up, x_down)
        part = total.astype(bf16).reshape(2, 320, D)
        part = jnp.concatenate([part[:, :256].reshape(2, 8, 32, D), part[:, 256:].reshape(2, 8, 8, D)], axis=2)
        return jnp.transpose(part, (1, 0, 2, 3)).reshape(16, 40, D), (near, got)

    def finish(part_z, part_x, *earlier):
        part_x = summed(exchange(part_x, ("ylo", "z", "yhi")))
        part_z = exchange(part_z, ("x", "yhi", "ylo"))
        return summed(after(part_z, *earlier) if earlier else part_z), part_x

    def share(part_z, part_x):
        part_x = jnp.transpose(part_x.reshape(5, 8, 8, 128), (2, 1, 0, 3)).reshape(64, 640)
        parts = lax.all_gather(jnp.concatenate([part_z, part_x], axis=1), REP, axis=0)
        return parts.reshape(2, 4, 2, 64, 1536)

    shared = [None] * LAYERS
    thin_grads, head_grads, unit_grads = [None] * LAYERS, [None] * LAYERS, [None] * LAYERS
    running, ring_state = grad_out, None
    for layer in reversed(range(LAYERS)):
        wqkv, wproj, wup, wdown = weights[layer]
        first_in, normed_one, inv_one, qkv, ctx, second_in, normed_two, inv_two, upper, activ, gain_one, gain_two = kept[layer]
        if ring_state is not None:
            running = after(running, *ring_state[0])
        g_bdown = jnp.sum(running, axis=0)
        grad_yb = both(running.astype(bf16))
        grad_upper = dot_nt(grad_yb, wdown) * gelu_slope(upper)
        g_ubias = jnp.sum(grad_upper, axis=0)
        grad_ub = grad_upper.astype(bf16)
        grad_two = halves_summed(dot_nt, grad_ub, wup)
        back_two, g_gain_two, g_shift_two = norm_back(grad_two, normed_two, inv_two, gain_two)
        grad_mid = running + back_two
        g_bproj = jnp.sum(grad_mid, axis=0)
        grad_midb = grad_mid.astype(bf16)
        if ring_state is not None:
            grad_midb = after(grad_midb, *ring_state[1], *x_state[0])
            part_x_before = part_x
        grad_midb = both(grad_midb)
        grad_ctx = dot_nt(grad_midb, wproj).astype(bf16)
        part_x, x_state = ring_x(activ, grad_yb, ctx, grad_midb)
        grad_qkv, g_bq, g_bv = attend_back(qkv, ctx, grad_ctx, rows, cols, slopes)
        if ring_state is not None:
            later = (after(part_z, grad_qkv), part_x_before)
            grad_qkv = after(grad_qkv, *ring_state[2], *x_state[0])
        part_z, ring_state = ring_z(second_in, grad_ub, first_in, grad_qkv)
        if layer == 0:
            grad_qkv = after(grad_qkv, *ring_state[0])
        grad_one = halves_summed(dot_nt, grad_qkv, wqkv)
        if layer == 0:
            grad_one = after(grad_one, *ring_state[1])
            shared[1] = share(*finish(*later, *ring_state[1]))
        back_one, g_gain_one, g_shift_one = norm_back(grad_one, normed_one, inv_one, gain_one)
        running = grad_mid + back_one

        thin_grads[layer] = [g_gain_one, g_gain_two, g_shift_one, g_shift_two, g_bproj, g_bdown]
        head_grads[layer] = [jnp.sum(g, axis=0).reshape(4, 128) for g in (g_bq, g_bv)]
        unit_grads[layer] = g_ubias.reshape(4, 512)

    shared[0] = share(*finish(part_z, part_x))

    thin = jnp.stack(thin_grads[0] + thin_grads[1]).reshape(LAYERS, 6, 4, 2, 128)
    heads = jnp.stack(head_grads[0] + head_grads[1], axis=1)
    heads = rolled(heads, (4 - z) % 4).reshape(4, LAYERS, 2, 2, 1, 64)
    mine = lax.broadcasted_iota(jnp.int32, (4, LAYERS, 2, 2, 2, 64), 4) == core
    heads = jnp.where(mine, heads, 0.0).reshape(4, LAYERS, 2, 2, 128)
    units = rolled(jnp.stack(unit_grads, axis=1), (4 - z) % 4).reshape(4, LAYERS, 2, 1, 256)
    mine = lax.broadcasted_iota(jnp.int32, (4, LAYERS, 2, 2, 256), 3) == core
    units = jnp.where(mine, units, 0.0).reshape(4, LAYERS, 2, 4, 128)
    thin = jnp.transpose(thin, (2, 3, 0, 1, 4))
    heads = jnp.transpose(heads, (0, 3, 1, 2, 4))
    units = jnp.transpose(units, (0, 2, 1, 3, 4))
    part = jnp.concatenate([thin[:, :, :, :4], heads, thin[:, :, :, 4:], units], axis=3)
    part = jnp.sum(exchange(part.reshape(8, 24, 128), SHARD), axis=0)
    part = jnp.sum(to_all(part, REP, 16), axis=0).reshape(LAYERS, 12, 128)
    g_wide = jnp.transpose(part[:, :8], (0, 2, 1))
    g_up, g_qkv, g_down, g_proj = assemble(at, shared[0], shared[1])
    return (
        hidden_out,
        running,
        g_qkv,
        g_proj.reshape(LAYERS, 128, D),
        g_up,
        g_down.reshape(LAYERS, 512, D),
        g_wide[:, :, :2],
        g_wide[:, :, 2:],
        part[:, 8:].reshape(LAYERS, 512),
    )


def solution(mesh):
    fine = Mesh(mesh.devices.reshape(2, 4, 2, 4, 2), AXES)
    tokens = P(AXES)
    wide_tokens = P(AXES, None)
    params = P(None, ("x", "yhi"), None)
    return jax.shard_map(
        local,
        mesh=fine,
        in_specs=(wide_tokens, tokens, wide_tokens, params, params, params, params, params, params, P(None, ("x", "yhi"))),
        out_specs=(wide_tokens, wide_tokens, params, params, params, params, params, params, P(None, ("x", "yhi"))),
        check_vma=False,
    )
```
